32 devices in a mesh: context: 8 (over y, x, core), tensor: 4 (over z).
Axes of the slice: x: 2, y: 2, z: 4, core: 2. Of those that a mesh axis runs over, the one named last changes fastest.
Arguments:
- activations: bfloat16 [4096, 3072], P('context', 'tensor'), may hold values from -6 to 6
- qkv_weight: bfloat16 [3072, 3, 4096], P(None, None, 'tensor'), may hold values from -0.109375 to 0.109375
- log_decay: float32 [4096, 32], P('context', 'tensor'), may hold values from -1.5 to 0, as said below
- lengths: int32 [8], P('context'), may hold values from 256 to 512, as said below
- out_grad: bfloat16 [4096, 4096], P('context', 'tensor'), may hold values from -0.0014648438 to 0.0014648438
Outputs:
- weight_grad: float32 [3072, 3, 4096], P('context', None, 'tensor')
The draws below stay inside these ranges and needn't reach their ends.
Inputs may be any that keep to these rules, and one draw needn't show every extreme that they name: `log_decay`: Negative; entries vary from token to token. `lengths`: each entry is a multiple of 256; the live tokens are the first slots of their shard; in every draw at least one shard is full.
All inputs are finite; a program needn't handle non-finite values.
Results may differ from the reference program's by a relative error of at most 0.015.
Values may be sent and summed in bfloat16 or wider, within the bound.
A program may use at most 128 MiB of HBM per device.

```python
import math
import jax
import jax.numpy as jnp
from jax import lax

D = 3072
HEAD = 128
BLOCK = 256
TOK_DEV = 512
HEAD_COUNT = 32
TOKEN_SLOTS = 4096


def draw_log_decay(key, part):
    random_seed_keys = jax.random.split(jax.random.fold_in(key, 17), 7)
    shard_count = TOKEN_SLOTS // TOK_DEV
    fast_share = 0.5
    is_fast = jax.random.uniform(random_seed_keys[0], (HEAD_COUNT,)) < fast_share
    fast_rate = jnp.exp(jax.random.uniform(random_seed_keys[1], (HEAD_COUNT,), minval=math.log(1.0 / 50.0), maxval=math.log(1.0 / 30.0)))
    slow_rate = jnp.exp(jax.random.uniform(random_seed_keys[2], (HEAD_COUNT,), minval=math.log(0.1), maxval=math.log(0.3))) / TOKEN_SLOTS
    head_rate = jnp.where(is_fast, fast_rate, slow_rate)
    shard_factor = jnp.exp(jax.random.uniform(random_seed_keys[3], (shard_count, HEAD_COUNT), minval=math.log(0.5), maxval=math.log(2.0)))
    token_factor = jax.random.uniform(random_seed_keys[4], (TOKEN_SLOTS, HEAD_COUNT), minval=0.7, maxval=1.4)
    baseline_decay_rate = jnp.repeat(shard_factor, TOK_DEV, axis=0) * token_factor * head_rate[None, :]
    flurry_location = jax.random.randint(random_seed_keys[5], (2,), 0, TOKEN_SLOTS)
    flurry_depth = -jnp.log(1.0 - jax.random.uniform(random_seed_keys[6], (2, HEAD_COUNT), minval=0.2, maxval=0.5))
    token_position = jnp.arange(TOKEN_SLOTS)
    flurry_list = jnp.sum((token_position[:, None, None] == flurry_location[None, :, None]) * flurry_depth[None], axis=1)
    return (-(baseline_decay_rate + flurry_list)).astype(jnp.float32)


def draw_lengths(key, part):
    random_seed_keys = jax.random.split(jax.random.fold_in(key, 29), 2)
    shard_count = TOKEN_SLOTS // TOK_DEV
    block_count = TOK_DEV // BLOCK
    block_live = jax.random.randint(random_seed_keys[0], (shard_count,), 1, block_count + 1)
    full_shard = jax.random.randint(random_seed_keys[1], (), 0, shard_count)
    block_live = jnp.where(jnp.arange(shard_count) == full_shard, block_count, block_live)
    return (block_live * BLOCK).astype(jnp.int32)


def with_spikes(values, own_key, source, target, shards_of, factor):
    owner, partner = [(jnp.arange(values.shape[position]) // (values.shape[position] // shards_of)).reshape([-1 if axis == position else 1 for axis in range(values.ndim)]) for position in (source, target)]
    chosen = jax.random.permutation(own_key, shards_of)[partner]
    strong = (owner == chosen) | (owner == (partner + shards_of // 2) % shards_of)
    return jnp.where(strong, factor * values, values)


def steps_of(rng, extent, pieces, low, largest):
    gain, own = 1.0, jax.random.fold_in(rng, 6)
    for axis_at, shards_of in pieces:
        steps = jnp.exp(jax.random.uniform(jax.random.fold_in(own, axis_at), (shards_of,), jnp.float32, low / len(pieces), largest / len(pieces)))
        gain = gain * jnp.repeat(steps, extent[axis_at] // shards_of).reshape([-1 if axis == axis_at else 1 for axis in range(len(extent))])
    return gain


def gaussian(key, shape, width, reach, pieces=(), held_as=jnp.bfloat16):
    array = width * jax.random.normal(key, shape, jnp.float32)
    if pieces:
        array = array * steps_of(key, shape, pieces, -0.22, 0.18)
    return jnp.clip(array, -reach, reach).astype(held_as)


def gaussian_with(stream_key, shape, width, most, cuts, heavy, kind=jnp.bfloat16):
    values = width * jax.random.normal(stream_key, shape, jnp.float32)
    if cuts:
        values = values * steps_of(stream_key, shape, cuts, -0.22, 0.18)
    return jnp.clip(with_spikes(values, jax.random.fold_in(stream_key, 3), *heavy), -most, most).astype(kind)


def setup_inputs(seed: int = 0) -> dict:
    splits = jax.random.split(jax.random.key(seed), 6)
    activations = gaussian_with(splits[0], (TOKEN_SLOTS, D), 1.0, 6.0, ((0, 8), (1, 4)), (0, 1, 8, 2.0))
    qkv_weight = gaussian(splits[1], (D, 3, HEAD_COUNT * HEAD), D ** -0.5, 0.109375, ((2, 4),))
    log_decay = draw_log_decay(jax.random.fold_in(splits[5], 71), 0)
    lengths = draw_lengths(jax.random.fold_in(splits[5], 71), 0)
    out_grad = gaussian(splits[4], (TOKEN_SLOTS, HEAD_COUNT * HEAD), (1.0 / TOKEN_SLOTS), 0.0014648438, ((0, 8), (1, 4)))
    return {"activations": activations, "qkv_weight": qkv_weight, "log_decay": log_decay, "lengths": lengths, "out_grad": out_grad}


def rounded(value):
    return lax.optimization_barrier(value.astype(jnp.bfloat16)).astype(jnp.float32)


def shard_sums(query, key_matrix_rows, value_matrix_rows, output_gradient, decays):
    run_sum = jnp.cumsum(decays, axis=0)
    shard_sum = run_sum[-1]
    score_scale_factor = HEAD ** -0.5
    until_finish = jnp.exp(shard_sum[None, :] - run_sum)
    decayed_key_rows = rounded(key_matrix_rows.astype(jnp.float32) * until_finish[:, :, None])
    partition_state = jnp.einsum("jla,jlu->lau", decayed_key_rows, value_matrix_rows.astype(jnp.float32)).astype(jnp.bfloat16)
    decayed_query_rows = rounded(query.astype(jnp.float32) * (score_scale_factor * jnp.exp(run_sum))[:, :, None])
    state_gradient = jnp.einsum("jla,jlu->lau", decayed_query_rows, output_gradient.astype(jnp.float32)).astype(jnp.bfloat16)
    return partition_state, state_gradient, shard_sum.astype(jnp.bfloat16)


def shard_grads(query, key_matrix_rows, value_matrix_rows, output_gradient, decays, is_live, incoming, from_later):
    run_sum = jnp.cumsum(decays, axis=0)
    shard_sum = run_sum[-1]
    score_scale_factor = HEAD ** -0.5
    token_position = jnp.arange(TOK_DEV, dtype=jnp.int32)
    causal = token_position[:, None] >= token_position[None, :]
    gap_matrix = run_sum.T[:, :, None] - run_sum.T[:, None, :]
    decay_matrix = jnp.exp(jnp.where(causal[None], gap_matrix, -jnp.inf))
    query_wide_float = query.astype(jnp.float32)
    key_wide_float = key_matrix_rows.astype(jnp.float32)
    value_wide_float = value_matrix_rows.astype(jnp.float32)
    gradient_wide_float = output_gradient.astype(jnp.float32)
    probability_wide_float = rounded(jnp.einsum("thd,shd->hts", query_wide_float, key_wide_float) * score_scale_factor * decay_matrix)
    score_wide_float = rounded(jnp.einsum("thd,shd->hts", gradient_wide_float, value_wide_float) * decay_matrix)
    arriving_wide_float = rounded(incoming)
    subsequent_wide_float = rounded(from_later)
    since_beginning = jnp.exp(run_sum)[:, :, None]
    until_finish = jnp.exp(shard_sum[None, :] - run_sum)[:, :, None]
    query_gradient = score_scale_factor * (jnp.einsum("zmb,bzw->mzw", score_wide_float, key_wide_float) + since_beginning * jnp.einsum("bzf,zof->bzo", gradient_wide_float, arriving_wide_float))
    key_gradient = score_scale_factor * jnp.einsum("rvz,vrj->zrj", score_wide_float, query_wide_float) + until_finish * jnp.einsum("bzf,zof->bzo", value_wide_float, subsequent_wide_float)
    value_gradient = jnp.einsum("rvz,vrj->zrj", probability_wide_float, gradient_wide_float) + until_finish * jnp.einsum("cnf,nfg->cng", key_wide_float, subsequent_wide_float)
    stacked = jnp.stack([query_gradient, key_gradient, value_gradient], axis=1) * is_live[:, None, None, None]
    return stacked.astype(jnp.bfloat16).reshape(TOK_DEV, 3 * HEAD_COUNT * HEAD)


def decay_step(running, shard_item):
    partition_state, shard_total = shard_item
    updated = jnp.exp(shard_total.astype(jnp.float32))[:, None, None] * running + partition_state.astype(jnp.float32)
    return updated, running


def reference(activations, qkv_weight, log_decay, lengths, out_grad):
    shards = TOKEN_SLOTS // TOK_DEV
    col_width = HEAD_COUNT * HEAD
    token_position = jnp.arange(TOKEN_SLOTS, dtype=jnp.int32)
    is_live = (token_position % TOK_DEV < jnp.repeat(lengths, TOK_DEV)).astype(jnp.float32)
    projected = jnp.dot(activations, qkv_weight.reshape(D, 3 * col_width), preferred_element_type=jnp.float32).astype(jnp.bfloat16)
    projected = (projected * is_live.astype(jnp.bfloat16)[:, None]).reshape(shards, TOK_DEV, 3, HEAD_COUNT, HEAD)
    output_gradient = out_grad.reshape(shards, TOK_DEV, HEAD_COUNT, HEAD)
    decays = (log_decay * is_live[:, None]).reshape(shards, TOK_DEV, HEAD_COUNT)
    live_shards = is_live.reshape(shards, TOK_DEV)
    input_shards = activations.reshape(shards, TOK_DEV, D)
    states, grad_states, totals = lax.map(lambda shard_item: shard_sums(shard_item[0][:, 0], shard_item[0][:, 1], shard_item[0][:, 2], shard_item[1], shard_item[2]), (projected, output_gradient, decays))
    start_state = jnp.zeros((HEAD_COUNT, HEAD, HEAD), jnp.float32)
    _, incoming = lax.scan(decay_step, start_state, (states, totals))
    _, from_later = lax.scan(decay_step, start_state, (grad_states, totals), reverse=True)

    def grads_step(running, shard_item):
        input_shard, qkv_shard, grad_shard, decay_shard, live_shard, incoming_shard, later_shard = shard_item
        qkv_grad = shard_grads(qkv_shard[:, 0], qkv_shard[:, 1], qkv_shard[:, 2], grad_shard, decay_shard, live_shard, incoming_shard, later_shard)
        partial_grad = jnp.dot(input_shard.T, qkv_grad, preferred_element_type=jnp.float32).astype(jnp.bfloat16)
        return running + partial_grad.astype(jnp.float32), None

    start_grad = jnp.zeros((D, 3 * col_width), jnp.float32)
    weight_grad, _ = lax.scan(grads_step, start_grad, (input_shards, projected, output_gradient, decays, live_shards, incoming, from_later))
    return weight_grad.reshape(D, 3, col_width)
```

```python
import functools

import jax
import jax.numpy as jnp
from jax import lax
from jax.experimental import pallas as pl
from jax.experimental.pallas import tpu as pltpu
from jax.sharding import PartitionSpec as P


F32 = jnp.float32
BF16 = jnp.bfloat16


def contract(a, b, dims):
    return lax.dot_general(a, b, (dims, ((), ())), preferred_element_type=F32)


ROWS = ((0,), (0,))
LANES = ((1,), (1,))
PLAIN = ((1,), (0,))


def states_kernel(scale, q_ref, k_ref, v_ref, g_ref, c_ref, state_ref, grad_ref):
    c = c_ref[...]
    total = c[-1:, :]
    weighted_k = (k_ref[...].astype(F32) * jnp.exp(total - c)).astype(BF16)
    state_ref[0] = contract(weighted_k, v_ref[...], ROWS).astype(BF16)
    weighted_q = (q_ref[...].astype(F32) * (scale * jnp.exp(c))).astype(BF16)
    grad_ref[0] = contract(weighted_q, g_ref[...], ROWS).astype(BF16)


def intra_kernel(scale, q_ref, k_ref, v_ref, g_ref, c_ref, ct_ref, dq_ref, dk_ref, dv_ref):
    head = pl.program_id(0)
    q, k, v, g = q_ref[...], k_ref[...], v_ref[...], g_ref[...]
    tokens, width = q.shape
    column = jnp.concatenate([c_ref[...]] * (tokens // width), axis=1)
    gap = column - ct_ref[pl.ds(head, 1), :]
    row_at = lax.broadcasted_iota(jnp.int32, (tokens, tokens), 0)
    col_at = lax.broadcasted_iota(jnp.int32, (tokens, tokens), 1)
    decay = jnp.exp(jnp.where(row_at >= col_at, gap, -jnp.inf))
    prob = (contract(q, k, LANES) * scale * decay).astype(BF16)
    score = (contract(g, v, LANES) * decay).astype(BF16)
    dq_ref[...] = scale * contract(score, k, PLAIN)
    dk_ref[...] = scale * contract(score, q, ROWS)
    dv_ref[...] = contract(prob, g, ROWS)


def inter_kernel(scale, len_ref, k_ref, v_ref, g_ref, c_ref, in_ref, later_ref, dq_ref, dk_ref, dv_ref,
                 oq_ref, ok_ref, ov_ref):
    c = c_ref[...]
    live = lax.broadcasted_iota(jnp.int32, c.shape, 0) < len_ref[0]
    until = jnp.exp(c[-1:, :] - c)
    dq = dq_ref[...] + scale * jnp.exp(c) * contract(g_ref[...], in_ref[0], LANES)
    dk = dk_ref[...] + until * contract(v_ref[...], later_ref[0], LANES)
    dv = dv_ref[...] + until * contract(k_ref[...], later_ref[0], PLAIN)
    oq_ref[...] = jnp.where(live, dq, 0.0).astype(BF16)
    ok_ref[...] = jnp.where(live, dk, 0.0).astype(BF16)
    ov_ref[...] = jnp.where(live, dv, 0.0).astype(BF16)


def swap(value, size, distance):
    return lax.ppermute(value, "context", [(i, i ^ distance) for i in range(size)])


PIECES = 4
TILE = 256


def project_kernel(act_ref, live_ref, total_ref, weight_ref, every_ref, q_ref, k_ref, v_ref, totals_ref,
                   weights, sums, own_sem, weight_sem, send_sem, recv_sem, total_send, total_recv):
    size, me = lax.axis_size("tensor"), lax.axis_index("tensor")
    shard_count, shard = lax.axis_size("context"), lax.axis_index("context")
    depth = act_ref.shape[1]
    piece = act_ref.shape[0] // PIECES
    columns = q_ref.shape[1]
    tiles = columns // TILE

    def load(owner, part):
        rows = pl.ds(pl.multiple_of(owner * depth, depth), depth)
        return pltpu.make_async_copy(weight_ref.at[part, rows], weights.at[owner, part], weight_sem.at[owner, part])

    for at in range(size):
        owner = lax.rem(me + at, size)
        for part in range(3):
            load(owner, part).start()

    barrier = pltpu.get_barrier_semaphore()
    for target in (me - 1, me + 1):
        @pl.when((target >= 0) & (target < size))
        def _():
            pl.semaphore_signal(barrier, inc=1, device_id={"tensor": target}, device_id_type=pl.DeviceIdType.MESH)

    @pl.loop(1, shard_count)
    def _(step):
        peer = lax.rem(shard + step, shard_count)
        pl.semaphore_signal(barrier, inc=1, device_id={"context": peer}, device_id_type=pl.DeviceIdType.MESH)

    neighbours = jnp.where(me > 0, 1, 0) + jnp.where(me < size - 1, 1, 0)
    pl.semaphore_wait(barrier, neighbours + shard_count - 1)

    def rows_of(at):
        return pl.ds(pl.multiple_of(at * piece, piece), piece)

    def send(source, owner, at, side):
        return pltpu.make_async_remote_copy(
            src_ref=source,
            dst_ref=every_ref.at[owner, rows_of(at)],
            send_sem=send_sem.at[side, owner, at],
            recv_sem=recv_sem.at[owner, at],
            device_id={"tensor": me + 1 - 2 * side},
            device_id_type=pl.DeviceIdType.MESH,
        )

    def has_target(side):
        target = me + 1 - 2 * side
        return (target >= 0) & (target < size)

    def send_total(step):
        peer = lax.rem(shard + step, shard_count)
        return pltpu.make_async_remote_copy(
            src_ref=total_ref,
            dst_ref=totals_ref.at[shard],
            send_sem=total_send.at[peer],
            recv_sem=total_recv.at[shard],
            device_id={"context": peer},
            device_id_type=pl.DeviceIdType.MESH,
        )

    for at in range(PIECES):
        for side in range(2):
            @pl.when(has_target(side))
            def _():
                send(act_ref.at[rows_of(at)], me, at, side).start()

    @pl.loop(1, shard_count)
    def _(step):
        send_total(step).start()

    own = pltpu.make_async_copy(act_ref, every_ref.at[me], own_sem)
    own.start()
    totals_ref[shard] = total_ref[...]

    for part in range(3):
        load(me, part).wait()

    @pl.loop(0, 3 * tiles)
    def _(tile):
        part = tile // tiles
        cols = pl.ds(pl.multiple_of(lax.rem(tile, tiles) * TILE, TILE), TILE)
        sums[part, :, cols] = jnp.dot(act_ref[...], weights[me, part, :, cols], preferred_element_type=F32)

    own.wait()
    for distance in range(1, size):
        for side in range(2):
            owner = me + (2 * side - 1) * distance

            @pl.when((owner >= 0) & (owner < size))
            def _():
                for part in range(3):
                    load(owner, part).wait()

        @pl.loop(0, PIECES)
        def _(at):
            for side in range(2):
                owner = me + (2 * side - 1) * distance

                @pl.when((owner >= 0) & (owner < size))
                def _():
                    pltpu.make_async_copy(
                        every_ref.at[owner, rows_of(at)], every_ref.at[owner, rows_of(at)], recv_sem.at[owner, at]
                    ).wait()

                    @pl.when(has_target(side))
                    def _():
                        send(every_ref.at[owner, rows_of(at)], owner, at, side).start()

            @pl.loop(0, 2)
            def _(side):
                owner = me + (2 * side - 1) * distance

                @pl.when((owner >= 0) & (owner < size))
                def _():
                    @pl.loop(0, 3 * tiles)
                    def _(tile):
                        part = tile // tiles
                        cols = pl.ds(pl.multiple_of(lax.rem(tile, tiles) * TILE, TILE), TILE)
                        sums[part, rows_of(at), cols] += jnp.dot(
                            every_ref[owner, rows_of(at), :], weights[owner, part, :, cols], preferred_element_type=F32
                        )

    live = live_ref[...]
    for part, ref in enumerate((q_ref, k_ref, v_ref)):
        @pl.loop(0, tiles)
        def _(tile):
            cols = pl.ds(pl.multiple_of(tile * TILE, TILE), TILE)
            ref[:, cols] = (sums[part, :, cols] * live).astype(BF16)

    for side in range(2):
        @pl.when(has_target(side))
        def _():
            for distance in range(size):
                owner = me + (2 * side - 1) * distance

                @pl.when((owner >= 0) & (owner < size))
                def _():
                    for at in range(PIECES):
                        send(every_ref.at[owner, rows_of(at)], owner, at, side).wait_send()

    @pl.loop(1, shard_count)
    def _(step):
        peer = lax.rem(shard + step, shard_count)
        send_total(step).wait_send()
        pltpu.make_async_copy(total_ref, totals_ref.at[peer], total_recv.at[peer]).wait()


def project(activations, weight, live, total, shard_count, size):
    tokens, depth = activations.shape
    columns = weight.shape[2]
    vmem = pl.BlockSpec(memory_space=pltpu.VMEM)
    heads_out = [jax.ShapeDtypeStruct((tokens, columns), BF16)] * 3
    return pl.pallas_call(
        project_kernel,
        in_specs=[vmem] * 3 + [pl.BlockSpec(memory_space=pl.ANY)],
        out_specs=[vmem] * 5,
        out_shape=[jax.ShapeDtypeStruct((size, tokens, depth), BF16)]
        + heads_out
        + [jax.ShapeDtypeStruct((shard_count,) + total.shape, F32)],
        scratch_shapes=[
            pltpu.VMEM((size, 3, depth, columns), BF16),
            pltpu.VMEM((3, tokens, columns), F32),
            pltpu.SemaphoreType.DMA,
            pltpu.SemaphoreType.DMA((size, 3)),
            pltpu.SemaphoreType.DMA((2, size, PIECES)),
            pltpu.SemaphoreType.DMA((size, PIECES)),
            pltpu.SemaphoreType.DMA((shard_count,)),
            pltpu.SemaphoreType.DMA((shard_count,)),
        ],
        compiler_params=pltpu.CompilerParams(collective_id=0, has_side_effects=True, vmem_limit_bytes=48 << 20),
        name="project",
    )(activations, live, total, weight)


def flips(chip):
    bx, by = lax.rem(chip, 2), chip // 2
    return chip + 1 - 2 * bx, chip + 2 - 4 * by, 3 - chip


def gather_kernel(act_ref, live_ref, total_ref, weight_ref, q_ref, k_ref, v_ref, totals_ref, rows_ref,
                  every, weights, sums, weight_sem, send_sem, recv_sem, total_send, total_recv,
                  local_sem, pair_send, pair_recv, row_send, row_recv):
    size, me = lax.axis_size("tensor"), lax.axis_index("tensor")
    shard_count, shard = lax.axis_size("context"), lax.axis_index("context")
    core, chip = lax.rem(shard, 2), shard // 2
    chip_x, chip_y, chip_far = flips(chip)
    depth = act_ref.shape[1]
    piece = act_ref.shape[0] // PIECES
    columns = q_ref.shape[1]
    tiles = columns // TILE
    half = rows_ref.shape[-1]

    def load(owner, part):
        rows = pl.ds(pl.multiple_of(owner * depth, depth), depth)
        return pltpu.make_async_copy(weight_ref.at[part, rows], weights.at[owner, part], weight_sem.at[owner, part])

    for at in range(size):
        owner = lax.rem(me + at, size)
        for part in range(3):
            load(owner, part).start()

    barrier = pltpu.get_barrier_semaphore()
    for target in (me - 1, me + 1):
        @pl.when((target >= 0) & (target < size))
        def _():
            pl.semaphore_signal(barrier, inc=1, device_id={"tensor": target}, device_id_type=pl.DeviceIdType.MESH)

    @pl.loop(1, shard_count)
    def _(step):
        peer = lax.rem(shard + step, shard_count)
        pl.semaphore_signal(barrier, inc=1, device_id={"context": peer}, device_id_type=pl.DeviceIdType.MESH)

    neighbours = jnp.where(me > 0, 1, 0) + jnp.where(me < size - 1, 1, 0)
    pl.semaphore_wait(barrier, neighbours + shard_count - 1)

    def rows_of(at):
        return pl.ds(pl.multiple_of(at * piece, piece), piece)

    def half_of(which):
        return pl.ds(pl.multiple_of(which * half, half), half)

    def send(source, owner, at, side):
        return pltpu.make_async_remote_copy(
            src_ref=source,
            dst_ref=every.at[owner, rows_of(at)],
            send_sem=send_sem.at[side, owner, at],
            recv_sem=recv_sem.at[owner, at],
            device_id={"tensor": me + 1 - 2 * side},
            device_id_type=pl.DeviceIdType.MESH,
        )

    def has_target(side):
        target = me + 1 - 2 * side
        return (target >= 0) & (target < size)

    def send_total(step):
        peer = lax.rem(shard + step, shard_count)
        return pltpu.make_async_remote_copy(
            src_ref=total_ref,
            dst_ref=totals_ref.at[shard],
            send_sem=total_send.at[peer],
            recv_sem=total_recv.at[shard],
            device_id={"context": peer},
            device_id_type=pl.DeviceIdType.MESH,
        )

    def keep(source, at, order, which):
        return pltpu.make_async_copy(
            source.at[rows_of(at), half_of(core)], rows_ref.at[order, which, 0, rows_of(at)], local_sem.at[order, which, at]
        )

    def pair(source, at, order, which):
        return pltpu.make_async_remote_copy(
            src_ref=source.at[rows_of(at), half_of(1 - core)],
            dst_ref=rows_ref.at[order, which, 1, rows_of(at)],
            send_sem=pair_send.at[order, which, at],
            recv_sem=pair_recv.at[order, which, at],
            device_id={"context": chip * 2 + 1 - core},
            device_id_type=pl.DeviceIdType.MESH,
        )

    def across(source, at, order, which, other):
        target = core + other - 2 * core * other
        return pltpu.make_async_remote_copy(
            src_ref=source.at[rows_of(at), half_of(target)],
            dst_ref=rows_ref.at[order, which, 2 + other, rows_of(at)],
            send_sem=row_send.at[order, which, other, at],
            recv_sem=row_recv.at[order, which, other, at],
            device_id={"context": (chip_x, chip_y)[order] * 2 + target},
            device_id_type=pl.DeviceIdType.MESH,
        )

    def deliver(source, owner, at):
        for order in range(2):
            near, later = (chip_x, chip_y)[order], (chip_y, chip_x)[order]

            @pl.when((owner == chip) | (owner == later))
            def _():
                which = jnp.where(owner == chip, 0, 1)
                keep(source, at, order, which).start()
                pair(source, at, order, which).start()

            @pl.when((owner == near) | (owner == chip_far))
            def _():
                which = jnp.where(owner == near, 0, 1)
                for other in range(2):
                    across(source, at, order, which, other).start()

    for at in range(PIECES):
        for side in range(2):
            @pl.when(has_target(side))
            def _():
                send(act_ref.at[rows_of(at)], me, at, side).start()

    @pl.loop(1, shard_count)
    def _(step):
        send_total(step).start()

    @pl.loop(0, PIECES)
    def _(at):
        deliver(act_ref, me, at)

    totals_ref[shard] = total_ref[...]

    for part in range(3):
        load(me, part).wait()

    @pl.loop(0, 3 * tiles)
    def _(tile):
        part = tile // tiles
        cols = pl.ds(pl.multiple_of(lax.rem(tile, tiles) * TILE, TILE), TILE)
        sums[part, :, cols] = jnp.dot(act_ref[...], weights[me, part, :, cols], preferred_element_type=F32)

    for distance in range(1, size):
        for side in range(2):
            owner = me + (2 * side - 1) * distance

            @pl.when((owner >= 0) & (owner < size))
            def _():
                for part in range(3):
                    load(owner, part).wait()

        @pl.loop(0, PIECES)
        def _(at):
            for side in range(2):
                owner = me + (2 * side - 1) * distance

                @pl.when((owner >= 0) & (owner < size))
                def _():
                    pltpu.make_async_copy(
                        every.at[owner, rows_of(at)], every.at[owner, rows_of(at)], recv_sem.at[owner, at]
                    ).wait()

                    @pl.when(has_target(side))
                    def _():
                        send(every.at[owner, rows_of(at)], owner, at, side).start()

                    deliver(every.at[owner], owner, at)

            @pl.loop(0, 2)
            def _(side):
                owner = me + (2 * side - 1) * distance

                @pl.when((owner >= 0) & (owner < size))
                def _():
                    @pl.loop(0, 3 * tiles)
                    def _(tile):
                        part = tile // tiles
                        cols = pl.ds(pl.multiple_of(lax.rem(tile, tiles) * TILE, TILE), TILE)
                        sums[part, rows_of(at), cols] += jnp.dot(
                            every[owner, rows_of(at), :], weights[owner, part, :, cols], preferred_element_type=F32
                        )

    live = live_ref[...]
    for part, ref in enumerate((q_ref, k_ref, v_ref)):
        @pl.loop(0, tiles)
        def _(tile):
            cols = pl.ds(pl.multiple_of(tile * TILE, TILE), TILE)
            ref[:, cols] = (sums[part, :, cols] * live).astype(BF16)

    for side in range(2):
        @pl.when(has_target(side))
        def _():
            for distance in range(size):
                owner = me + (2 * side - 1) * distance

                @pl.when((owner >= 0) & (owner < size))
                def _():
                    for at in range(PIECES):
                        send(every.at[owner, rows_of(at)], owner, at, side).wait_send()

    @pl.loop(1, shard_count)
    def _(step):
        peer = lax.rem(shard + step, shard_count)
        send_total(step).wait_send()
        pltpu.make_async_copy(total_ref, totals_ref.at[peer], total_recv.at[peer]).wait()

    @pl.loop(0, PIECES)
    def _(at):
        for order in range(2):
            for which in range(2):
                keep(act_ref, at, order, which).wait()
                pair(act_ref, at, order, which).wait()
                for other in range(2):
                    across(act_ref, at, order, which, other).wait()


def gather(activations, weight, live, total, shard_count, size):
    tokens, depth = activations.shape
    columns = weight.shape[2]
    half = size * depth // shard_count
    vmem = pl.BlockSpec(memory_space=pltpu.VMEM)
    heads_out = [jax.ShapeDtypeStruct((tokens, columns), BF16)] * 3
    return pl.pallas_call(
        gather_kernel,
        in_specs=[vmem] * 3 + [pl.BlockSpec(memory_space=pl.ANY)],
        out_specs=[vmem] * 5,
        out_shape=heads_out
        + [
            jax.ShapeDtypeStruct((shard_count,) + total.shape, F32),
            jax.ShapeDtypeStruct((2, 2, 4, tokens, half), BF16),
        ],
        scratch_shapes=[
            pltpu.VMEM((size, tokens, depth), BF16),
            pltpu.VMEM((size, 3, depth, columns), BF16),
            pltpu.VMEM((3, tokens, columns), F32),
            pltpu.SemaphoreType.DMA((size, 3)),
            pltpu.SemaphoreType.DMA((2, size, PIECES)),
            pltpu.SemaphoreType.DMA((size, PIECES)),
            pltpu.SemaphoreType.DMA((shard_count,)),
            pltpu.SemaphoreType.DMA((shard_count,)),
            pltpu.SemaphoreType.DMA((2, 2, PIECES)),
            pltpu.SemaphoreType.DMA((2, 2, PIECES)),
            pltpu.SemaphoreType.DMA((2, 2, PIECES)),
            pltpu.SemaphoreType.DMA((2, 2, 2, PIECES)),
            pltpu.SemaphoreType.DMA((2, 2, 2, PIECES)),
        ],
        compiler_params=pltpu.CompilerParams(collective_id=0, has_side_effects=True, vmem_limit_bytes=VMEM_GATHER << 20),
        name="gather",
    )(activations, live, total, weight)


def attend_kernel(scale, len_ref, totals_ref, q_ref, k_ref, v_ref, g_ref, c_ref, ct_ref, rows_ref, out_ref,
                  wide, own, pair, mixed, mixed_in, prefix, prefix_in, incoming, later, sums, grads, hop, hop_in,
                  own_sem, mixed_send, mixed_recv, prefix_sem, pair_send, pair_recv, near_send, near_recv,
                  relay_send, relay_recv, hop_send, hop_recv):
    shard = lax.axis_index("context")
    core, chip = lax.rem(shard, 2), shard // 2
    others = flips(chip)
    chip_x, chip_y, chip_far = others
    partner = chip * 2 + 1 - core
    tokens, columns = q_ref.shape
    heads = c_ref.shape[1]
    width = columns // heads
    half = heads // 2
    block = tokens // 2
    shard_count = lax.axis_size("context")
    is_low = core == 0

    barrier = pltpu.get_barrier_semaphore()
    for target in (partner, chip_x * 2 + core, chip_y * 2 + core, chip_far * 2 + core):
        pl.semaphore_signal(barrier, inc=1, device_id={"context": target}, device_id_type=pl.DeviceIdType.MESH)

    def move(source, target, send_sem, recv_sem, peer):
        return pltpu.make_async_remote_copy(
            src_ref=source, dst_ref=target, send_sem=send_sem, recv_sem=recv_sem,
            device_id={"context": peer}, device_id_type=pl.DeviceIdType.MESH,
        )

    def cols_of(head):
        return pl.ds(pl.multiple_of(head * width, width), width)

    for head in range(heads):
        wide[head] = jnp.broadcast_to(c_ref[:, head : head + 1], (tokens, width))

    @pl.loop(0, heads)
    def _(head):
        cols = cols_of(head)
        c = wide[head]
        total = c[tokens - 1 :, :]
        weighted_k = (k_ref[:, cols].astype(F32) * jnp.exp(total - c)).astype(BF16)
        own[0, head] = contract(weighted_k, v_ref[:, cols], ROWS).astype(BF16)
        weighted_q = (q_ref[:, cols].astype(F32) * (scale * jnp.exp(c))).astype(BF16)
        own[1, head] = contract(weighted_q, g_ref[:, cols], ROWS).astype(BF16)

    pl.semaphore_wait(barrier, 4)
    own_move = move(own, pair, own_sem.at[0], own_sem.at[1], partner)
    own_move.start()

    def intra(first, last):
        @pl.loop(first, last)
        def _(head):
            cols = cols_of(head)
            at = [slice(index * block, (index + 1) * block) for index in range(2)]
            q, k, v, g = [[ref[rows, cols] for rows in at] for ref in (q_ref, k_ref, v_ref, g_ref)]
            dq, dk, dv = [None] * 2, [None] * 2, [None] * 2

            def add(held, index, value):
                held[index] = value if held[index] is None else held[index] + value

            for t in range(2):
                column = jnp.concatenate([wide[head, at[t], :]] * (block // width), axis=1)
                for s in range(t + 1):
                    gap = column - ct_ref[pl.ds(head, 1), at[s]]
                    if s == t:
                        row_at = lax.broadcasted_iota(jnp.int32, (block, block), 0)
                        col_at = lax.broadcasted_iota(jnp.int32, (block, block), 1)
                        gap = jnp.where(row_at >= col_at, gap, -jnp.inf)
                    decay = jnp.exp(gap)
                    prob = (contract(q[t], k[s], LANES) * scale * decay).astype(BF16)
                    score = (contract(g[t], v[s], LANES) * decay).astype(BF16)
                    add(dq, t, contract(score, k[s], PLAIN))
                    add(dk, s, contract(score, q[t], ROWS))
                    add(dv, s, contract(prob, g[t], ROWS))
            for index in range(2):
                sums[0, head, at[index]] = scale * dq[index]
                sums[1, head, at[index]] = scale * dk[index]
                sums[2, head, at[index]] = dv[index]

    def factor(exponent):
        return jnp.exp(jnp.full((1, width), exponent, F32))

    def total_of(which, head):
        return totals_ref[which, head]

    intra(0, FIRST)
    own_move.wait()

    for at in range(half):
        head = core * half + at
        mine, theirs = [[ref[kind, head].astype(F32) for kind in range(2)] for ref in (own, pair)]
        low, high = [[jnp.where(is_low == first, mine[kind], theirs[kind]) for kind in range(2)] for first in (True, False)]
        mixed[0, at] = (factor(total_of(chip * 2 + 1, head)) * low[0] + high[0]).astype(BF16)
        mixed[1, at] = (low[1] + factor(total_of(chip * 2, head)) * high[1]).astype(BF16)

    def mixed_move(step):
        kind = jnp.where(others[step] > chip, 0, 1)
        return move(mixed.at[kind], mixed_in.at[step], mixed_send.at[step], mixed_recv.at[step], others[step] * 2 + core)

    for step in (2, 0, 1):
        mixed_move(step).start()

    intra(FIRST, SECOND)

    for step in range(3):
        mixed_move(step).wait()

    for at in range(half):
        head = core * half + at
        sum_in = jnp.zeros((width, width), F32)
        sum_later = jnp.zeros((width, width), F32)
        for step in range(3):
            peer = others[step]
            goes_up = peer > chip
            first = jnp.where(goes_up, chip, peer) * 2 + 1
            last = jnp.where(goes_up, peer, chip) * 2
            gap = jnp.float32(0.0)
            for which in range(shard_count):
                gap = gap + jnp.where((which > first) & (which < last), total_of(which, head), 0.0)
            term = factor(gap) * mixed_in[step, at].astype(F32)
            sum_in = sum_in + jnp.where(goes_up, 0.0, term)
            sum_later = sum_later + jnp.where(goes_up, term, 0.0)
        prefix[0, at] = sum_in.astype(BF16)
        prefix[1, at] = sum_later.astype(BF16)

    prefix_move = move(prefix, prefix_in, prefix_sem.at[0], prefix_sem.at[1], partner)
    prefix_move.start()
    intra(SECOND, heads)
    prefix_move.wait()

    for ref, side in ((prefix, core), (prefix_in, 1 - core)):
        for at in range(half):
            head = side * half + at
            sum_in, sum_later = ref[0, at].astype(F32), ref[1, at].astype(F32)
            incoming[head] = jnp.where(
                is_low, sum_in, factor(total_of(chip * 2, head)) * sum_in + pair[0, head].astype(F32)
            ).astype(BF16)
            later[head] = jnp.where(
                is_low, factor(total_of(chip * 2 + 1, head)) * sum_later + pair[1, head].astype(F32), sum_later
            ).astype(BF16)

    def pair_move(head):
        return move(grads.at[head, 0], grads.at[head, 1], pair_send.at[head], pair_recv.at[head], partner)

    def near_move(head):
        near = chip_x + lax.rem(head, 2) * (chip_y - chip_x)
        return move(grads.at[head, 0], grads.at[head, 2], near_send.at[head], near_recv.at[head], near * 2 + core)

    def relay_move(head):
        return move(grads.at[head, 2], grads.at[head, 3], relay_send.at[head], relay_recv.at[head], partner)

    def hop_move(head):
        target = chip_y + lax.rem(head, 2) * (chip_x - chip_y)
        return move(hop.at[head], hop_in.at[head], hop_send.at[head], hop_recv.at[head], target * 2 + core)

    live = lax.broadcasted_iota(jnp.int32, (tokens, width), 0) < len_ref[0]

    @pl.loop(0, heads)
    def _(head):
        cols = cols_of(head)
        c = wide[head]
        until = jnp.exp(c[tokens - 1 :, :] - c)
        k, v, g = k_ref[:, cols], v_ref[:, cols], g_ref[:, cols]
        dq = sums[0, head] + scale * jnp.exp(c) * contract(g, incoming[head], LANES)
        dk = sums[1, head] + until * contract(v, later[head], LANES)
        dv = sums[2, head] + until * contract(k, later[head], PLAIN)
        for part, value in enumerate((dq, dk, dv)):
            grads[head, 0, :, part * width : (part + 1) * width] = jnp.where(live, value, 0.0).astype(BF16)
        near_move(head).start()
        pair_move(head).start()

    def product(head, which):
        lhs = rows_ref[lax.rem(head, 2), which].reshape(4 * tokens, rows_ref.shape[-1])
        return contract(lhs, grads[head].reshape(4 * tokens, 3 * width), ROWS)

    @pl.loop(0, half)
    def _(at):
        for index in range(2):
            near_move(2 * at + index).wait_recv()
            relay_move(2 * at + index).start()

        @pl.loop(2 * at, 2 * at + 2)
        def _(head):
            pair_move(head).wait_recv()
            relay_move(head).wait_recv()
            hop[head] = product(head, 1).astype(BF16)
            hop_move(head).start()

        @pl.loop(2 * at, 2 * at + 2)
        def _(head):
            value = product(head, 0)
            for part in range(3):
                out_ref[part, :, cols_of(head)] = value[:, part * width : (part + 1) * width]

    @pl.loop(0, heads)
    def _(head):
        hop_move(head).wait_recv()
        for part in range(3):
            out_ref[part, :, cols_of(head)] += hop_in[head, :, part * width : (part + 1) * width].astype(F32)

    @pl.loop(0, heads)
    def _(head):
        near_move(head).wait_send()
        pair_move(head).wait_send()
        relay_move(head).wait_send()
        hop_move(head).wait_send()


def attend(scale, lengths, totals, q, k, v, out_grad, run_sum, rows):
    tokens, columns = q.shape
    heads = run_sum.shape[1]
    width = columns // heads
    half = heads // 2
    depth = rows.shape[-1]
    vmem = pl.BlockSpec(memory_space=pltpu.VMEM)
    smem = pl.BlockSpec(memory_space=pltpu.SMEM)
    dma = pltpu.SemaphoreType.DMA
    return pl.pallas_call(
        functools.partial(attend_kernel, scale),
        in_specs=[smem] * 2 + [vmem] * 7,
        out_specs=vmem,
        out_shape=jax.ShapeDtypeStruct((3, depth, columns), F32),
        scratch_shapes=[
            pltpu.VMEM((heads, tokens, width), F32),
            pltpu.VMEM((2, heads, width, width), BF16),
            pltpu.VMEM((2, heads, width, width), BF16),
            pltpu.VMEM((2, half, width, width), BF16),
            pltpu.VMEM((3, half, width, width), BF16),
            pltpu.VMEM((2, half, width, width), BF16),
            pltpu.VMEM((2, half, width, width), BF16),
            pltpu.VMEM((heads, width, width), BF16),
            pltpu.VMEM((heads, width, width), BF16),
            pltpu.VMEM((3, heads, tokens, width), F32),
            pltpu.VMEM((heads, 4, tokens, 3 * width), BF16),
            pltpu.VMEM((heads, depth, 3 * width), BF16),
            pltpu.VMEM((heads, depth, 3 * width), BF16),
            dma((2,)), dma((3,)), dma((3,)), dma((2,)),
        ] + [dma((heads,))] * 8,
        compiler_params=pltpu.CompilerParams(collective_id=1, has_side_effects=True, vmem_limit_bytes=VMEM_ATTEND << 20),
        name="attend",
    )(lengths, totals, q, k, v, out_grad, run_sum, run_sum.T, rows)


FIRST, SECOND = 2, 6
VMEM_GATHER, VMEM_ATTEND = 30, 30


def pick(value, bit, mine, me):
    at = (me >> (bit + 1)) & 1
    return lax.dynamic_index_in_dim(value, at if mine else 1 - at, value.ndim - 3 - bit, keepdims=True)


def scatter_sum(lhs, rhs, bits, me, size):
    def times(block):
        flat = block.reshape((-1,) + block.shape[-2:])
        if flat.shape[0] == 1:
            result = contract(flat[0], rhs, ROWS)
        else:
            result = contract(flat, rhs, ((1,), (0,)))
        return result.reshape(block.shape[:-2] + (block.shape[-1], rhs.shape[1]))

    received = []
    keep = lhs
    for bit in bits:
        send = times(pick(keep, bit, False, me))
        for value in received:
            send = send + pick(value, bit, False, me).astype(F32)
        keep = pick(keep, bit, True, me)
        received = [pick(value, bit, True, me) for value in received]
        received.append(swap(send.astype(BF16), size, 2 << bit))
    total = times(keep)
    for value in received:
        total = total + value.astype(F32)
    return total.reshape(lhs.shape[-1], rhs.shape[1])


def is_square(shard_count, size):
    chips = shard_count // 2
    return chips == size and chips.bit_length() - 1 == 2


def shards(activations, qkv_weight, log_decay, lengths, out_grad):
    size = lax.axis_size("context")
    me = lax.axis_index("context")
    core = me & 1
    chip = me >> 1
    chips = size // 2
    tokens = activations.shape[0]
    heads = log_decay.shape[1]
    columns = out_grad.shape[1]
    width = columns // heads
    half = heads // 2
    scale = width ** -0.5

    token_at = jnp.arange(tokens, dtype=jnp.int32)
    live = token_at < lengths[0]
    run_sum = jnp.cumsum(log_decay * live.astype(F32)[:, None], axis=0)
    run_wide = jnp.repeat(run_sum, width, axis=1)
    run_rows = run_sum.T
    own_total = run_sum[-1].astype(BF16).astype(F32)
    total_block = jnp.broadcast_to(jnp.pad(own_total, (0, 128 - heads))[None], (8, 128))
    live_column = live.astype(F32)[:, None]
    if is_square(size, lax.axis_size("tensor")):
        q, k, v, totals, rows = gather(
            activations, qkv_weight.transpose(1, 0, 2), live_column, total_block, size, lax.axis_size("tensor")
        )
        result = attend(scale, lengths, totals[:, 0, :heads], q, k, v, out_grad, run_sum, rows)
        return result.transpose(1, 0, 2)

    every, q, k, v, totals = project(
        activations, qkv_weight.transpose(1, 0, 2), live_column, total_block, size, lax.axis_size("tensor")
    )
    totals = totals[:, 0, :heads]

    rows = qkv_weight.shape[0] // size
    blocks = every.shape[2] // (2 * rows)
    low_rows, high_rows = [
        jnp.stack(
            [every[:, :, (2 * at + which) * rows : (2 * at + which + 1) * rows] for at in range(blocks)], axis=1
        ).reshape(chips, tokens, rows)
        for which in (0, 1)
    ]
    own_rows = jnp.where(core == 0, low_rows, high_rows)
    other_rows = swap(jnp.where(core == 0, high_rows, low_rows), size, 1)
    lhs = jnp.concatenate([own_rows, other_rows], axis=1)

    depth = chips.bit_length() - 1
    orders = (tuple(range(depth)), tuple(reversed(range(depth))))
    lhs = lhs.reshape((2,) * depth + lhs.shape[1:])
    lefts = []
    for order in orders:
        if not depth:
            lefts.append(lhs)
            continue
        moved = swap(pick(lhs, order[0], False, me), size, 2 << order[0])
        lefts.append(jnp.concatenate([pick(lhs, order[0], True, me), moved], axis=-2))

    head_spec = pl.BlockSpec((tokens, width), lambda h: (0, h))
    square_spec = pl.BlockSpec((1, width, width), lambda h: (h, 0, 0))
    wide = lambda kind: jax.ShapeDtypeStruct((tokens, columns), kind)
    squares = jax.ShapeDtypeStruct((heads, width, width), BF16)
    state, grad_state = pl.pallas_call(
        functools.partial(states_kernel, scale),
        grid=(heads,),
        in_specs=[head_spec] * 5,
        out_specs=[square_spec] * 2,
        out_shape=[squares] * 2,
        cost_estimate=pl.CostEstimate(flops=4 * tokens * columns * width, bytes_accessed=12 * tokens * columns, transcendentals=0),
        name="states",
    )(q, k, v, out_grad, run_wide)

    both = jnp.stack([state, grad_state])
    other = swap(both, size, 1)
    mine_half = lax.dynamic_slice_in_dim(both, core * half, half, 1).astype(F32)
    other_half = lax.dynamic_slice_in_dim(other, core * half, half, 1).astype(F32)
    pair_totals = lax.dynamic_slice_in_dim(totals, chip * 2, 2, 0)
    pair_half = lax.dynamic_slice_in_dim(pair_totals, core * half, half, 1)
    low, high = [jnp.where(core == which, mine_half, other_half) for which in (0, 1)]
    chip_state = (jnp.exp(pair_half[1])[:, None, None] * low[0] + high[0]).astype(BF16)
    chip_grad = (low[1] + jnp.exp(pair_half[0])[:, None, None] * high[1]).astype(BF16)

    arrivals = [
        swap(jnp.where((chip ^ step) > chip, chip_state, chip_grad), size, 2 * step) for step in range(1, chips)
    ]

    dq, dk, dv = pl.pallas_call(
        functools.partial(intra_kernel, scale),
        grid=(heads,),
        in_specs=[head_spec] * 5 + [pl.BlockSpec((heads, tokens), lambda h: (0, 0))],
        out_specs=[head_spec] * 3,
        out_shape=[wide(F32)] * 3,
        cost_estimate=pl.CostEstimate(
            flops=10 * tokens * tokens * columns, bytes_accessed=24 * tokens * columns, transcendentals=heads * tokens * tokens
        ),
        name="intra",
    )(q, k, v, out_grad, run_wide, run_rows)

    arrivals, dq, dk, dv = lax.optimization_barrier((arrivals, dq, dk, dv))
    upto = jnp.cumsum(totals, axis=0)
    totals_half = lax.dynamic_slice_in_dim(totals, core * half, half, 1)
    upto_half = lax.dynamic_slice_in_dim(upto, core * half, half, 1)
    chip_before = lax.dynamic_index_in_dim(upto_half - totals_half, chip * 2, 0, keepdims=False)
    chip_upto = lax.dynamic_index_in_dim(upto_half, chip * 2 + 1, 0, keepdims=False)
    incoming = jnp.zeros((half, width, width), F32)
    later = jnp.zeros((half, width, width), F32)
    for step in range(1, chips):
        peer = chip ^ step
        goes_up = peer > chip
        arrived = arrivals[step - 1].astype(F32)
        peer_upto = lax.dynamic_index_in_dim(upto_half, peer * 2 + 1, 0, keepdims=False)
        peer_before = lax.dynamic_index_in_dim(upto_half - totals_half, peer * 2, 0, keepdims=False)
        gap = jnp.where(goes_up, peer_before - chip_upto, chip_before - peer_upto)
        term = jnp.exp(gap)[:, None, None] * arrived
        incoming = incoming + jnp.where(goes_up, 0.0, term)
        later = later + jnp.where(goes_up, term, 0.0)
    from_chips = jnp.stack([incoming, later]).astype(BF16)
    other_chips = swap(from_chips, size, 1)
    is_low = core == 0
    from_chips = jnp.concatenate(
        [jnp.where(is_low, from_chips, other_chips), jnp.where(is_low, other_chips, from_chips)], axis=1
    ).astype(F32)
    incoming = jnp.where(
        is_low, from_chips[0], jnp.exp(pair_totals[0])[:, None, None] * from_chips[0] + other[0].astype(F32)
    ).astype(BF16)
    later = jnp.where(
        is_low, jnp.exp(pair_totals[1])[:, None, None] * from_chips[1] + other[1].astype(F32), from_chips[1]
    ).astype(BF16)

    grads = pl.pallas_call(
        functools.partial(inter_kernel, scale),
        grid=(heads,),
        in_specs=[pl.BlockSpec(memory_space=pltpu.SMEM)] + [head_spec] * 4 + [square_spec] * 2 + [head_spec] * 3,
        out_specs=[head_spec] * 3,
        out_shape=[wide(BF16)] * 3,
        cost_estimate=pl.CostEstimate(flops=6 * tokens * columns * width, bytes_accessed=28 * tokens * columns, transcendentals=0),
        name="inter",
    )(lengths, k, v, out_grad, run_wide, incoming, later, dq, dk, dv)

    results = []
    piece = columns // 2
    for part in grads:
        halves = [part[:, :piece], part[:, piece:]]
        if depth:
            moved = [swap(value, size, 2 << order[0]) for value, order in zip(halves, orders)]
            others = swap(jnp.concatenate(moved, axis=1), size, 1)
        partner = swap(part, size, 1)
        pieces = []
        for at, order in enumerate(orders):
            columns_at = slice(at * piece, (at + 1) * piece)
            rhs = [halves[at], partner[:, columns_at]]
            if depth:
                rhs += [moved[at], others[:, columns_at]]
            pieces.append(scatter_sum(lefts[at], jnp.concatenate(rhs, axis=0), order[1:], me, size))
        results.append(jnp.concatenate(pieces, axis=1))
    return jnp.stack(results, axis=1)


def solution(mesh):
    return jax.shard_map(
        shards,
        mesh=mesh,
        in_specs=(
            P("context", "tensor"),
            P(None, None, "tensor"),
            P("context", "tensor"),
            P("context"),
            P("context", "tensor"),
        ),
        out_specs=P("context", None, "tensor"),
        check_vma=False,
    )
```

```python
import functools

import jax
import jax.numpy as jnp
from jax import lax
from jax.experimental import pallas as pl
from jax.experimental.pallas import tpu as pltpu
from jax.sharding import PartitionSpec as P


F32 = jnp.float32
BF16 = jnp.bfloat16


def contract(a, b, dims):
    return lax.dot_general(a, b, (dims, ((), ())), preferred_element_type=F32)


ROWS = ((0,), (0,))
LANES = ((1,), (1,))
PLAIN = ((1,), (0,))


def states_kernel(scale, q_ref, k_ref, v_ref, g_ref, c_ref, state_ref, grad_ref):
    c = c_ref[...]
    total = c[-1:, :]
    weighted_k = (k_ref[...].astype(F32) * jnp.exp(total - c)).astype(BF16)
    state_ref[0] = contract(weighted_k, v_ref[...], ROWS).astype(BF16)
    weighted_q = (q_ref[...].astype(F32) * (scale * jnp.exp(c))).astype(BF16)
    grad_ref[0] = contract(weighted_q, g_ref[...], ROWS).astype(BF16)


def intra_kernel(scale, q_ref, k_ref, v_ref, g_ref, c_ref, ct_ref, dq_ref, dk_ref, dv_ref):
    head = pl.program_id(0)
    q, k, v, g = q_ref[...], k_ref[...], v_ref[...], g_ref[...]
    tokens, width = q.shape
    column = jnp.concatenate([c_ref[...]] * (tokens // width), axis=1)
    gap = column - ct_ref[pl.ds(head, 1), :]
    row_at = lax.broadcasted_iota(jnp.int32, (tokens, tokens), 0)
    col_at = lax.broadcasted_iota(jnp.int32, (tokens, tokens), 1)
    decay = jnp.exp(jnp.where(row_at >= col_at, gap, -jnp.inf))
    prob = (contract(q, k, LANES) * scale * decay).astype(BF16)
    score = (contract(g, v, LANES) * decay).astype(BF16)
    dq_ref[...] = scale * contract(score, k, PLAIN)
    dk_ref[...] = scale * contract(score, q, ROWS)
    dv_ref[...] = contract(prob, g, ROWS)


def inter_kernel(scale, len_ref, k_ref, v_ref, g_ref, c_ref, in_ref, later_ref, dq_ref, dk_ref, dv_ref,
                 oq_ref, ok_ref, ov_ref):
    c = c_ref[...]
    live = lax.broadcasted_iota(jnp.int32, c.shape, 0) < len_ref[0]
    until = jnp.exp(c[-1:, :] - c)
    dq = dq_ref[...] + scale * jnp.exp(c) * contract(g_ref[...], in_ref[0], LANES)
    dk = dk_ref[...] + until * contract(v_ref[...], later_ref[0], LANES)
    dv = dv_ref[...] + until * contract(k_ref[...], later_ref[0], PLAIN)
    oq_ref[...] = jnp.where(live, dq, 0.0).astype(BF16)
    ok_ref[...] = jnp.where(live, dk, 0.0).astype(BF16)
    ov_ref[...] = jnp.where(live, dv, 0.0).astype(BF16)


def swap(value, size, distance):
    return lax.ppermute(value, "context", [(i, i ^ distance) for i in range(size)])


PIECES = 4
TILE = 256


def project_kernel(act_ref, live_ref, total_ref, weight_ref, every_ref, q_ref, k_ref, v_ref, totals_ref,
                   weights, sums, own_sem, weight_sem, send_sem, recv_sem, total_send, total_recv):
    size, me = lax.axis_size("tensor"), lax.axis_index("tensor")
    shard_count, shard = lax.axis_size("context"), lax.axis_index("context")
    depth = act_ref.shape[1]
    piece = act_ref.shape[0] // PIECES
    columns = q_ref.shape[1]
    tiles = columns // TILE

    def load(owner, part):
        rows = pl.ds(pl.multiple_of(owner * depth, depth), depth)
        return pltpu.make_async_copy(weight_ref.at[part, rows], weights.at[owner, part], weight_sem.at[owner, part])

    for at in range(size):
        owner = lax.rem(me + at, size)
        for part in range(3):
            load(owner, part).start()

    barrier = pltpu.get_barrier_semaphore()
    for target in (me - 1, me + 1):
        @pl.when((target >= 0) & (target < size))
        def _():
            pl.semaphore_signal(barrier, inc=1, device_id={"tensor": target}, device_id_type=pl.DeviceIdType.MESH)

    @pl.loop(1, shard_count)
    def _(step):
        peer = lax.rem(shard + step, shard_count)
        pl.semaphore_signal(barrier, inc=1, device_id={"context": peer}, device_id_type=pl.DeviceIdType.MESH)

    neighbours = jnp.where(me > 0, 1, 0) + jnp.where(me < size - 1, 1, 0)
    pl.semaphore_wait(barrier, neighbours + shard_count - 1)

    def rows_of(at):
        return pl.ds(pl.multiple_of(at * piece, piece), piece)

    def send(source, owner, at, side):
        return pltpu.make_async_remote_copy(
            src_ref=source,
            dst_ref=every_ref.at[owner, rows_of(at)],
            send_sem=send_sem.at[side, owner, at],
            recv_sem=recv_sem.at[owner, at],
            device_id={"tensor": me + 1 - 2 * side},
            device_id_type=pl.DeviceIdType.MESH,
        )

    def has_target(side):
        target = me + 1 - 2 * side
        return (target >= 0) & (target < size)

    def send_total(step):
        peer = lax.rem(shard + step, shard_count)
        return pltpu.make_async_remote_copy(
            src_ref=total_ref,
            dst_ref=totals_ref.at[shard],
            send_sem=total_send.at[peer],
            recv_sem=total_recv.at[shard],
            device_id={"context": peer},
            device_id_type=pl.DeviceIdType.MESH,
        )

    for at in range(PIECES):
        for side in range(2):
            @pl.when(has_target(side))
            def _():
                send(act_ref.at[rows_of(at)], me, at, side).start()

    @pl.loop(1, shard_count)
    def _(step):
        send_total(step).start()

    own = pltpu.make_async_copy(act_ref, every_ref.at[me], own_sem)
    own.start()
    totals_ref[shard] = total_ref[...]

    for part in range(3):
        load(me, part).wait()

    @pl.loop(0, 3 * tiles)
    def _(tile):
        part = tile // tiles
        cols = pl.ds(pl.multiple_of(lax.rem(tile, tiles) * TILE, TILE), TILE)
        sums[part, :, cols] = jnp.dot(act_ref[...], weights[me, part, :, cols], preferred_element_type=F32)

    own.wait()
    for distance in range(1, size):
        for side in range(2):
            owner = me + (2 * side - 1) * distance

            @pl.when((owner >= 0) & (owner < size))
            def _():
                for part in range(3):
                    load(owner, part).wait()

        @pl.loop(0, PIECES)
        def _(at):
            for side in range(2):
                owner = me + (2 * side - 1) * distance

                @pl.when((owner >= 0) & (owner < size))
                def _():
                    pltpu.make_async_copy(
                        every_ref.at[owner, rows_of(at)], every_ref.at[owner, rows_of(at)], recv_sem.at[owner, at]
                    ).wait()

                    @pl.when(has_target(side))
                    def _():
                        send(every_ref.at[owner, rows_of(at)], owner, at, side).start()

            @pl.loop(0, 2)
            def _(side):
                owner = me + (2 * side - 1) * distance

                @pl.when((owner >= 0) & (owner < size))
                def _():
                    @pl.loop(0, 3 * tiles)
                    def _(tile):
                        part = tile // tiles
                        cols = pl.ds(pl.multiple_of(lax.rem(tile, tiles) * TILE, TILE), TILE)
                        sums[part, rows_of(at), cols] += jnp.dot(
                            every_ref[owner, rows_of(at), :], weights[owner, part, :, cols], preferred_element_type=F32
                        )

    live = live_ref[...]
    for part, ref in enumerate((q_ref, k_ref, v_ref)):
        @pl.loop(0, tiles)
        def _(tile):
            cols = pl.ds(pl.multiple_of(tile * TILE, TILE), TILE)
            ref[:, cols] = (sums[part, :, cols] * live).astype(BF16)

    for side in range(2):
        @pl.when(has_target(side))
        def _():
            for distance in range(size):
                owner = me + (2 * side - 1) * distance

                @pl.when((owner >= 0) & (owner < size))
                def _():
                    for at in range(PIECES):
                        send(every_ref.at[owner, rows_of(at)], owner, at, side).wait_send()

    @pl.loop(1, shard_count)
    def _(step):
        peer = lax.rem(shard + step, shard_count)
        send_total(step).wait_send()
        pltpu.make_async_copy(total_ref, totals_ref.at[peer], total_recv.at[peer]).wait()


def project(activations, weight, live, total, shard_count, size):
    tokens, depth = activations.shape
    columns = weight.shape[2]
    vmem = pl.BlockSpec(memory_space=pltpu.VMEM)
    heads_out = [jax.ShapeDtypeStruct((tokens, columns), BF16)] * 3
    return pl.pallas_call(
        project_kernel,
        in_specs=[vmem] * 3 + [pl.BlockSpec(memory_space=pl.ANY)],
        out_specs=[vmem] * 5,
        out_shape=[jax.ShapeDtypeStruct((size, tokens, depth), BF16)]
        + heads_out
        + [jax.ShapeDtypeStruct((shard_count,) + total.shape, F32)],
        scratch_shapes=[
            pltpu.VMEM((size, 3, depth, columns), BF16),
            pltpu.VMEM((3, tokens, columns), F32),
            pltpu.SemaphoreType.DMA,
            pltpu.SemaphoreType.DMA((size, 3)),
            pltpu.SemaphoreType.DMA((2, size, PIECES)),
            pltpu.SemaphoreType.DMA((size, PIECES)),
            pltpu.SemaphoreType.DMA((shard_count,)),
            pltpu.SemaphoreType.DMA((shard_count,)),
        ],
        compiler_params=pltpu.CompilerParams(collective_id=0, has_side_effects=True, vmem_limit_bytes=48 << 20),
        name="project",
    )(activations, live, total, weight)


def flips(chip):
    bx, by = lax.rem(chip, 2), chip // 2
    return chip + 1 - 2 * bx, chip + 2 - 4 * by, 3 - chip


def fused_kernel(scale, len_ref, act_ref, decay_ref, grad_ref, weight_ref, out_ref,
                 every, decay, run, wide, totals, own_total, qkv, g_ref, sums, rows_ref, acc, own, pair, mixed, mixed_in,
                 prefix, prefix_in, incoming, later,
                 input_sem, weight_sem, send_sem, recv_sem, total_send, total_recv, local_sem, mate_send, mate_recv,
                 row_send, row_recv, own_send, own_recv, mixed_send, mixed_recv, prefix_sem, pair_send, pair_recv,
                 near_send, near_recv, relay_send, relay_recv, hop_send, hop_recv, ready):
    size, me = lax.axis_size("tensor"), lax.axis_index("tensor")
    shard_count, shard = lax.axis_size("context"), lax.axis_index("context")
    core, chip = lax.rem(shard, 2), shard // 2
    others = flips(chip)
    chip_x, chip_y, chip_far = others
    partner = chip * 2 + 1 - core
    is_low = core == 0
    tokens, depth = act_ref.shape
    columns = grad_ref.shape[1]
    heads = decay_ref.shape[0]
    width = columns // heads
    half = heads // 2
    piece = tokens // PIECES
    tiles = columns // TILE
    strip = rows_ref.shape[-1]
    block = tokens // 2
    last = jnp.maximum(me, size - 1 - me)

    def move(source, target, send_at, recv_at, peer):
        return pltpu.make_async_remote_copy(
            src_ref=source, dst_ref=target, send_sem=send_at, recv_sem=recv_at,
            device_id={"context": peer}, device_id_type=pl.DeviceIdType.MESH,
        )

    def rows_of(at):
        return pl.ds(pl.multiple_of(at * piece, piece), piece)

    def cols_of(head):
        return pl.ds(pl.multiple_of(head * width, width), width)

    def strip_of(which):
        return pl.ds(pl.multiple_of(which * strip, strip), strip)

    def at_order(index):
        return lax.rem(core * half + index, heads)

    def send(source, owner, at, side):
        return pltpu.make_async_remote_copy(
            src_ref=source,
            dst_ref=every.at[owner, rows_of(at)],
            send_sem=send_sem.at[side, owner, at],
            recv_sem=recv_sem.at[owner, at],
            device_id={"tensor": me + 1 - 2 * side},
            device_id_type=pl.DeviceIdType.MESH,
        )

    def has_target(side):
        target = me + 1 - 2 * side
        return (target >= 0) & (target < size)

    def send_total(step):
        peer = lax.rem(shard + step, shard_count)
        return move(own_total, totals.at[shard], total_send.at[peer], total_recv.at[shard], peer)

    def keep(source, at, order, which):
        return pltpu.make_async_copy(
            source.at[rows_of(at), strip_of(core)], rows_ref.at[order, which, 0, rows_of(at)], local_sem.at[order, which, at]
        )

    def mate(source, at, order, which):
        return move(
            source.at[rows_of(at), strip_of(1 - core)], rows_ref.at[order, which, 1, rows_of(at)],
            mate_send.at[order, which, at], mate_recv.at[order, which, at], partner,
        )

    def across(source, at, order, which, other):
        target = core + other - 2 * core * other
        return move(
            source.at[rows_of(at), strip_of(target)], rows_ref.at[order, which, 2 + other, rows_of(at)],
            row_send.at[order, which, other, at], row_recv.at[order, which, other, at], others[order] * 2 + target,
        )

    def deliver(source, owner, at):
        for order in range(2):
            near, far = others[order], others[1 - order]

            @pl.when((owner == near) | (owner == chip_far))
            def _():
                which = jnp.where(owner == near, 0, 1)
                for other in range(2):
                    across(source, at, order, which, other).start()

            @pl.when((owner == chip) | (owner == far))
            def _():
                which = jnp.where(owner == chip, 0, 1)
                keep(source, at, order, which).start()
                mate(source, at, order, which).start()

    act_copy = pltpu.make_async_copy(act_ref, every.at[me], input_sem.at[0])
    decay_copy = pltpu.make_async_copy(decay_ref, decay, input_sem.at[1])
    grad_copy = pltpu.make_async_copy(grad_ref, g_ref, input_sem.at[2])

    barrier = pltpu.get_barrier_semaphore()
    for target in (me - 1, me + 1):
        @pl.when((target >= 0) & (target < size))
        def _():
            pl.semaphore_signal(barrier, inc=1, device_id={"tensor": target}, device_id_type=pl.DeviceIdType.MESH)

    @pl.loop(1, shard_count)
    def _(step):
        peer = lax.rem(shard + step, shard_count)
        pl.semaphore_signal(barrier, inc=1, device_id={"context": peer}, device_id_type=pl.DeviceIdType.MESH)

    act_copy.start()
    decay_copy.start()
    act_copy.wait()
    decay_copy.wait()
    neighbours = jnp.where(me > 0, 1, 0) + jnp.where(me < size - 1, 1, 0)
    pl.semaphore_wait(barrier, neighbours + shard_count - 1)

    for at in range(PIECES):
        for side in range(2):
            @pl.when(has_target(side))
            def _():
                send(every.at[me, rows_of(at)], me, at, side).start()

    @pl.loop(0, PIECES)
    def _(at):
        deliver(every.at[me], me, at)

    def running_sums():
        token_at = lax.broadcasted_iota(jnp.int32, (heads, tokens), 1)
        masked = jnp.where(token_at < len_ref[0], decay[...], 0.0)
        row_at = lax.broadcasted_iota(jnp.int32, (tokens, tokens), 0)
        col_at = lax.broadcasted_iota(jnp.int32, (tokens, tokens), 1)
        upto = jnp.where(row_at <= col_at, 1.0, 0.0)
        c = lax.dot_general(
            masked, upto, (PLAIN, ((), ())), precision=lax.Precision.HIGHEST, preferred_element_type=F32
        )
        run[...] = c
        total = c[:, tokens - 1 :].astype(BF16).astype(F32)
        own_total[...] = jnp.broadcast_to(total, own_total.shape)
        totals[shard] = jnp.broadcast_to(total, own_total.shape)
        column = jnp.concatenate([c, jnp.zeros((width - heads, tokens), F32)], axis=0).T
        for head in range(heads):
            wide[head] = jnp.broadcast_to(column[:, head : head + 1], (tokens, width))

    def states(at):
        @pl.loop(0, heads)
        def _(head):
            cols, rows = cols_of(head), rows_of(at)
            c = wide[head, rows, :]
            total = wide[head, tokens - 1 :, :]
            weighted_k = (qkv[1, rows, cols].astype(F32) * jnp.exp(total - c)).astype(BF16)
            acc[0, head] += contract(weighted_k, qkv[2, rows, cols], ROWS)
            weighted_q = (qkv[0, rows, cols].astype(F32) * (scale * jnp.exp(c))).astype(BF16)
            acc[1, head] += contract(weighted_q, g_ref[rows, cols], ROWS)

    def project_all(weights):
        def load(owner, part):
            rows = pl.ds(pl.multiple_of(owner * depth, depth), depth)
            return pltpu.make_async_copy(weight_ref.at[part, rows], weights.at[owner, part], weight_sem.at[owner, part])

        for at in range(size):
            owner = lax.rem(me + at, size)
            for part in range(3):
                load(owner, part).start()
        grad_copy.start()

        running_sums()

        @pl.loop(1, shard_count)
        def _(step):
            send_total(step).start()

        acc[...] = jnp.zeros_like(acc)
        for part in range(3):
            load(me, part).wait()

        def tile_at(tile):
            return tile // tiles, pl.ds(pl.multiple_of(lax.rem(tile, tiles) * TILE, TILE), TILE)

        @pl.loop(0, 3 * tiles)
        def _(tile):
            part, cols = tile_at(tile)
            sums[part, :, cols] = jnp.dot(every[me], weights[me, part, :, cols], preferred_element_type=F32)

        grad_copy.wait()

        for distance in range(1, size):
            for side in range(2):
                owner = me + (2 * side - 1) * distance

                @pl.when((owner >= 0) & (owner < size))
                def _():
                    for part in range(3):
                        load(owner, part).wait()

            @pl.loop(0, PIECES)
            def _(at):
                rows = rows_of(at)
                for side in range(2):
                    owner = me + (2 * side - 1) * distance

                    @pl.when((owner >= 0) & (owner < size))
                    def _():
                        pltpu.make_async_copy(
                            every.at[owner, rows], every.at[owner, rows], recv_sem.at[owner, at]
                        ).wait()

                        @pl.when(has_target(side))
                        def _():
                            send(every.at[owner, rows], owner, at, side).start()

                        deliver(every.at[owner], owner, at)

                @pl.loop(0, 2)
                def _(side):
                    owner = me + (2 * side - 1) * distance
                    valid = (owner >= 0) & (owner < size)

                    def product(part, cols):
                        return sums[part, rows, cols] + jnp.dot(
                            every[owner, rows, :], weights[owner, part, :, cols], preferred_element_type=F32
                        )

                    @pl.when(valid & (distance < last))
                    def _():
                        @pl.loop(0, 3 * tiles)
                        def _(tile):
                            part, cols = tile_at(tile)
                            sums[part, rows, cols] = product(part, cols)

                    if distance >= size // 2:
                        @pl.when(valid & (distance == last))
                        def _():
                            token_at = at * piece + lax.broadcasted_iota(jnp.int32, (piece, TILE), 0)
                            live = token_at < len_ref[0]

                            @pl.loop(0, 3 * tiles)
                            def _(tile):
                                part, cols = tile_at(tile)
                                qkv[part, rows, cols] = jnp.where(live, product(part, cols), 0.0).astype(BF16)

                            states(at)

    pl.run_scoped(project_all, pltpu.VMEM((size, 3, depth, columns), BF16))
    own[...] = acc[...].astype(BF16)

    def half_move(index):
        side = index + core - 2 * index * core
        part = pl.ds((1 - side) * half, half)
        return move(own.at[:, part], pair.at[:, part], own_send.at[index], own_recv.at[index], partner)

    def half_wait(index):
        side = index + core - 2 * index * core
        part = pl.ds(side * half, half)
        pltpu.make_async_copy(pair.at[:, part], pair.at[:, part], own_recv.at[index]).wait()

    def mixed_move(step):
        kind = jnp.where(others[step] > chip, 0, 1)
        return move(mixed.at[kind], mixed_in.at[step], mixed_send.at[step], mixed_recv.at[step], others[step] * 2 + core)

    prefix_move = move(prefix, prefix_in, prefix_sem.at[0], prefix_sem.at[1], partner)

    def total_of(which, head):
        return totals[which, pl.ds(head, 1), :]

    def intra(first, stop):
        @pl.loop(first, stop)
        def _(index):
            head = at_order(index)
            cols = cols_of(head)
            at = [slice(part * block, (part + 1) * block) for part in range(2)]
            q, k, v = [[qkv[part, rows, cols] for rows in at] for part in range(3)]
            g = [g_ref[rows, cols] for rows in at]
            dq, dk, dv = [None] * 2, [None] * 2, [None] * 2

            def add(held, part, value):
                held[part] = value if held[part] is None else held[part] + value

            for t in range(2):
                column = jnp.concatenate([wide[head, at[t], :]] * (block // width), axis=1)
                for s in range(t + 1):
                    gap = column - run[pl.ds(head, 1), at[s]]
                    if s == t:
                        row_at = lax.broadcasted_iota(jnp.int32, (block, block), 0)
                        col_at = lax.broadcasted_iota(jnp.int32, (block, block), 1)
                        gap = jnp.where(row_at >= col_at, gap, -jnp.inf)
                    decayed = jnp.exp(gap)
                    prob = (contract(q[t], k[s], LANES) * scale * decayed).astype(BF16)
                    score = (contract(g[t], v[s], LANES) * decayed).astype(BF16)
                    add(dq, t, contract(score, k[s], PLAIN))
                    add(dk, s, contract(score, q[t], ROWS))
                    add(dv, s, contract(prob, g[t], ROWS))
            for part in range(2):
                sums[0, at[part], cols] = scale * dq[part]
                sums[1, at[part], cols] = scale * dk[part]
                sums[2, at[part], cols] = dv[part]

    def spread(ref, at, head):
        sum_in, sum_later = ref[0, at].astype(F32), ref[1, at].astype(F32)
        incoming[head] = jnp.where(
            is_low, sum_in, jnp.exp(total_of(chip * 2, head)) * sum_in + pair[0, head].astype(F32)
        ).astype(BF16)
        later[head] = jnp.where(
            is_low, jnp.exp(total_of(chip * 2 + 1, head)) * sum_later + pair[1, head].astype(F32), sum_later
        ).astype(BF16)

    def finish_all(grads, hop, hop_in):
        for target in (partner, chip_x * 2 + core, chip_y * 2 + core):
            pl.semaphore_signal(ready, inc=1, device_id={"context": target}, device_id_type=pl.DeviceIdType.MESH)

        for index in range(2):
            half_move(index).start()

        @pl.loop(1, shard_count)
        def _(step):
            peer = lax.rem(shard + step, shard_count)
            pltpu.make_async_copy(own_total, totals.at[peer], total_recv.at[peer]).wait()

        intra(0, FIRST)
        half_wait(0)

        for at in range(half):
            head = core * half + at
            mine, theirs = [[ref[kind, head].astype(F32) for kind in range(2)] for ref in (own, pair)]
            low, high = [
                [jnp.where(is_low == first, mine[kind], theirs[kind]) for kind in range(2)] for first in (True, False)
            ]
            mixed[0, at] = (jnp.exp(total_of(chip * 2 + 1, head)) * low[0] + high[0]).astype(BF16)
            mixed[1, at] = (low[1] + jnp.exp(total_of(chip * 2, head)) * high[1]).astype(BF16)

        for step in (2, 0, 1):
            mixed_move(step).start()

        intra(FIRST, SECOND)
        half_wait(1)
        for step in range(3):
            mixed_move(step).wait_recv()

        for at in range(half):
            head = core * half + at
            sum_in = jnp.zeros((width, width), F32)
            sum_later = jnp.zeros((width, width), F32)
            for step in range(3):
                peer = others[step]
                goes_up = peer > chip
                first = jnp.where(goes_up, chip, peer) * 2 + 1
                stop = jnp.where(goes_up, peer, chip) * 2
                gap = jnp.zeros((1, width), F32)
                for which in range(shard_count):
                    gap = gap + jnp.where((which > first) & (which < stop), total_of(which, head), 0.0)
                term = jnp.exp(gap) * mixed_in[step, at].astype(F32)
                sum_in = sum_in + jnp.where(goes_up, 0.0, term)
                sum_later = sum_later + jnp.where(goes_up, term, 0.0)
            prefix[0, at] = sum_in.astype(BF16)
            prefix[1, at] = sum_later.astype(BF16)

        prefix_move.start()
        for at in range(half):
            spread(prefix, at, core * half + at)
        pl.semaphore_wait(ready, 3)

        def pair_move(head):
            return move(grads.at[head, 0], grads.at[head, 1], pair_send.at[head], pair_recv.at[head], partner)

        def near_move(head):
            near = chip_x + lax.rem(head, 2) * (chip_y - chip_x)
            return move(grads.at[head, 0], grads.at[head, 2], near_send.at[head], near_recv.at[head], near * 2 + core)

        def relay_move(head):
            return move(grads.at[head, 2], grads.at[head, 3], relay_send.at[head], relay_recv.at[head], partner)

        def hop_move(head):
            target = chip_y + lax.rem(head, 2) * (chip_x - chip_y)
            return move(hop.at[head], hop_in.at[head], hop_send.at[head], hop_recv.at[head], target * 2 + core)

        live = lax.broadcasted_iota(jnp.int32, (tokens, width), 0) < len_ref[0]

        def inter(first, stop):
            @pl.loop(first, stop)
            def _(index):
                head = at_order(index)
                cols = cols_of(head)
                c = wide[head]
                until = jnp.exp(wide[head, tokens - 1 :, :] - c)
                k, v, g = qkv[1, :, cols], qkv[2, :, cols], g_ref[:, cols]
                dq = sums[0, :, cols] + scale * jnp.exp(c) * contract(g, incoming[head], LANES)
                dk = sums[1, :, cols] + until * contract(v, later[head], LANES)
                dv = sums[2, :, cols] + until * contract(k, later[head], PLAIN)
                for part, value in enumerate((dq, dk, dv)):
                    grads[head, 0, :, part * width : (part + 1) * width] = jnp.where(live, value, 0.0).astype(BF16)
                near_move(head).start()
                pair_move(head).start()

        inter(0, half)
        intra(SECOND, heads)
        prefix_move.wait_recv()
        for at in range(half):
            spread(prefix_in, at, (1 - core) * half + at)
        inter(half, heads)

        @pl.loop(0, PIECES)
        def _(at):
            for order in range(2):
                for which in range(2):
                    keep(every.at[me], at, order, which).wait()
                    mate(every.at[me], at, order, which).wait_recv()
                    for other in range(2):
                        across(every.at[me], at, order, which, other).wait_recv()

        def product(head, which):
            lhs = rows_ref[lax.rem(head, 2), which].reshape(4 * tokens, strip)
            return contract(lhs, grads[head].reshape(4 * tokens, 3 * width), ROWS)

        def relay(index):
            head = at_order(index)
            near_move(head).wait_recv()
            relay_move(head).start()

        @pl.loop(0, half)
        def _(index):
            relay(index)

        @pl.loop(0, half // 2)
        def _(group):
            for index in range(2):
                relay(half + 2 * group + index)

            def head_at(index):
                return 2 * group + lax.rem(index, 2) + (index // 2) * half

            @pl.loop(0, 4)
            def _(index):
                head = head_at(index)
                pair_move(head).wait_recv()
                relay_move(head).wait_recv()
                hop[head] = product(head, 1).astype(BF16)
                hop_move(head).start()

            @pl.loop(0, 4)
            def _(index):
                head = head_at(index)
                value = product(head, 0)
                for part in range(3):
                    out_ref[part, :, cols_of(head)] = value[:, part * width : (part + 1) * width]

        @pl.loop(0, heads)
        def _(index):
            head = 2 * (index // 4) + lax.rem(index, 2) + (lax.rem(index, 4) // 2) * half
            hop_move(head).wait_recv()
            for part in range(3):
                out_ref[part, :, cols_of(head)] += hop_in[head, :, part * width : (part + 1) * width].astype(F32)

        @pl.loop(0, heads)
        def _(head):
            near_move(head).wait_send()
            pair_move(head).wait_send()
            relay_move(head).wait_send()
            hop_move(head).wait_send()

    pl.run_scoped(
        finish_all,
        pltpu.VMEM((heads, 4, tokens, 3 * width), BF16),
        pltpu.VMEM((heads, strip, 3 * width), BF16),
        pltpu.VMEM((heads, strip, 3 * width), BF16),
    )

    for side in range(2):
        @pl.when(has_target(side))
        def _():
            for distance in range(size):
                owner = me + (2 * side - 1) * distance

                @pl.when((owner >= 0) & (owner < size))
                def _():
                    for at in range(PIECES):
                        send(every.at[owner, rows_of(at)], owner, at, side).wait_send()

    @pl.loop(1, shard_count)
    def _(step):
        send_total(step).wait_send()

    @pl.loop(0, PIECES)
    def _(at):
        for order in range(2):
            for which in range(2):
                mate(every.at[me], at, order, which).wait_send()
                for other in range(2):
                    across(every.at[me], at, order, which, other).wait_send()

    for index in range(2):
        half_move(index).wait_send()
    for step in range(3):
        mixed_move(step).wait_send()
    prefix_move.wait_send()


def fused(scale, lengths, activations, decay, out_grad, weight, shard_count, size):
    tokens, depth = activations.shape
    columns = out_grad.shape[1]
    heads = decay.shape[0]
    width = columns // heads
    half = heads // 2
    strip = size * depth // shard_count
    dma = pltpu.SemaphoreType.DMA
    away = pl.BlockSpec(memory_space=pltpu.HBM)
    return pl.pallas_call(
        functools.partial(fused_kernel, scale),
        in_specs=[pl.BlockSpec(memory_space=pltpu.SMEM)] + [away] * 4,
        out_specs=pl.BlockSpec(memory_space=pltpu.VMEM),
        out_shape=jax.ShapeDtypeStruct((3, strip, columns), F32),
        scratch_shapes=[
            pltpu.VMEM((size, tokens, depth), BF16),
            pltpu.VMEM((heads, tokens), F32),
            pltpu.VMEM((heads, tokens), F32),
            pltpu.VMEM((heads, tokens, width), F32),
            pltpu.VMEM((shard_count, heads, width), F32),
            pltpu.VMEM((heads, width), F32),
            pltpu.VMEM((3, tokens, columns), BF16),
            pltpu.VMEM((tokens, columns), BF16),
            pltpu.VMEM((3, tokens, columns), F32),
            pltpu.VMEM((2, 2, 4, tokens, strip), BF16),
            pltpu.VMEM((2, heads, width, width), F32),
            pltpu.VMEM((2, heads, width, width), BF16),
            pltpu.VMEM((2, heads, width, width), BF16),
            pltpu.VMEM((2, half, width, width), BF16),
            pltpu.VMEM((3, half, width, width), BF16),
            pltpu.VMEM((2, half, width, width), BF16),
            pltpu.VMEM((2, half, width, width), BF16),
            pltpu.VMEM((heads, width, width), BF16),
            pltpu.VMEM((heads, width, width), BF16),
            dma((3,)),
            dma((size, 3)),
            dma((2, size, PIECES)),
            dma((size, PIECES)),
            dma((shard_count,)),
            dma((shard_count,)),
            dma((2, 2, PIECES)),
            dma((2, 2, PIECES)),
            dma((2, 2, PIECES)),
            dma((2, 2, 2, PIECES)),
            dma((2, 2, 2, PIECES)),
            dma((2,)),
            dma((2,)),
            dma((3,)),
            dma((3,)),
            dma((2,)),
        ] + [dma((heads,))] * 8 + [pltpu.SemaphoreType.REGULAR],
        compiler_params=pltpu.CompilerParams(collective_id=1, has_side_effects=True, vmem_limit_bytes=GRANT << 20),
        name="fused",
    )(lengths, activations, decay, out_grad, weight)


FIRST, SECOND = 2, 6
GRANT = 44


def pick(value, bit, mine, me):
    at = (me >> (bit + 1)) & 1
    return lax.dynamic_index_in_dim(value, at if mine else 1 - at, value.ndim - 3 - bit, keepdims=True)


def scatter_sum(lhs, rhs, bits, me, size):
    def times(block):
        flat = block.reshape((-1,) + block.shape[-2:])
        if flat.shape[0] == 1:
            result = contract(flat[0], rhs, ROWS)
        else:
            result = contract(flat, rhs, ((1,), (0,)))
        return result.reshape(block.shape[:-2] + (block.shape[-1], rhs.shape[1]))

    received = []
    keep = lhs
    for bit in bits:
        send = times(pick(keep, bit, False, me))
        for value in received:
            send = send + pick(value, bit, False, me).astype(F32)
        keep = pick(keep, bit, True, me)
        received = [pick(value, bit, True, me) for value in received]
        received.append(swap(send.astype(BF16), size, 2 << bit))
    total = times(keep)
    for value in received:
        total = total + value.astype(F32)
    return total.reshape(lhs.shape[-1], rhs.shape[1])


def is_square(shard_count, size):
    chips = shard_count // 2
    return chips == size and chips.bit_length() - 1 == 2


def shards(activations, qkv_weight, log_decay, lengths, out_grad):
    size = lax.axis_size("context")
    me = lax.axis_index("context")
    core = me & 1
    chip = me >> 1
    chips = size // 2
    tokens = activations.shape[0]
    heads = log_decay.shape[1]
    columns = out_grad.shape[1]
    width = columns // heads
    half = heads // 2
    scale = width ** -0.5

    if is_square(size, lax.axis_size("tensor")):
        return fused(
            scale, lengths, activations, log_decay.T, out_grad, qkv_weight.transpose(1, 0, 2), size, lax.axis_size("tensor")
        ).transpose(1, 0, 2)

    token_at = jnp.arange(tokens, dtype=jnp.int32)
    live = token_at < lengths[0]
    run_sum = jnp.cumsum(log_decay * live.astype(F32)[:, None], axis=0)
    run_wide = jnp.repeat(run_sum, width, axis=1)
    run_rows = run_sum.T
    own_total = run_sum[-1].astype(BF16).astype(F32)
    total_block = jnp.broadcast_to(jnp.pad(own_total, (0, 128 - heads))[None], (8, 128))
    live_column = live.astype(F32)[:, None]
    every, q, k, v, totals = project(
        activations, qkv_weight.transpose(1, 0, 2), live_column, total_block, size, lax.axis_size("tensor")
    )
    totals = totals[:, 0, :heads]

    rows = qkv_weight.shape[0] // size
    blocks = every.shape[2] // (2 * rows)
    low_rows, high_rows = [
        jnp.stack(
            [every[:, :, (2 * at + which) * rows : (2 * at + which + 1) * rows] for at in range(blocks)], axis=1
        ).reshape(chips, tokens, rows)
        for which in (0, 1)
    ]
    own_rows = jnp.where(core == 0, low_rows, high_rows)
    other_rows = swap(jnp.where(core == 0, high_rows, low_rows), size, 1)
    lhs = jnp.concatenate([own_rows, other_rows], axis=1)

    depth = chips.bit_length() - 1
    orders = (tuple(range(depth)), tuple(reversed(range(depth))))
    lhs = lhs.reshape((2,) * depth + lhs.shape[1:])
    lefts = []
    for order in orders:
        if not depth:
            lefts.append(lhs)
            continue
        moved = swap(pick(lhs, order[0], False, me), size, 2 << order[0])
        lefts.append(jnp.concatenate([pick(lhs, order[0], True, me), moved], axis=-2))

    head_spec = pl.BlockSpec((tokens, width), lambda h: (0, h))
    square_spec = pl.BlockSpec((1, width, width), lambda h: (h, 0, 0))
    wide = lambda kind: jax.ShapeDtypeStruct((tokens, columns), kind)
    squares = jax.ShapeDtypeStruct((heads, width, width), BF16)
    state, grad_state = pl.pallas_call(
        functools.partial(states_kernel, scale),
        grid=(heads,),
        in_specs=[head_spec] * 5,
        out_specs=[square_spec] * 2,
        out_shape=[squares] * 2,
        cost_estimate=pl.CostEstimate(flops=4 * tokens * columns * width, bytes_accessed=12 * tokens * columns, transcendentals=0),
        name="states",
    )(q, k, v, out_grad, run_wide)

    both = jnp.stack([state, grad_state])
    other = swap(both, size, 1)
    mine_half = lax.dynamic_slice_in_dim(both, core * half, half, 1).astype(F32)
    other_half = lax.dynamic_slice_in_dim(other, core * half, half, 1).astype(F32)
    pair_totals = lax.dynamic_slice_in_dim(totals, chip * 2, 2, 0)
    pair_half = lax.dynamic_slice_in_dim(pair_totals, core * half, half, 1)
    low, high = [jnp.where(core == which, mine_half, other_half) for which in (0, 1)]
    chip_state = (jnp.exp(pair_half[1])[:, None, None] * low[0] + high[0]).astype(BF16)
    chip_grad = (low[1] + jnp.exp(pair_half[0])[:, None, None] * high[1]).astype(BF16)

    arrivals = [
        swap(jnp.where((chip ^ step) > chip, chip_state, chip_grad), size, 2 * step) for step in range(1, chips)
    ]

    dq, dk, dv = pl.pallas_call(
        functools.partial(intra_kernel, scale),
        grid=(heads,),
        in_specs=[head_spec] * 5 + [pl.BlockSpec((heads, tokens), lambda h: (0, 0))],
        out_specs=[head_spec] * 3,
        out_shape=[wide(F32)] * 3,
        cost_estimate=pl.CostEstimate(
            flops=10 * tokens * tokens * columns, bytes_accessed=24 * tokens * columns, transcendentals=heads * tokens * tokens
        ),
        name="intra",
    )(q, k, v, out_grad, run_wide, run_rows)

    arrivals, dq, dk, dv = lax.optimization_barrier((arrivals, dq, dk, dv))
    upto = jnp.cumsum(totals, axis=0)
    totals_half = lax.dynamic_slice_in_dim(totals, core * half, half, 1)
    upto_half = lax.dynamic_slice_in_dim(upto, core * half, half, 1)
    chip_before = lax.dynamic_index_in_dim(upto_half - totals_half, chip * 2, 0, keepdims=False)
    chip_upto = lax.dynamic_index_in_dim(upto_half, chip * 2 + 1, 0, keepdims=False)
    incoming = jnp.zeros((half, width, width), F32)
    later = jnp.zeros((half, width, width), F32)
    for step in range(1, chips):
        peer = chip ^ step
        goes_up = peer > chip
        arrived = arrivals[step - 1].astype(F32)
        peer_upto = lax.dynamic_index_in_dim(upto_half, peer * 2 + 1, 0, keepdims=False)
        peer_before = lax.dynamic_index_in_dim(upto_half - totals_half, peer * 2, 0, keepdims=False)
        gap = jnp.where(goes_up, peer_before - chip_upto, chip_before - peer_upto)
        term = jnp.exp(gap)[:, None, None] * arrived
        incoming = incoming + jnp.where(goes_up, 0.0, term)
        later = later + jnp.where(goes_up, term, 0.0)
    from_chips = jnp.stack([incoming, later]).astype(BF16)
    other_chips = swap(from_chips, size, 1)
    is_low = core == 0
    from_chips = jnp.concatenate(
        [jnp.where(is_low, from_chips, other_chips), jnp.where(is_low, other_chips, from_chips)], axis=1
    ).astype(F32)
    incoming = jnp.where(
        is_low, from_chips[0], jnp.exp(pair_totals[0])[:, None, None] * from_chips[0] + other[0].astype(F32)
    ).astype(BF16)
    later = jnp.where(
        is_low, jnp.exp(pair_totals[1])[:, None, None] * from_chips[1] + other[1].astype(F32), from_chips[1]
    ).astype(BF16)

    grads = pl.pallas_call(
        functools.partial(inter_kernel, scale),
        grid=(heads,),
        in_specs=[pl.BlockSpec(memory_space=pltpu.SMEM)] + [head_spec] * 4 + [square_spec] * 2 + [head_spec] * 3,
        out_specs=[head_spec] * 3,
        out_shape=[wide(BF16)] * 3,
        cost_estimate=pl.CostEstimate(flops=6 * tokens * columns * width, bytes_accessed=28 * tokens * columns, transcendentals=0),
        name="inter",
    )(lengths, k, v, out_grad, run_wide, incoming, later, dq, dk, dv)

    results = []
    piece = columns // 2
    for part in grads:
        halves = [part[:, :piece], part[:, piece:]]
        if depth:
            moved = [swap(value, size, 2 << order[0]) for value, order in zip(halves, orders)]
            others = swap(jnp.concatenate(moved, axis=1), size, 1)
        partner = swap(part, size, 1)
        pieces = []
        for at, order in enumerate(orders):
            columns_at = slice(at * piece, (at + 1) * piece)
            rhs = [halves[at], partner[:, columns_at]]
            if depth:
                rhs += [moved[at], others[:, columns_at]]
            pieces.append(scatter_sum(lefts[at], jnp.concatenate(rhs, axis=0), order[1:], me, size))
        results.append(jnp.concatenate(pieces, axis=1))
    return jnp.stack(results, axis=1)


def solution(mesh):
    return jax.shard_map(
        shards,
        mesh=mesh,
        in_specs=(
            P("context", "tensor"),
            P(None, None, "tensor"),
            P("context", "tensor"),
            P("context"),
            P("context", "tensor"),
        ),
        out_specs=P("context", None, "tensor"),
        check_vma=False,
    )
```

```python
import functools

import jax
import jax.numpy as jnp
from jax import lax
from jax.experimental import pallas as pl
from jax.experimental.pallas import tpu as pltpu
from jax.sharding import PartitionSpec as P


F32 = jnp.float32
BF16 = jnp.bfloat16


def contract(a, b, dims):
    return lax.dot_general(a, b, (dims, ((), ())), preferred_element_type=F32)


ROWS = ((0,), (0,))
LANES = ((1,), (1,))
PLAIN = ((1,), (0,))


def states_kernel(scale, q_ref, k_ref, v_ref, g_ref, c_ref, state_ref, grad_ref):
    c = c_ref[...]
    total = c[-1:, :]
    weighted_k = (k_ref[...].astype(F32) * jnp.exp(total - c)).astype(BF16)
    state_ref[0] = contract(weighted_k, v_ref[...], ROWS).astype(BF16)
    weighted_q = (q_ref[...].astype(F32) * (scale * jnp.exp(c))).astype(BF16)
    grad_ref[0] = contract(weighted_q, g_ref[...], ROWS).astype(BF16)


def intra_kernel(scale, q_ref, k_ref, v_ref, g_ref, c_ref, ct_ref, dq_ref, dk_ref, dv_ref):
    head = pl.program_id(0)
    q, k, v, g = q_ref[...], k_ref[...], v_ref[...], g_ref[...]
    tokens, width = q.shape
    column = jnp.concatenate([c_ref[...]] * (tokens // width), axis=1)
    gap = column - ct_ref[pl.ds(head, 1), :]
    row_at = lax.broadcasted_iota(jnp.int32, (tokens, tokens), 0)
    col_at = lax.broadcasted_iota(jnp.int32, (tokens, tokens), 1)
    decay = jnp.exp(jnp.where(row_at >= col_at, gap, -jnp.inf))
    prob = (contract(q, k, LANES) * scale * decay).astype(BF16)
    score = (contract(g, v, LANES) * decay).astype(BF16)
    dq_ref[...] = scale * contract(score, k, PLAIN)
    dk_ref[...] = scale * contract(score, q, ROWS)
    dv_ref[...] = contract(prob, g, ROWS)


def inter_kernel(scale, len_ref, k_ref, v_ref, g_ref, c_ref, in_ref, later_ref, dq_ref, dk_ref, dv_ref,
                 oq_ref, ok_ref, ov_ref):
    c = c_ref[...]
    live = lax.broadcasted_iota(jnp.int32, c.shape, 0) < len_ref[0]
    until = jnp.exp(c[-1:, :] - c)
    dq = dq_ref[...] + scale * jnp.exp(c) * contract(g_ref[...], in_ref[0], LANES)
    dk = dk_ref[...] + until * contract(v_ref[...], later_ref[0], LANES)
    dv = dv_ref[...] + until * contract(k_ref[...], later_ref[0], PLAIN)
    oq_ref[...] = jnp.where(live, dq, 0.0).astype(BF16)
    ok_ref[...] = jnp.where(live, dk, 0.0).astype(BF16)
    ov_ref[...] = jnp.where(live, dv, 0.0).astype(BF16)


def swap(value, size, distance):
    return lax.ppermute(value, "context", [(i, i ^ distance) for i in range(size)])


PIECES = 4
TILE = 512


def project_kernel(act_ref, live_ref, total_ref, weight_ref, every_ref, q_ref, k_ref, v_ref, totals_ref,
                   weights, sums, own_sem, weight_sem, send_sem, recv_sem, total_send, total_recv):
    size, me = lax.axis_size("tensor"), lax.axis_index("tensor")
    shard_count, shard = lax.axis_size("context"), lax.axis_index("context")
    depth = act_ref.shape[1]
    piece = act_ref.shape[0] // PIECES
    columns = q_ref.shape[1]
    tiles = columns // TILE

    def load(owner, part):
        rows = pl.ds(pl.multiple_of(owner * depth, depth), depth)
        return pltpu.make_async_copy(weight_ref.at[part, rows], weights.at[owner, part], weight_sem.at[owner, part])

    for at in range(size):
        owner = lax.rem(me + at, size)
        for part in range(3):
            load(owner, part).start()

    barrier = pltpu.get_barrier_semaphore()
    for target in (me - 1, me + 1):
        @pl.when((target >= 0) & (target < size))
        def _():
            pl.semaphore_signal(barrier, inc=1, device_id={"tensor": target}, device_id_type=pl.DeviceIdType.MESH)

    @pl.loop(1, shard_count)
    def _(step):
        peer = lax.rem(shard + step, shard_count)
        pl.semaphore_signal(barrier, inc=1, device_id={"context": peer}, device_id_type=pl.DeviceIdType.MESH)

    neighbours = jnp.where(me > 0, 1, 0) + jnp.where(me < size - 1, 1, 0)
    pl.semaphore_wait(barrier, neighbours + shard_count - 1)

    def rows_of(at):
        return pl.ds(pl.multiple_of(at * piece, piece), piece)

    def send(source, owner, at, side):
        return pltpu.make_async_remote_copy(
            src_ref=source,
            dst_ref=every_ref.at[owner, rows_of(at)],
            send_sem=send_sem.at[side, owner, at],
            recv_sem=recv_sem.at[owner, at],
            device_id={"tensor": me + 1 - 2 * side},
            device_id_type=pl.DeviceIdType.MESH,
        )

    def has_target(side):
        target = me + 1 - 2 * side
        return (target >= 0) & (target < size)

    def send_total(step):
        peer = lax.rem(shard + step, shard_count)
        return pltpu.make_async_remote_copy(
            src_ref=total_ref,
            dst_ref=totals_ref.at[shard],
            send_sem=total_send.at[peer],
            recv_sem=total_recv.at[shard],
            device_id={"context": peer},
            device_id_type=pl.DeviceIdType.MESH,
        )

    for at in range(PIECES):
        for side in range(2):
            @pl.when(has_target(side))
            def _():
                send(act_ref.at[rows_of(at)], me, at, side).start()

    @pl.loop(1, shard_count)
    def _(step):
        send_total(step).start()

    own = pltpu.make_async_copy(act_ref, every_ref.at[me], own_sem)
    own.start()
    totals_ref[shard] = total_ref[...]

    for part in range(3):
        load(me, part).wait()

    @pl.loop(0, 3 * tiles)
    def _(tile):
        part = tile // tiles
        cols = pl.ds(pl.multiple_of(lax.rem(tile, tiles) * TILE, TILE), TILE)
        sums[part, :, cols] = jnp.dot(act_ref[...], weights[me, part, :, cols], preferred_element_type=F32)

    own.wait()
    for distance in range(1, size):
        for side in range(2):
            owner = me + (2 * side - 1) * distance

            @pl.when((owner >= 0) & (owner < size))
            def _():
                for part in range(3):
                    load(owner, part).wait()

        @pl.loop(0, PIECES)
        def _(at):
            for side in range(2):
                owner = me + (2 * side - 1) * distance

                @pl.when((owner >= 0) & (owner < size))
                def _():
                    pltpu.make_async_copy(
                        every_ref.at[owner, rows_of(at)], every_ref.at[owner, rows_of(at)], recv_sem.at[owner, at]
                    ).wait()

                    @pl.when(has_target(side))
                    def _():
                        send(every_ref.at[owner, rows_of(at)], owner, at, side).start()

            @pl.loop(0, 2)
            def _(side):
                owner = me + (2 * side - 1) * distance

                @pl.when((owner >= 0) & (owner < size))
                def _():
                    @pl.loop(0, 3 * tiles)
                    def _(tile):
                        part = tile // tiles
                        cols = pl.ds(pl.multiple_of(lax.rem(tile, tiles) * TILE, TILE), TILE)
                        sums[part, rows_of(at), cols] += jnp.dot(
                            every_ref[owner, rows_of(at), :], weights[owner, part, :, cols], preferred_element_type=F32
                        )

    live = live_ref[...]
    for part, ref in enumerate((q_ref, k_ref, v_ref)):
        @pl.loop(0, tiles)
        def _(tile):
            cols = pl.ds(pl.multiple_of(tile * TILE, TILE), TILE)
            ref[:, cols] = (sums[part, :, cols] * live).astype(BF16)

    for side in range(2):
        @pl.when(has_target(side))
        def _():
            for distance in range(size):
                owner = me + (2 * side - 1) * distance

                @pl.when((owner >= 0) & (owner < size))
                def _():
                    for at in range(PIECES):
                        send(every_ref.at[owner, rows_of(at)], owner, at, side).wait_send()

    @pl.loop(1, shard_count)
    def _(step):
        peer = lax.rem(shard + step, shard_count)
        send_total(step).wait_send()
        pltpu.make_async_copy(total_ref, totals_ref.at[peer], total_recv.at[peer]).wait()


def project(activations, weight, live, total, shard_count, size):
    tokens, depth = activations.shape
    columns = weight.shape[2]
    vmem = pl.BlockSpec(memory_space=pltpu.VMEM)
    heads_out = [jax.ShapeDtypeStruct((tokens, columns), BF16)] * 3
    return pl.pallas_call(
        project_kernel,
        in_specs=[vmem] * 3 + [pl.BlockSpec(memory_space=pl.ANY)],
        out_specs=[vmem] * 5,
        out_shape=[jax.ShapeDtypeStruct((size, tokens, depth), BF16)]
        + heads_out
        + [jax.ShapeDtypeStruct((shard_count,) + total.shape, F32)],
        scratch_shapes=[
            pltpu.VMEM((size, 3, depth, columns), BF16),
            pltpu.VMEM((3, tokens, columns), F32),
            pltpu.SemaphoreType.DMA,
            pltpu.SemaphoreType.DMA((size, 3)),
            pltpu.SemaphoreType.DMA((2, size, PIECES)),
            pltpu.SemaphoreType.DMA((size, PIECES)),
            pltpu.SemaphoreType.DMA((shard_count,)),
            pltpu.SemaphoreType.DMA((shard_count,)),
        ],
        compiler_params=pltpu.CompilerParams(collective_id=0, has_side_effects=True, vmem_limit_bytes=48 << 20),
        name="project",
    )(activations, live, total, weight)


def flips(chip):
    bx, by = lax.rem(chip, 2), chip // 2
    return chip + 1 - 2 * bx, chip + 2 - 4 * by, 3 - chip


def fused_kernel(scale, len_ref, act_ref, decay_ref, grad_ref, weight_ref, out_ref,
                 every, decay, run, wide, totals, own_total, qkv, g_ref, sums, rows_ref, acc, own, pair, mixed, mixed_in,
                 prefix, prefix_in, incoming, later, detour,
                 input_sem, weight_sem, send_sem, recv_sem, total_send, total_recv, local_sem, mate_send, mate_recv,
                 row_send, row_recv, own_send, own_recv, mixed_send, mixed_recv, prefix_sem, pair_send, pair_recv,
                 near_send, near_recv, relay_send, relay_recv, hop_send, hop_recv, detour_recv, detour_send, ready, opened):
    size, me = lax.axis_size("tensor"), lax.axis_index("tensor")
    shard_count, shard = lax.axis_size("context"), lax.axis_index("context")
    core, chip = lax.rem(shard, 2), shard // 2
    others = flips(chip)
    chip_x, chip_y, chip_far = others
    partner = chip * 2 + 1 - core
    is_low = core == 0
    tokens, depth = act_ref.shape
    columns = grad_ref.shape[1]
    heads = decay_ref.shape[0]
    width = columns // heads
    half = heads // 2
    piece = tokens // PIECES
    tiles = columns // TILE
    strip = rows_ref.shape[-1]
    block = tokens // 2
    last = jnp.maximum(me, size - 1 - me)
    is_end = (me == 0) | (me == size - 1)
    inward = jnp.where(me == 0, 1, size - 2)
    is_inner = (me == 1) | (me == size - 2)
    outward = jnp.where(me == 1, 0, size - 1)

    def move(source, target, send_at, recv_at, peer):
        return pltpu.make_async_remote_copy(
            src_ref=source, dst_ref=target, send_sem=send_at, recv_sem=recv_at,
            device_id={"context": peer}, device_id_type=pl.DeviceIdType.MESH,
        )

    def whole(view, sem):
        return pltpu.make_async_copy(view, view, sem)

    def rows_of(at):
        return pl.ds(pl.multiple_of(at * piece, piece), piece)

    def cols_of(head):
        return pl.ds(pl.multiple_of(head * width, width), width)

    def strip_of(which):
        return pl.ds(pl.multiple_of(which * strip, strip), strip)

    def at_order(index):
        return lax.rem(core * half + index, heads)

    def send(source, owner, at, side):
        return pltpu.make_async_remote_copy(
            src_ref=source,
            dst_ref=every.at[owner, rows_of(at)],
            send_sem=send_sem.at[side, owner],
            recv_sem=recv_sem.at[owner, at],
            device_id={"tensor": me + 1 - 2 * side},
            device_id_type=pl.DeviceIdType.MESH,
        )

    def has_target(side):
        target = me + 1 - 2 * side
        return (target >= 0) & (target < size)

    def send_total(step):
        peer = lax.rem(shard + step, shard_count)
        return move(own_total, totals.at[shard], total_send, total_recv, peer)

    def keep(source, at, order, which):
        return pltpu.make_async_copy(
            source.at[rows_of(at), strip_of(core)], rows_ref.at[order, which, 0, rows_of(at)], local_sem
        )

    def mate(source, at, order, which):
        return move(
            source.at[rows_of(at), strip_of(1 - core)], rows_ref.at[order, which, 1, rows_of(at)],
            mate_send, mate_recv, partner,
        )

    def across(source, at, order, which, other):
        target = core + other - 2 * core * other
        return move(
            source.at[rows_of(at), strip_of(target)], rows_ref.at[order, which, 2 + other, rows_of(at)],
            row_send, row_recv, others[order] * 2 + target,
        )

    def deliver(source, owner, at):
        for order in range(2):
            near, far = others[order], others[1 - order]

            @pl.when((owner == near) | (owner == chip_far))
            def _():
                which = jnp.where(owner == near, 0, 1)
                for other in range(2):
                    across(source, at, order, which, other).start()

            @pl.when((owner == chip) | (owner == far))
            def _():
                which = jnp.where(owner == chip, 0, 1)
                keep(source, at, order, which).start()
                mate(source, at, order, which).start()

    act_copy = pltpu.make_async_copy(act_ref, every.at[me], input_sem.at[0])
    decay_copy = pltpu.make_async_copy(decay_ref, decay, input_sem.at[1])
    grad_copy = pltpu.make_async_copy(grad_ref, g_ref, input_sem.at[2])

    barrier = pltpu.get_barrier_semaphore()
    for target in (me - 1, me + 1):
        @pl.when((target >= 0) & (target < size))
        def _():
            pl.semaphore_signal(barrier, inc=1, device_id={"tensor": target}, device_id_type=pl.DeviceIdType.MESH)

    @pl.loop(1, shard_count)
    def _(step):
        peer = lax.rem(shard + step, shard_count)
        pl.semaphore_signal(barrier, inc=1, device_id={"context": peer}, device_id_type=pl.DeviceIdType.MESH)

    @pl.when(is_inner)
    def _():
        for near in (chip_x, chip_y):
            pl.semaphore_signal(
                barrier, inc=1, device_id={"context": near * 2 + core, "tensor": outward}, device_id_type=pl.DeviceIdType.MESH
            )

    act_copy.start()
    decay_copy.start()
    act_copy.wait()
    decay_copy.wait()
    neighbours = jnp.where(me > 0, 1, 0) + jnp.where(me < size - 1, 1, 0) + jnp.where(is_end, 2, 0)
    pl.semaphore_wait(barrier, neighbours + shard_count - 1)

    for at in range(PIECES):
        for side in range(2):
            @pl.when(has_target(side))
            def _():
                send(every.at[me, rows_of(at)], me, at, side).start()

    @pl.loop(0, PIECES)
    def _(at):
        deliver(every.at[me], me, at)

    def running_sums():
        token_at = lax.broadcasted_iota(jnp.int32, (heads, tokens), 1)
        masked = jnp.where(token_at < len_ref[0], decay[...], 0.0)
        row_at = lax.broadcasted_iota(jnp.int32, (tokens, tokens), 0)
        col_at = lax.broadcasted_iota(jnp.int32, (tokens, tokens), 1)
        upto = jnp.where(row_at <= col_at, 1.0, 0.0)
        c = lax.dot_general(
            masked, upto, (PLAIN, ((), ())), precision=lax.Precision.HIGHEST, preferred_element_type=F32
        )
        run[...] = c
        total = c[:, tokens - 1 :].astype(BF16).astype(F32)
        own_total[...] = jnp.broadcast_to(total, own_total.shape)
        totals[shard] = jnp.broadcast_to(total, own_total.shape)
        column = jnp.concatenate([c, jnp.zeros((width - heads, tokens), F32)], axis=0).T
        for head in range(heads):
            wide[head] = jnp.broadcast_to(column[:, head : head + 1], (tokens, width))

    def states(at):
        @pl.loop(0, heads, unroll=UNROLL)
        def _(head):
            cols, rows = cols_of(head), rows_of(at)
            c = wide[head, rows, :]
            total = wide[head, tokens - 1 :, :]
            weighted_k = (qkv[1, rows, cols].astype(F32) * jnp.exp(total - c)).astype(BF16)
            acc[0, head] += contract(weighted_k, qkv[2, rows, cols], ROWS)
            weighted_q = (qkv[0, rows, cols].astype(F32) * (scale * jnp.exp(c))).astype(BF16)
            acc[1, head] += contract(weighted_q, g_ref[rows, cols], ROWS)

    def project_all(weights):
        def load(owner, part):
            rows = pl.ds(pl.multiple_of(owner * depth, depth), depth)
            return pltpu.make_async_copy(weight_ref.at[part, rows], weights.at[owner, part], weight_sem.at[owner])

        def loaded(owner):
            return pltpu.make_async_copy(weights.at[owner], weights.at[owner], weight_sem.at[owner])

        for at in range(size):
            owner = lax.rem(me + at, size)
            for part in range(3):
                load(owner, part).start()
        grad_copy.start()

        running_sums()

        @pl.loop(1, shard_count)
        def _(step):
            send_total(step).start()

        acc[...] = jnp.zeros_like(acc)
        loaded(me).wait()

        def tile_at(tile):
            return tile // tiles, pl.ds(pl.multiple_of(lax.rem(tile, tiles) * TILE, TILE), TILE)

        @pl.loop(0, 3 * tiles)
        def _(tile):
            part, cols = tile_at(tile)
            sums[part, :, cols] = jnp.dot(every[me], weights[me, part, :, cols], preferred_element_type=F32)

        grad_copy.wait()

        for distance in range(1, size):
            for side in range(2):
                owner = me + (2 * side - 1) * distance

                @pl.when((owner >= 0) & (owner < size))
                def _():
                    loaded(owner).wait()

            @pl.loop(0, PIECES)
            def _(at):
                rows = rows_of(at)
                for side in range(2):
                    owner = me + (2 * side - 1) * distance

                    @pl.when((owner >= 0) & (owner < size))
                    def _():
                        pltpu.make_async_copy(
                            every.at[owner, rows], every.at[owner, rows], recv_sem.at[owner, at]
                        ).wait()

                        @pl.when(has_target(side))
                        def _():
                            send(every.at[owner, rows], owner, at, side).start()

                        deliver(every.at[owner], owner, at)

                @pl.loop(0, 2)
                def _(side):
                    owner = me + (2 * side - 1) * distance
                    valid = (owner >= 0) & (owner < size)

                    def product(part, cols):
                        return sums[part, rows, cols] + jnp.dot(
                            every[owner, rows, :], weights[owner, part, :, cols], preferred_element_type=F32
                        )

                    @pl.when(valid & (distance < last))
                    def _():
                        @pl.loop(0, 3 * tiles)
                        def _(tile):
                            part, cols = tile_at(tile)
                            sums[part, rows, cols] = product(part, cols)

                    if distance >= size // 2:
                        @pl.when(valid & (distance == last))
                        def _():
                            token_at = at * piece + lax.broadcasted_iota(jnp.int32, (piece, TILE), 0)
                            live = token_at < len_ref[0]

                            @pl.loop(0, 3 * tiles)
                            def _(tile):
                                part, cols = tile_at(tile)
                                qkv[part, rows, cols] = jnp.where(live, product(part, cols), 0.0).astype(BF16)

                            states(at)

    pl.run_scoped(project_all, pltpu.VMEM((size, 3, depth, columns), BF16))
    own[...] = acc[...].astype(BF16)

    def half_move(index):
        side = index + core - 2 * index * core
        part = pl.ds((1 - side) * half, half)
        return move(own.at[:, part], pair.at[:, part], own_send.at[index], own_recv.at[index], partner)

    def half_wait(index):
        side = index + core - 2 * index * core
        part = pl.ds(side * half, half)
        pltpu.make_async_copy(pair.at[:, part], pair.at[:, part], own_recv.at[index]).wait()

    def mixed_move(step):
        kind = jnp.where(others[step] > chip, 0, 1)
        return move(mixed.at[kind], mixed_in.at[step], mixed_send.at[step], mixed_recv.at[step], others[step] * 2 + core)

    prefix_move = move(prefix, prefix_in, prefix_sem.at[0], prefix_sem.at[1], partner)

    def total_of(which, head):
        return totals[which, pl.ds(head, 1), :]

    def intra(first, stop):
        @pl.loop(first, stop)
        def _(index):
            head = at_order(index)
            cols = cols_of(head)
            at = [slice(part * block, (part + 1) * block) for part in range(2)]
            q, k, v = [[qkv[part, rows, cols] for rows in at] for part in range(3)]
            g = [g_ref[rows, cols] for rows in at]
            dq, dk, dv = [None] * 2, [None] * 2, [None] * 2

            def add(held, part, value):
                held[part] = value if held[part] is None else held[part] + value

            for t in range(2):
                column = jnp.concatenate([wide[head, at[t], :]] * (block // width), axis=1)
                for s in range(t + 1):
                    gap = column - run[pl.ds(head, 1), at[s]]
                    if s == t:
                        row_at = lax.broadcasted_iota(jnp.int32, (block, block), 0)
                        col_at = lax.broadcasted_iota(jnp.int32, (block, block), 1)
                        gap = jnp.where(row_at >= col_at, gap, -jnp.inf)
                    decayed = jnp.exp(gap)
                    prob = (contract(q[t], k[s], LANES) * scale * decayed).astype(BF16)
                    score = (contract(g[t], v[s], LANES) * decayed).astype(BF16)
                    add(dq, t, contract(score, k[s], PLAIN))
                    add(dk, s, contract(score, q[t], ROWS))
                    add(dv, s, contract(prob, g[t], ROWS))
            for part in range(2):
                sums[0, at[part], cols] = scale * dq[part]
                sums[1, at[part], cols] = scale * dk[part]
                sums[2, at[part], cols] = dv[part]

    def spread(ref, at, head):
        sum_in, sum_later = ref[0, at].astype(F32), ref[1, at].astype(F32)
        incoming[head] = jnp.where(
            is_low, sum_in, jnp.exp(total_of(chip * 2, head)) * sum_in + pair[0, head].astype(F32)
        ).astype(BF16)
        later[head] = jnp.where(
            is_low, jnp.exp(total_of(chip * 2 + 1, head)) * sum_later + pair[1, head].astype(F32), sum_later
        ).astype(BF16)

    def settle():
        for side in range(2):
            @pl.when(has_target(side))
            def _():
                for distance in range(size):
                    owner = me + (2 * side - 1) * distance

                    @pl.when((owner >= 0) & (owner < size))
                    def _():
                        whole(every.at[owner], send_sem.at[side, owner]).wait()

        whole(totals.at[pl.ds(0, shard_count - 1)], total_send).wait()
        whole(rows_ref.at[:, :, 1], mate_send).wait()
        whole(rows_ref.at[:, :, pl.ds(2, 2)], row_send).wait()

        for index in range(2):
            half_move(index).wait_send()
        for step in range(3):
            mixed_move(step).wait_send()
        prefix_move.wait_send()

    def finish_all(grads, hop, hop_in):
        for target in (partner, chip_x * 2 + core, chip_y * 2 + core):
            pl.semaphore_signal(ready, inc=1, device_id={"context": target}, device_id_type=pl.DeviceIdType.MESH)

        @pl.when(is_end)
        def _():
            pl.semaphore_signal(opened, inc=1, device_id={"tensor": inward}, device_id_type=pl.DeviceIdType.MESH)

        for index in range(2):
            half_move(index).start()

        whole(totals.at[pl.ds(0, shard_count - 1)], total_recv).wait()

        intra(0, FIRST)
        half_wait(0)

        for at in range(half):
            head = core * half + at
            mine, theirs = [[ref[kind, head].astype(F32) for kind in range(2)] for ref in (own, pair)]
            low, high = [
                [jnp.where(is_low == first, mine[kind], theirs[kind]) for kind in range(2)] for first in (True, False)
            ]
            mixed[0, at] = (jnp.exp(total_of(chip * 2 + 1, head)) * low[0] + high[0]).astype(BF16)
            mixed[1, at] = (low[1] + jnp.exp(total_of(chip * 2, head)) * high[1]).astype(BF16)

        for step in (2, 0, 1):
            mixed_move(step).start()

        intra(FIRST, SECOND)
        half_wait(1)
        for step in range(3):
            mixed_move(step).wait_recv()

        for at in range(half):
            head = core * half + at
            sum_in = jnp.zeros((width, width), F32)
            sum_later = jnp.zeros((width, width), F32)
            for step in range(3):
                peer = others[step]
                goes_up = peer > chip
                first = jnp.where(goes_up, chip, peer) * 2 + 1
                stop = jnp.where(goes_up, peer, chip) * 2
                gap = jnp.zeros((1, width), F32)
                for which in range(shard_count):
                    gap = gap + jnp.where((which > first) & (which < stop), total_of(which, head), 0.0)
                term = jnp.exp(gap) * mixed_in[step, at].astype(F32)
                sum_in = sum_in + jnp.where(goes_up, 0.0, term)
                sum_later = sum_later + jnp.where(goes_up, term, 0.0)
            prefix[0, at] = sum_in.astype(BF16)
            prefix[1, at] = sum_later.astype(BF16)

        prefix_move.start()
        for at in range(half):
            spread(prefix, at, core * half + at)
        pl.semaphore_wait(ready, 3)

        def pair_move(head):
            return move(grads.at[head, 0], grads.at[head, 1], pair_send, pair_recv.at[head], partner)

        def near_move(head):
            near = chip_x + lax.rem(head, 2) * (chip_y - chip_x)
            return move(grads.at[head, 0], grads.at[head, 2], near_send, near_recv.at[head], near * 2 + core)

        def out_move(slot):
            head = at_order(half - 2 + slot)
            near = chip_x + lax.rem(head, 2) * (chip_y - chip_x)
            return pltpu.make_async_remote_copy(
                src_ref=grads.at[head, 0], dst_ref=detour.at[slot], send_sem=near_send, recv_sem=detour_recv.at[slot],
                device_id={"context": near * 2 + core, "tensor": inward}, device_id_type=pl.DeviceIdType.MESH,
            )

        def back_move(slot):
            head = at_order(half - 2 + slot)
            return pltpu.make_async_remote_copy(
                src_ref=detour.at[slot], dst_ref=grads.at[head, 2], send_sem=detour_send, recv_sem=near_recv.at[head],
                device_id={"tensor": outward}, device_id_type=pl.DeviceIdType.MESH,
            )

        def hand_back(slot):
            whole(detour.at[slot], detour_recv.at[slot]).wait()
            back_move(slot).start()

        def relay_move(head):
            return move(grads.at[head, 2], grads.at[head, 3], relay_send, relay_recv.at[head], partner)

        def hop_move(head):
            target = chip_y + lax.rem(head, 2) * (chip_x - chip_y)
            return move(hop.at[head], hop_in.at[head], hop_send, hop_recv.at[head], target * 2 + core)

        live = lax.broadcasted_iota(jnp.int32, (tokens, width), 0) < len_ref[0]

        def inter(first, stop):
            @pl.loop(first, stop)
            def _(index):
                head = at_order(index)
                cols = cols_of(head)
                c = wide[head]
                until = jnp.exp(wide[head, tokens - 1 :, :] - c)
                k, v, g = qkv[1, :, cols], qkv[2, :, cols], g_ref[:, cols]
                dq = sums[0, :, cols] + scale * jnp.exp(c) * contract(g, incoming[head], LANES)
                dk = sums[1, :, cols] + until * contract(v, later[head], LANES)
                dv = sums[2, :, cols] + until * contract(k, later[head], PLAIN)
                for part, value in enumerate((dq, dk, dv)):
                    grads[head, 0, :, part * width : (part + 1) * width] = jnp.where(live, value, 0.0).astype(BF16)
                around = is_end & (index >= half - 2) & (index < half)

                @pl.when(around)
                def _():
                    out_move(index - (half - 2)).start()

                @pl.when(jnp.logical_not(around))
                def _():
                    near_move(head).start()

                pair_move(head).start()

        inter(0, half)
        intra(SECOND, heads)
        prefix_move.wait_recv()
        for at in range(half):
            spread(prefix_in, at, (1 - core) * half + at)
        inter(half, heads)

        whole(rows_ref.at[:, :, 0], local_sem).wait()
        whole(rows_ref.at[:, :, 1], mate_recv).wait()
        whole(rows_ref.at[:, :, pl.ds(2, 2)], row_recv).wait()

        def product(head, which):
            lhs = rows_ref[lax.rem(head, 2), which].reshape(4 * tokens, strip)
            return contract(lhs, grads[head].reshape(4 * tokens, 3 * width), ROWS)

        def relay(index):
            head = at_order(index)
            near_move(head).wait_recv()
            relay_move(head).start()

        for index in range(half - 2):
            relay(index)

        @pl.when(jnp.logical_not(is_end))
        def _():
            for index in (half - 2, half - 1):
                relay(index)

        @pl.when(is_inner)
        def _():
            pl.semaphore_wait(opened, 1)
            for slot in range(2):
                hand_back(slot)

        @pl.loop(0, half // 2)
        def _(group):
            for index in range(2):
                relay(half + 2 * group + index)

            @pl.when(is_end & (group == half // 2 - 1))
            def _():
                for index in (half - 2, half - 1):
                    relay(index)

            def head_at(index):
                return 2 * group + lax.rem(index, 2) + (index // 2) * half

            @pl.loop(0, 4)
            def _(index):
                head = head_at(index)
                pair_move(head).wait_recv()
                relay_move(head).wait_recv()
                hop[head] = product(head, 1).astype(BF16)
                hop_move(head).start()

            @pl.loop(0, 4)
            def _(index):
                head = head_at(index)
                value = product(head, 0)
                for part in range(3):
                    out_ref[part, :, cols_of(head)] = value[:, part * width : (part + 1) * width]

        settle()

        @pl.when(is_inner)
        def _():
            whole(detour, detour_send).wait()

        whole(grads.at[:, 0], near_send).wait()
        whole(grads.at[:, 0], pair_send).wait()
        whole(grads.at[:, 0], relay_send).wait()

        @pl.loop(0, heads)
        def _(index):
            head = 2 * (index // 4) + lax.rem(index, 2) + (lax.rem(index, 4) // 2) * half
            hop_move(head).wait_recv()
            for part in range(3):
                out_ref[part, :, cols_of(head)] += hop_in[head, :, part * width : (part + 1) * width].astype(F32)

        whole(hop, hop_send).wait()

    pl.run_scoped(
        finish_all,
        pltpu.VMEM((heads, 4, tokens, 3 * width), BF16),
        pltpu.VMEM((heads, strip, 3 * width), BF16),
        pltpu.VMEM((heads, strip, 3 * width), BF16),
    )


def fused(scale, lengths, activations, decay, out_grad, weight, shard_count, size):
    tokens, depth = activations.shape
    columns = out_grad.shape[1]
    heads = decay.shape[0]
    width = columns // heads
    half = heads // 2
    strip = size * depth // shard_count
    dma = pltpu.SemaphoreType.DMA
    away = pl.BlockSpec(memory_space=pltpu.HBM)
    return pl.pallas_call(
        functools.partial(fused_kernel, scale),
        in_specs=[pl.BlockSpec(memory_space=pltpu.SMEM)] + [away] * 4,
        out_specs=pl.BlockSpec(memory_space=pltpu.VMEM),
        out_shape=jax.ShapeDtypeStruct((3, strip, columns), F32),
        scratch_shapes=[
            pltpu.VMEM((size, tokens, depth), BF16),
            pltpu.VMEM((heads, tokens), F32),
            pltpu.VMEM((heads, tokens), F32),
            pltpu.VMEM((heads, tokens, width), F32),
            pltpu.VMEM((shard_count, heads, width), F32),
            pltpu.VMEM((heads, width), F32),
            pltpu.VMEM((3, tokens, columns), BF16),
            pltpu.VMEM((tokens, columns), BF16),
            pltpu.VMEM((3, tokens, columns), F32),
            pltpu.VMEM((2, 2, 4, tokens, strip), BF16),
            pltpu.VMEM((2, heads, width, width), F32),
            pltpu.VMEM((2, heads, width, width), BF16),
            pltpu.VMEM((2, heads, width, width), BF16),
            pltpu.VMEM((2, half, width, width), BF16),
            pltpu.VMEM((3, half, width, width), BF16),
            pltpu.VMEM((2, half, width, width), BF16),
            pltpu.VMEM((2, half, width, width), BF16),
            pltpu.VMEM((heads, width, width), BF16),
            pltpu.VMEM((heads, width, width), BF16),
            pltpu.VMEM((2, tokens, 3 * width), BF16),
            dma((3,)),
            dma((size,)),
            dma((2, size)),
            dma((size, PIECES)),
            dma,
            dma,
            dma,
            dma,
            dma,
            dma,
            dma,
            dma((2,)),
            dma((2,)),
            dma((3,)),
            dma((3,)),
            dma((2,)),
        ] + [dma, dma((heads,))] * 4 + [dma((2,)), dma, pltpu.SemaphoreType.REGULAR, pltpu.SemaphoreType.REGULAR],
        compiler_params=pltpu.CompilerParams(collective_id=1, has_side_effects=True, vmem_limit_bytes=GRANT << 20),
        name="fused",
    )(lengths, *(pltpu.with_memory_space_constraint(value, pltpu.HBM) for value in (activations, decay, out_grad, weight)))


FIRST, SECOND = 1, 5
GRANT = 46
UNROLL = 4


def pick(value, bit, mine, me):
    at = (me >> (bit + 1)) & 1
    return lax.dynamic_index_in_dim(value, at if mine else 1 - at, value.ndim - 3 - bit, keepdims=True)


def scatter_sum(lhs, rhs, bits, me, size):
    def times(block):
        flat = block.reshape((-1,) + block.shape[-2:])
        if flat.shape[0] == 1:
            result = contract(flat[0], rhs, ROWS)
        else:
            result = contract(flat, rhs, ((1,), (0,)))
        return result.reshape(block.shape[:-2] + (block.shape[-1], rhs.shape[1]))

    received = []
    keep = lhs
    for bit in bits:
        send = times(pick(keep, bit, False, me))
        for value in received:
            send = send + pick(value, bit, False, me).astype(F32)
        keep = pick(keep, bit, True, me)
        received = [pick(value, bit, True, me) for value in received]
        received.append(swap(send.astype(BF16), size, 2 << bit))
    total = times(keep)
    for value in received:
        total = total + value.astype(F32)
    return total.reshape(lhs.shape[-1], rhs.shape[1])


def is_square(shard_count, size):
    chips = shard_count // 2
    return chips == size and chips.bit_length() - 1 == 2


def shards(activations, qkv_weight, log_decay, lengths, out_grad):
    size = lax.axis_size("context")
    me = lax.axis_index("context")
    core = me & 1
    chip = me >> 1
    chips = size // 2
    tokens = activations.shape[0]
    heads = log_decay.shape[1]
    columns = out_grad.shape[1]
    width = columns // heads
    half = heads // 2
    scale = width ** -0.5

    if is_square(size, lax.axis_size("tensor")):
        return fused(
            scale, lengths, activations, log_decay.T, out_grad, qkv_weight.transpose(1, 0, 2), size, lax.axis_size("tensor")
        ).transpose(1, 0, 2)

    token_at = jnp.arange(tokens, dtype=jnp.int32)
    live = token_at < lengths[0]
    run_sum = jnp.cumsum(log_decay * live.astype(F32)[:, None], axis=0)
    run_wide = jnp.repeat(run_sum, width, axis=1)
    run_rows = run_sum.T
    own_total = run_sum[-1].astype(BF16).astype(F32)
    total_block = jnp.broadcast_to(jnp.pad(own_total, (0, 128 - heads))[None], (8, 128))
    live_column = live.astype(F32)[:, None]
    every, q, k, v, totals = project(
        activations, qkv_weight.transpose(1, 0, 2), live_column, total_block, size, lax.axis_size("tensor")
    )
    totals = totals[:, 0, :heads]

    rows = qkv_weight.shape[0] // size
    blocks = every.shape[2] // (2 * rows)
    low_rows, high_rows = [
        jnp.stack(
            [every[:, :, (2 * at + which) * rows : (2 * at + which + 1) * rows] for at in range(blocks)], axis=1
        ).reshape(chips, tokens, rows)
        for which in (0, 1)
    ]
    own_rows = jnp.where(core == 0, low_rows, high_rows)
    other_rows = swap(jnp.where(core == 0, high_rows, low_rows), size, 1)
    lhs = jnp.concatenate([own_rows, other_rows], axis=1)

    depth = chips.bit_length() - 1
    orders = (tuple(range(depth)), tuple(reversed(range(depth))))
    lhs = lhs.reshape((2,) * depth + lhs.shape[1:])
    lefts = []
    for order in orders:
        if not depth:
            lefts.append(lhs)
            continue
        moved = swap(pick(lhs, order[0], False, me), size, 2 << order[0])
        lefts.append(jnp.concatenate([pick(lhs, order[0], True, me), moved], axis=-2))

    head_spec = pl.BlockSpec((tokens, width), lambda h: (0, h))
    square_spec = pl.BlockSpec((1, width, width), lambda h: (h, 0, 0))
    wide = lambda kind: jax.ShapeDtypeStruct((tokens, columns), kind)
    squares = jax.ShapeDtypeStruct((heads, width, width), BF16)
    state, grad_state = pl.pallas_call(
        functools.partial(states_kernel, scale),
        grid=(heads,),
        in_specs=[head_spec] * 5,
        out_specs=[square_spec] * 2,
        out_shape=[squares] * 2,
        cost_estimate=pl.CostEstimate(flops=4 * tokens * columns * width, bytes_accessed=12 * tokens * columns, transcendentals=0),
        name="states",
    )(q, k, v, out_grad, run_wide)

    both = jnp.stack([state, grad_state])
    other = swap(both, size, 1)
    mine_half = lax.dynamic_slice_in_dim(both, core * half, half, 1).astype(F32)
    other_half = lax.dynamic_slice_in_dim(other, core * half, half, 1).astype(F32)
    pair_totals = lax.dynamic_slice_in_dim(totals, chip * 2, 2, 0)
    pair_half = lax.dynamic_slice_in_dim(pair_totals, core * half, half, 1)
    low, high = [jnp.where(core == which, mine_half, other_half) for which in (0, 1)]
    chip_state = (jnp.exp(pair_half[1])[:, None, None] * low[0] + high[0]).astype(BF16)
    chip_grad = (low[1] + jnp.exp(pair_half[0])[:, None, None] * high[1]).astype(BF16)

    arrivals = [
        swap(jnp.where((chip ^ step) > chip, chip_state, chip_grad), size, 2 * step) for step in range(1, chips)
    ]

    dq, dk, dv = pl.pallas_call(
        functools.partial(intra_kernel, scale),
        grid=(heads,),
        in_specs=[head_spec] * 5 + [pl.BlockSpec((heads, tokens), lambda h: (0, 0))],
        out_specs=[head_spec] * 3,
        out_shape=[wide(F32)] * 3,
        cost_estimate=pl.CostEstimate(
            flops=10 * tokens * tokens * columns, bytes_accessed=24 * tokens * columns, transcendentals=heads * tokens * tokens
        ),
        name="intra",
    )(q, k, v, out_grad, run_wide, run_rows)

    arrivals, dq, dk, dv = lax.optimization_barrier((arrivals, dq, dk, dv))
    upto = jnp.cumsum(totals, axis=0)
    totals_half = lax.dynamic_slice_in_dim(totals, core * half, half, 1)
    upto_half = lax.dynamic_slice_in_dim(upto, core * half, half, 1)
    chip_before = lax.dynamic_index_in_dim(upto_half - totals_half, chip * 2, 0, keepdims=False)
    chip_upto = lax.dynamic_index_in_dim(upto_half, chip * 2 + 1, 0, keepdims=False)
    incoming = jnp.zeros((half, width, width), F32)
    later = jnp.zeros((half, width, width), F32)
    for step in range(1, chips):
        peer = chip ^ step
        goes_up = peer > chip
        arrived = arrivals[step - 1].astype(F32)
        peer_upto = lax.dynamic_index_in_dim(upto_half, peer * 2 + 1, 0, keepdims=False)
        peer_before = lax.dynamic_index_in_dim(upto_half - totals_half, peer * 2, 0, keepdims=False)
        gap = jnp.where(goes_up, peer_before - chip_upto, chip_before - peer_upto)
        term = jnp.exp(gap)[:, None, None] * arrived
        incoming = incoming + jnp.where(goes_up, 0.0, term)
        later = later + jnp.where(goes_up, term, 0.0)
    from_chips = jnp.stack([incoming, later]).astype(BF16)
    other_chips = swap(from_chips, size, 1)
    is_low = core == 0
    from_chips = jnp.concatenate(
        [jnp.where(is_low, from_chips, other_chips), jnp.where(is_low, other_chips, from_chips)], axis=1
    ).astype(F32)
    incoming = jnp.where(
        is_low, from_chips[0], jnp.exp(pair_totals[0])[:, None, None] * from_chips[0] + other[0].astype(F32)
    ).astype(BF16)
    later = jnp.where(
        is_low, jnp.exp(pair_totals[1])[:, None, None] * from_chips[1] + other[1].astype(F32), from_chips[1]
    ).astype(BF16)

    grads = pl.pallas_call(
        functools.partial(inter_kernel, scale),
        grid=(heads,),
        in_specs=[pl.BlockSpec(memory_space=pltpu.SMEM)] + [head_spec] * 4 + [square_spec] * 2 + [head_spec] * 3,
        out_specs=[head_spec] * 3,
        out_shape=[wide(BF16)] * 3,
        cost_estimate=pl.CostEstimate(flops=6 * tokens * columns * width, bytes_accessed=28 * tokens * columns, transcendentals=0),
        name="inter",
    )(lengths, k, v, out_grad, run_wide, incoming, later, dq, dk, dv)

    results = []
    piece = columns // 2
    for part in grads:
        halves = [part[:, :piece], part[:, piece:]]
        if depth:
            moved = [swap(value, size, 2 << order[0]) for value, order in zip(halves, orders)]
            others = swap(jnp.concatenate(moved, axis=1), size, 1)
        partner = swap(part, size, 1)
        pieces = []
        for at, order in enumerate(orders):
            columns_at = slice(at * piece, (at + 1) * piece)
            rhs = [halves[at], partner[:, columns_at]]
            if depth:
                rhs += [moved[at], others[:, columns_at]]
            pieces.append(scatter_sum(lefts[at], jnp.concatenate(rhs, axis=0), order[1:], me, size))
        results.append(jnp.concatenate(pieces, axis=1))
    return jnp.stack(results, axis=1)


def solution(mesh):
    step = jax.shard_map(
        shards,
        mesh=mesh,
        in_specs=(
            P("context", "tensor"),
            P(None, None, "tensor"),
            P("context", "tensor"),
            P("context"),
            P("context", "tensor"),
        ),
        out_specs=P("context", None, "tensor"),
        check_vma=False,
    )
    if is_square(mesh.shape["context"], mesh.shape["tensor"]):
        return step
    return step
```

```python
import functools

import jax
import jax.numpy as jnp
from jax import lax
from jax.experimental import pallas as pl
from jax.experimental.pallas import tpu as pltpu
from jax.sharding import PartitionSpec as P


F32 = jnp.float32
BF16 = jnp.bfloat16


def contract(a, b, dims):
    return lax.dot_general(a, b, (dims, ((), ())), preferred_element_type=F32)


ROWS = ((0,), (0,))
LANES = ((1,), (1,))
PLAIN = ((1,), (0,))


def states_kernel(scale, q_ref, k_ref, v_ref, g_ref, c_ref, state_ref, grad_ref):
    c = c_ref[...]
    total = c[-1:, :]
    weighted_k = (k_ref[...].astype(F32) * jnp.exp(total - c)).astype(BF16)
    state_ref[0] = contract(weighted_k, v_ref[...], ROWS).astype(BF16)
    weighted_q = (q_ref[...].astype(F32) * (scale * jnp.exp(c))).astype(BF16)
    grad_ref[0] = contract(weighted_q, g_ref[...], ROWS).astype(BF16)


def intra_kernel(scale, q_ref, k_ref, v_ref, g_ref, c_ref, ct_ref, dq_ref, dk_ref, dv_ref):
    head = pl.program_id(0)
    q, k, v, g = q_ref[...], k_ref[...], v_ref[...], g_ref[...]
    tokens, width = q.shape
    column = jnp.concatenate([c_ref[...]] * (tokens // width), axis=1)
    gap = column - ct_ref[pl.ds(head, 1), :]
    row_at = lax.broadcasted_iota(jnp.int32, (tokens, tokens), 0)
    col_at = lax.broadcasted_iota(jnp.int32, (tokens, tokens), 1)
    decay = jnp.exp(jnp.where(row_at >= col_at, gap, -jnp.inf))
    prob = (contract(q, k, LANES) * scale * decay).astype(BF16)
    score = (contract(g, v, LANES) * decay).astype(BF16)
    dq_ref[...] = scale * contract(score, k, PLAIN)
    dk_ref[...] = scale * contract(score, q, ROWS)
    dv_ref[...] = contract(prob, g, ROWS)


def inter_kernel(scale, len_ref, k_ref, v_ref, g_ref, c_ref, in_ref, later_ref, dq_ref, dk_ref, dv_ref,
                 oq_ref, ok_ref, ov_ref):
    c = c_ref[...]
    live = lax.broadcasted_iota(jnp.int32, c.shape, 0) < len_ref[0]
    until = jnp.exp(c[-1:, :] - c)
    dq = dq_ref[...] + scale * jnp.exp(c) * contract(g_ref[...], in_ref[0], LANES)
    dk = dk_ref[...] + until * contract(v_ref[...], later_ref[0], LANES)
    dv = dv_ref[...] + until * contract(k_ref[...], later_ref[0], PLAIN)
    oq_ref[...] = jnp.where(live, dq, 0.0).astype(BF16)
    ok_ref[...] = jnp.where(live, dk, 0.0).astype(BF16)
    ov_ref[...] = jnp.where(live, dv, 0.0).astype(BF16)


def swap(value, size, distance):
    return lax.ppermute(value, "context", [(i, i ^ distance) for i in range(size)])


PIECES = 4
TILE = 512


def project_kernel(act_ref, live_ref, total_ref, weight_ref, every_ref, q_ref, k_ref, v_ref, totals_ref,
                   weights, sums, own_sem, weight_sem, send_sem, recv_sem, total_send, total_recv):
    size, me = lax.axis_size("tensor"), lax.axis_index("tensor")
    shard_count, shard = lax.axis_size("context"), lax.axis_index("context")
    depth = act_ref.shape[1]
    piece = act_ref.shape[0] // PIECES
    columns = q_ref.shape[1]
    tiles = columns // TILE

    def load(owner, part):
        rows = pl.ds(pl.multiple_of(owner * depth, depth), depth)
        return pltpu.make_async_copy(weight_ref.at[part, rows], weights.at[owner, part], weight_sem.at[owner, part])

    for at in range(size):
        owner = lax.rem(me + at, size)
        for part in range(3):
            load(owner, part).start()

    barrier = pltpu.get_barrier_semaphore()
    for target in (me - 1, me + 1):
        @pl.when((target >= 0) & (target < size))
        def _():
            pl.semaphore_signal(barrier, inc=1, device_id={"tensor": target}, device_id_type=pl.DeviceIdType.MESH)

    @pl.loop(1, shard_count)
    def _(step):
        peer = lax.rem(shard + step, shard_count)
        pl.semaphore_signal(barrier, inc=1, device_id={"context": peer}, device_id_type=pl.DeviceIdType.MESH)

    neighbours = jnp.where(me > 0, 1, 0) + jnp.where(me < size - 1, 1, 0)
    pl.semaphore_wait(barrier, neighbours + shard_count - 1)

    def rows_of(at):
        return pl.ds(pl.multiple_of(at * piece, piece), piece)

    def send(source, owner, at, side):
        return pltpu.make_async_remote_copy(
            src_ref=source,
            dst_ref=every_ref.at[owner, rows_of(at)],
            send_sem=send_sem.at[side, owner, at],
            recv_sem=recv_sem.at[owner, at],
            device_id={"tensor": me + 1 - 2 * side},
            device_id_type=pl.DeviceIdType.MESH,
        )

    def has_target(side):
        target = me + 1 - 2 * side
        return (target >= 0) & (target < size)

    def send_total(step):
        peer = lax.rem(shard + step, shard_count)
        return pltpu.make_async_remote_copy(
            src_ref=total_ref,
            dst_ref=totals_ref.at[shard],
            send_sem=total_send.at[peer],
            recv_sem=total_recv.at[shard],
            device_id={"context": peer},
            device_id_type=pl.DeviceIdType.MESH,
        )

    for at in range(PIECES):
        for side in range(2):
            @pl.when(has_target(side))
            def _():
                send(act_ref.at[rows_of(at)], me, at, side).start()

    @pl.loop(1, shard_count)
    def _(step):
        send_total(step).start()

    own = pltpu.make_async_copy(act_ref, every_ref.at[me], own_sem)
    own.start()
    totals_ref[shard] = total_ref[...]

    for part in range(3):
        load(me, part).wait()

    @pl.loop(0, 3 * tiles)
    def _(tile):
        part = tile // tiles
        cols = pl.ds(pl.multiple_of(lax.rem(tile, tiles) * TILE, TILE), TILE)
        sums[part, :, cols] = jnp.dot(act_ref[...], weights[me, part, :, cols], preferred_element_type=F32)

    own.wait()
    for distance in range(1, size):
        for side in range(2):
            owner = me + (2 * side - 1) * distance

            @pl.when((owner >= 0) & (owner < size))
            def _():
                for part in range(3):
                    load(owner, part).wait()

        @pl.loop(0, PIECES)
        def _(at):
            for side in range(2):
                owner = me + (2 * side - 1) * distance

                @pl.when((owner >= 0) & (owner < size))
                def _():
                    pltpu.make_async_copy(
                        every_ref.at[owner, rows_of(at)], every_ref.at[owner, rows_of(at)], recv_sem.at[owner, at]
                    ).wait()

                    @pl.when(has_target(side))
                    def _():
                        send(every_ref.at[owner, rows_of(at)], owner, at, side).start()

            @pl.loop(0, 2)
            def _(side):
                owner = me + (2 * side - 1) * distance

                @pl.when((owner >= 0) & (owner < size))
                def _():
                    @pl.loop(0, 3 * tiles)
                    def _(tile):
                        part = tile // tiles
                        cols = pl.ds(pl.multiple_of(lax.rem(tile, tiles) * TILE, TILE), TILE)
                        sums[part, rows_of(at), cols] += jnp.dot(
                            every_ref[owner, rows_of(at), :], weights[owner, part, :, cols], preferred_element_type=F32
                        )

    live = live_ref[...]
    for part, ref in enumerate((q_ref, k_ref, v_ref)):
        @pl.loop(0, tiles)
        def _(tile):
            cols = pl.ds(pl.multiple_of(tile * TILE, TILE), TILE)
            ref[:, cols] = (sums[part, :, cols] * live).astype(BF16)

    for side in range(2):
        @pl.when(has_target(side))
        def _():
            for distance in range(size):
                owner = me + (2 * side - 1) * distance

                @pl.when((owner >= 0) & (owner < size))
                def _():
                    for at in range(PIECES):
                        send(every_ref.at[owner, rows_of(at)], owner, at, side).wait_send()

    @pl.loop(1, shard_count)
    def _(step):
        peer = lax.rem(shard + step, shard_count)
        send_total(step).wait_send()
        pltpu.make_async_copy(total_ref, totals_ref.at[peer], total_recv.at[peer]).wait()


def project(activations, weight, live, total, shard_count, size):
    tokens, depth = activations.shape
    columns = weight.shape[2]
    vmem = pl.BlockSpec(memory_space=pltpu.VMEM)
    heads_out = [jax.ShapeDtypeStruct((tokens, columns), BF16)] * 3
    return pl.pallas_call(
        project_kernel,
        in_specs=[vmem] * 3 + [pl.BlockSpec(memory_space=pl.ANY)],
        out_specs=[vmem] * 5,
        out_shape=[jax.ShapeDtypeStruct((size, tokens, depth), BF16)]
        + heads_out
        + [jax.ShapeDtypeStruct((shard_count,) + total.shape, F32)],
        scratch_shapes=[
            pltpu.VMEM((size, 3, depth, columns), BF16),
            pltpu.VMEM((3, tokens, columns), F32),
            pltpu.SemaphoreType.DMA,
            pltpu.SemaphoreType.DMA((size, 3)),
            pltpu.SemaphoreType.DMA((2, size, PIECES)),
            pltpu.SemaphoreType.DMA((size, PIECES)),
            pltpu.SemaphoreType.DMA((shard_count,)),
            pltpu.SemaphoreType.DMA((shard_count,)),
        ],
        compiler_params=pltpu.CompilerParams(collective_id=0, has_side_effects=True, vmem_limit_bytes=48 << 20),
        name="project",
    )(activations, live, total, weight)


def flips(chip):
    bx, by = lax.rem(chip, 2), chip // 2
    return chip + 1 - 2 * bx, chip + 2 - 4 * by, 3 - chip


def fused_kernel(scale, len_ref, act_ref, decay_ref, grad_ref, weight_ref, out_ref,
                 every, decay, run, wide, totals, own_total, qkv, g_ref, sums, rows_ref, acc, own, pair, mixed, mixed_in,
                 prefix, prefix_in, incoming, later, detour,
                 input_sem, weight_sem, send_sem, recv_sem, total_send, total_recv, local_sem, mate_send, mate_recv,
                 row_send, row_recv, own_send, own_recv, mixed_send, mixed_recv, prefix_sem, pair_send, pair_recv,
                 near_send, near_recv, relay_send, relay_recv, hop_send, hop_recv, detour_recv, detour_send, ready, opened):
    size, me = lax.axis_size("tensor"), lax.axis_index("tensor")
    shard_count, shard = lax.axis_size("context"), lax.axis_index("context")
    core, chip = lax.rem(shard, 2), shard // 2
    others = flips(chip)
    chip_x, chip_y, chip_far = others
    partner = chip * 2 + 1 - core
    is_low = core == 0
    tokens, depth = act_ref.shape
    columns = grad_ref.shape[1]
    heads = decay_ref.shape[0]
    width = columns // heads
    half = heads // 2
    piece = tokens // PIECES
    tiles = columns // TILE
    strip = rows_ref.shape[-1]
    block = tokens // 2
    last = jnp.maximum(me, size - 1 - me)
    is_end = (me == 0) | (me == size - 1)
    inward = jnp.where(me == 0, 1, size - 2)
    is_inner = (me == 1) | (me == size - 2)
    outward = jnp.where(me == 1, 0, size - 1)

    def move(source, target, send_at, recv_at, peer):
        return pltpu.make_async_remote_copy(
            src_ref=source, dst_ref=target, send_sem=send_at, recv_sem=recv_at,
            device_id={"context": peer}, device_id_type=pl.DeviceIdType.MESH,
        )

    def whole(view, sem):
        return pltpu.make_async_copy(view, view, sem)

    def rows_of(at):
        return pl.ds(pl.multiple_of(at * piece, piece), piece)

    def cols_of(head):
        return pl.ds(pl.multiple_of(head * width, width), width)

    def strip_of(which):
        return pl.ds(pl.multiple_of(which * strip, strip), strip)

    def at_order(index):
        return lax.rem(core * half + index, heads)

    def send(source, owner, at, side):
        return pltpu.make_async_remote_copy(
            src_ref=source,
            dst_ref=every.at[owner, rows_of(at)],
            send_sem=send_sem.at[side, owner],
            recv_sem=recv_sem.at[owner, at],
            device_id={"tensor": me + 1 - 2 * side},
            device_id_type=pl.DeviceIdType.MESH,
        )

    def has_target(side):
        target = me + 1 - 2 * side
        return (target >= 0) & (target < size)

    def send_total(step):
        peer = lax.rem(shard + step, shard_count)
        return move(own_total, totals.at[shard], total_send, total_recv, peer)

    def keep(source, at, order, which):
        return pltpu.make_async_copy(
            source.at[rows_of(at), strip_of(core)], rows_ref.at[order, which, 0, rows_of(at)], local_sem
        )

    def mate(source, at, order, which):
        return move(
            source.at[rows_of(at), strip_of(1 - core)], rows_ref.at[order, which, 1, rows_of(at)],
            mate_send, mate_recv, partner,
        )

    def across(source, at, order, which, other):
        target = core + other - 2 * core * other
        return move(
            source.at[rows_of(at), strip_of(target)], rows_ref.at[order, which, 2 + other, rows_of(at)],
            row_send, row_recv, others[order] * 2 + target,
        )

    def deliver(source, owner, at):
        for order in range(2):
            near, far = others[order], others[1 - order]

            @pl.when((owner == near) | (owner == chip_far))
            def _():
                which = jnp.where(owner == near, 0, 1)
                for other in range(2):
                    across(source, at, order, which, other).start()

            @pl.when((owner == chip) | (owner == far))
            def _():
                which = jnp.where(owner == chip, 0, 1)
                keep(source, at, order, which).start()
                mate(source, at, order, which).start()

    act_copy = pltpu.make_async_copy(act_ref, every.at[me], input_sem.at[0])
    decay_copy = pltpu.make_async_copy(decay_ref, decay, input_sem.at[1])
    grad_copy = pltpu.make_async_copy(grad_ref, g_ref, input_sem.at[2])

    barrier = pltpu.get_barrier_semaphore()
    for target in (me - 1, me + 1):
        @pl.when((target >= 0) & (target < size))
        def _():
            pl.semaphore_signal(barrier, inc=1, device_id={"tensor": target}, device_id_type=pl.DeviceIdType.MESH)

    @pl.loop(1, shard_count)
    def _(step):
        peer = lax.rem(shard + step, shard_count)
        pl.semaphore_signal(barrier, inc=1, device_id={"context": peer}, device_id_type=pl.DeviceIdType.MESH)

    @pl.when(is_inner)
    def _():
        for near in (chip_x, chip_y):
            pl.semaphore_signal(
                barrier, inc=1, device_id={"context": near * 2 + core, "tensor": outward}, device_id_type=pl.DeviceIdType.MESH
            )

    act_copy.start()
    decay_copy.start()
    neighbours = jnp.where(me > 0, 1, 0) + jnp.where(me < size - 1, 1, 0) + jnp.where(is_end, 2, 0)
    pl.semaphore_wait(barrier, neighbours + shard_count - 1)

    for at in range(PIECES):
        for side in range(2):
            @pl.when(has_target(side))
            def _():
                send(act_ref.at[rows_of(at)], me, at, side).start()

    @pl.loop(0, PIECES)
    def _(at):
        deliver(act_ref, me, at)

    def running_sums():
        token_at = lax.broadcasted_iota(jnp.int32, (heads, tokens), 1)
        masked = jnp.where(token_at < len_ref[0], decay[...], 0.0)
        row_at = lax.broadcasted_iota(jnp.int32, (tokens, tokens), 0)
        col_at = lax.broadcasted_iota(jnp.int32, (tokens, tokens), 1)
        upto = jnp.where(row_at <= col_at, 1.0, 0.0)
        c = lax.dot_general(
            masked, upto, (PLAIN, ((), ())), precision=lax.Precision.HIGHEST, preferred_element_type=F32
        )
        run[...] = c
        total = c[:, tokens - 1 :].astype(BF16).astype(F32)
        own_total[...] = jnp.broadcast_to(total, own_total.shape)
        totals[shard] = jnp.broadcast_to(total, own_total.shape)
        column = jnp.concatenate([c, jnp.zeros((width - heads, tokens), F32)], axis=0).T
        for head in range(heads):
            wide[head] = jnp.broadcast_to(column[:, head : head + 1], (tokens, width))

    def states(at):
        @pl.loop(0, heads, unroll=UNROLL)
        def _(head):
            cols, rows = cols_of(head), rows_of(at)
            c = wide[head, rows, :]
            total = wide[head, tokens - 1 :, :]
            weighted_k = (qkv[1, rows, cols].astype(F32) * jnp.exp(total - c)).astype(BF16)
            acc[0, head] += contract(weighted_k, qkv[2, rows, cols], ROWS)
            weighted_q = (qkv[0, rows, cols].astype(F32) * (scale * jnp.exp(c))).astype(BF16)
            acc[1, head] += contract(weighted_q, g_ref[rows, cols], ROWS)

    def project_all(weights):
        def load(owner, part):
            rows = pl.ds(pl.multiple_of(owner * depth, depth), depth)
            return pltpu.make_async_copy(weight_ref.at[part, rows], weights.at[owner, part], weight_sem.at[owner])

        def loaded(owner):
            return pltpu.make_async_copy(weights.at[owner], weights.at[owner], weight_sem.at[owner])

        for at in range(size):
            owner = lax.rem(me + at, size)
            for part in range(3):
                load(owner, part).start()
        grad_copy.start()

        decay_copy.wait()
        running_sums()

        @pl.loop(1, shard_count)
        def _(step):
            send_total(step).start()

        acc[...] = jnp.zeros_like(acc)
        act_copy.wait()
        loaded(me).wait()

        def tile_at(tile):
            return tile // tiles, pl.ds(pl.multiple_of(lax.rem(tile, tiles) * TILE, TILE), TILE)

        @pl.loop(0, 3 * tiles)
        def _(tile):
            part, cols = tile_at(tile)
            sums[part, :, cols] = jnp.dot(every[me], weights[me, part, :, cols], preferred_element_type=F32)

        grad_copy.wait()

        for distance in range(1, size):
            for side in range(2):
                owner = me + (2 * side - 1) * distance

                @pl.when((owner >= 0) & (owner < size))
                def _():
                    loaded(owner).wait()

            @pl.loop(0, PIECES)
            def _(at):
                rows = rows_of(at)
                for side in range(2):
                    owner = me + (2 * side - 1) * distance

                    @pl.when((owner >= 0) & (owner < size))
                    def _():
                        pltpu.make_async_copy(
                            every.at[owner, rows], every.at[owner, rows], recv_sem.at[owner, at]
                        ).wait()

                        @pl.when(has_target(side))
                        def _():
                            send(every.at[owner, rows], owner, at, side).start()

                        deliver(every.at[owner], owner, at)

                @pl.loop(0, 2)
                def _(side):
                    owner = me + (2 * side - 1) * distance
                    valid = (owner >= 0) & (owner < size)

                    def product(part, cols):
                        return sums[part, rows, cols] + jnp.dot(
                            every[owner, rows, :], weights[owner, part, :, cols], preferred_element_type=F32
                        )

                    @pl.when(valid & (distance < last))
                    def _():
                        @pl.loop(0, 3 * tiles)
                        def _(tile):
                            part, cols = tile_at(tile)
                            sums[part, rows, cols] = product(part, cols)

                    if distance >= size // 2:
                        @pl.when(valid & (distance == last))
                        def _():
                            token_at = at * piece + lax.broadcasted_iota(jnp.int32, (piece, TILE), 0)
                            live = token_at < len_ref[0]

                            @pl.loop(0, 3 * tiles)
                            def _(tile):
                                part, cols = tile_at(tile)
                                qkv[part, rows, cols] = jnp.where(live, product(part, cols), 0.0).astype(BF16)

                            states(at)

    pl.run_scoped(project_all, pltpu.VMEM((size, 3, depth, columns), BF16))
    own[...] = acc[...].astype(BF16)

    def half_move(index):
        side = index + core - 2 * index * core
        part = pl.ds((1 - side) * half, half)
        return move(own.at[:, part], pair.at[:, part], own_send.at[index], own_recv.at[index], partner)

    def half_wait(index):
        side = index + core - 2 * index * core
        part = pl.ds(side * half, half)
        pltpu.make_async_copy(pair.at[:, part], pair.at[:, part], own_recv.at[index]).wait()

    def mixed_move(step, part):
        kind = jnp.where(others[step] > chip, 0, 1)
        at = pl.ds(part * 2, 2)
        return move(
            mixed.at[kind, at], mixed_in.at[step, at], mixed_send, mixed_recv.at[step, part], others[step] * 2 + core
        )

    prefix_move = move(prefix, prefix_in, prefix_sem.at[0], prefix_sem.at[1], partner)

    def total_of(which, head):
        return totals[which, pl.ds(head, 1), :]

    def intra(first, stop):
        @pl.loop(first, stop)
        def _(index):
            head = at_order(index)
            cols = cols_of(head)
            at = [slice(part * block, (part + 1) * block) for part in range(2)]
            q, k, v = [[qkv[part, rows, cols] for rows in at] for part in range(3)]
            g = [g_ref[rows, cols] for rows in at]
            dq, dk, dv = [None] * 2, [None] * 2, [None] * 2

            def add(held, part, value):
                held[part] = value if held[part] is None else held[part] + value

            for t in range(2):
                column = jnp.concatenate([wide[head, at[t], :]] * (block // width), axis=1)
                for s in range(t + 1):
                    gap = column - run[pl.ds(head, 1), at[s]]
                    if s == t:
                        row_at = lax.broadcasted_iota(jnp.int32, (block, block), 0)
                        col_at = lax.broadcasted_iota(jnp.int32, (block, block), 1)
                        gap = jnp.where(row_at >= col_at, gap, -jnp.inf)
                    decayed = jnp.exp(gap)
                    prob = (contract(q[t], k[s], LANES) * scale * decayed).astype(BF16)
                    score = (contract(g[t], v[s], LANES) * decayed).astype(BF16)
                    add(dq, t, contract(score, k[s], PLAIN))
                    add(dk, s, contract(score, q[t], ROWS))
                    add(dv, s, contract(prob, g[t], ROWS))
            for part in range(2):
                sums[0, at[part], cols] = scale * dq[part]
                sums[1, at[part], cols] = scale * dk[part]
                sums[2, at[part], cols] = dv[part]

    def spread(ref, at, head):
        sum_in, sum_later = ref[0, at].astype(F32), ref[1, at].astype(F32)
        incoming[head] = jnp.where(
            is_low, sum_in, jnp.exp(total_of(chip * 2, head)) * sum_in + pair[0, head].astype(F32)
        ).astype(BF16)
        later[head] = jnp.where(
            is_low, jnp.exp(total_of(chip * 2 + 1, head)) * sum_later + pair[1, head].astype(F32), sum_later
        ).astype(BF16)

    def settle():
        for side in range(2):
            @pl.when(has_target(side))
            def _():
                for distance in range(size):
                    owner = me + (2 * side - 1) * distance

                    @pl.when((owner >= 0) & (owner < size))
                    def _():
                        whole(every.at[owner], send_sem.at[side, owner]).wait()

        whole(totals.at[pl.ds(0, shard_count - 1)], total_send).wait()
        whole(rows_ref.at[:, :, 1], mate_send).wait()
        whole(rows_ref.at[:, :, pl.ds(2, 2)], row_send).wait()

        for index in range(2):
            half_move(index).wait_send()
        whole(mixed_in, mixed_send).wait()
        prefix_move.wait_send()

    def finish_all(grads, hop, hop_in):
        for target in (partner, chip_x * 2 + core, chip_y * 2 + core):
            pl.semaphore_signal(ready, inc=1, device_id={"context": target}, device_id_type=pl.DeviceIdType.MESH)

        @pl.when(is_end)
        def _():
            pl.semaphore_signal(opened, inc=1, device_id={"tensor": inward}, device_id_type=pl.DeviceIdType.MESH)

        for index in range(2):
            half_move(index).start()

        whole(totals.at[pl.ds(0, shard_count - 1)], total_recv).wait()

        intra(0, FIRST)
        half_wait(0)

        for at in range(half):
            head = core * half + at
            mine, theirs = [[ref[kind, head].astype(F32) for kind in range(2)] for ref in (own, pair)]
            low, high = [
                [jnp.where(is_low == first, mine[kind], theirs[kind]) for kind in range(2)] for first in (True, False)
            ]
            mixed[0, at] = (jnp.exp(total_of(chip * 2 + 1, head)) * low[0] + high[0]).astype(BF16)
            mixed[1, at] = (low[1] + jnp.exp(total_of(chip * 2, head)) * high[1]).astype(BF16)

        for part in range(half // 2):
            for step in (2, 0, 1):
                mixed_move(step, part).start()

        def gather_states(part):
            for step in range(3):
                mixed_move(step, part).wait_recv()

            for at in range(2 * part, 2 * part + 2):
                head = core * half + at
                sum_in = jnp.zeros((width, width), F32)
                sum_later = jnp.zeros((width, width), F32)
                for step in range(3):
                    peer = others[step]
                    goes_up = peer > chip
                    first = jnp.where(goes_up, chip, peer) * 2 + 1
                    stop = jnp.where(goes_up, peer, chip) * 2
                    gap = jnp.zeros((1, width), F32)
                    for which in range(shard_count):
                        gap = gap + jnp.where((which > first) & (which < stop), total_of(which, head), 0.0)
                    term = jnp.exp(gap) * mixed_in[step, at].astype(F32)
                    sum_in = sum_in + jnp.where(goes_up, 0.0, term)
                    sum_later = sum_later + jnp.where(goes_up, term, 0.0)
                prefix[0, at] = sum_in.astype(BF16)
                prefix[1, at] = sum_later.astype(BF16)
                spread(prefix, at, head)

        def pair_move(head):
            return move(grads.at[head, 0], grads.at[head, 1], pair_send, pair_recv.at[head], partner)

        def near_move(head):
            near = chip_x + lax.rem(head, 2) * (chip_y - chip_x)
            return move(grads.at[head, 0], grads.at[head, 2], near_send, near_recv.at[head], near * 2 + core)

        def out_move(slot):
            head = at_order(half - 2 + slot)
            near = chip_x + lax.rem(head, 2) * (chip_y - chip_x)
            return pltpu.make_async_remote_copy(
                src_ref=grads.at[head, 0], dst_ref=detour.at[slot], send_sem=near_send, recv_sem=detour_recv.at[slot],
                device_id={"context": near * 2 + core, "tensor": inward}, device_id_type=pl.DeviceIdType.MESH,
            )

        def back_move(slot):
            head = at_order(half - 2 + slot)
            return pltpu.make_async_remote_copy(
                src_ref=detour.at[slot], dst_ref=grads.at[head, 2], send_sem=detour_send, recv_sem=near_recv.at[head],
                device_id={"tensor": outward}, device_id_type=pl.DeviceIdType.MESH,
            )

        def hand_back(slot):
            whole(detour.at[slot], detour_recv.at[slot]).wait()
            back_move(slot).start()

        def relay_move(head):
            return move(grads.at[head, 2], grads.at[head, 3], relay_send, relay_recv.at[head], partner)

        def hop_move(head):
            target = chip_y + lax.rem(head, 2) * (chip_x - chip_y)
            return move(hop.at[head], hop_in.at[head], hop_send, hop_recv.at[head], target * 2 + core)

        live = lax.broadcasted_iota(jnp.int32, (tokens, width), 0) < len_ref[0]

        def inter(first, stop):
            @pl.loop(first, stop)
            def _(index):
                head = at_order(index)
                cols = cols_of(head)
                c = wide[head]
                until = jnp.exp(wide[head, tokens - 1 :, :] - c)
                k, v, g = qkv[1, :, cols], qkv[2, :, cols], g_ref[:, cols]
                dq = sums[0, :, cols] + scale * jnp.exp(c) * contract(g, incoming[head], LANES)
                dk = sums[1, :, cols] + until * contract(v, later[head], LANES)
                dv = sums[2, :, cols] + until * contract(k, later[head], PLAIN)
                for part, value in enumerate((dq, dk, dv)):
                    grads[head, 0, :, part * width : (part + 1) * width] = jnp.where(live, value, 0.0).astype(BF16)
                around = is_end & (index >= half - 2) & (index < half)

                @pl.when(around)
                def _():
                    out_move(index - (half - 2)).start()

                @pl.when(jnp.logical_not(around))
                def _():
                    near_move(head).start()

                pair_move(head).start()

        intra(FIRST, 3)
        half_wait(1)
        for part in range(half // 2):
            gather_states(part)
            if part == 0:
                pl.semaphore_wait(ready, 3)
            inter(2 * part, 2 * part + 2)
            intra(2 * part + 3, 2 * part + 5)
        prefix_move.start()
        intra(half + 3, heads)
        prefix_move.wait_recv()
        for at in range(half):
            spread(prefix_in, at, (1 - core) * half + at)
        inter(half, heads)

        whole(rows_ref.at[:, :, 0], local_sem).wait()
        whole(rows_ref.at[:, :, 1], mate_recv).wait()
        whole(rows_ref.at[:, :, pl.ds(2, 2)], row_recv).wait()

        def product(head, which):
            lhs = rows_ref[lax.rem(head, 2), which].reshape(4 * tokens, strip)
            return contract(lhs, grads[head].reshape(4 * tokens, 3 * width), ROWS)

        def relay(index):
            head = at_order(index)
            near_move(head).wait_recv()
            relay_move(head).start()

        for index in range(half - 2):
            relay(index)

        @pl.when(jnp.logical_not(is_end))
        def _():
            for index in (half - 2, half - 1):
                relay(index)

        @pl.when(is_inner)
        def _():
            pl.semaphore_wait(opened, 1)
            for slot in range(2):
                hand_back(slot)

        @pl.loop(0, half // 2)
        def _(group):
            for index in range(2):
                relay(half + 2 * group + index)

            @pl.when(is_end & (group == half // 2 - 1))
            def _():
                for index in (half - 2, half - 1):
                    relay(index)

            def head_at(index):
                return 2 * group + lax.rem(index, 2) + (index // 2) * half

            @pl.loop(0, 4)
            def _(index):
                head = head_at(index)
                pair_move(head).wait_recv()
                relay_move(head).wait_recv()
                hop[head] = product(head, 1).astype(BF16)
                hop_move(head).start()

            @pl.loop(0, 4)
            def _(index):
                head = head_at(index)
                value = product(head, 0)
                for part in range(3):
                    out_ref[part, :, cols_of(head)] = value[:, part * width : (part + 1) * width]

        settle()

        @pl.when(is_inner)
        def _():
            whole(detour, detour_send).wait()

        whole(grads.at[:, 0], near_send).wait()
        whole(grads.at[:, 0], pair_send).wait()
        whole(grads.at[:, 0], relay_send).wait()

        @pl.loop(0, heads)
        def _(index):
            head = 2 * (index // 4) + lax.rem(index, 2) + (lax.rem(index, 4) // 2) * half
            hop_move(head).wait_recv()
            for part in range(3):
                out_ref[part, :, cols_of(head)] += hop_in[head, :, part * width : (part + 1) * width].astype(F32)

        whole(hop, hop_send).wait()

    pl.run_scoped(
        finish_all,
        pltpu.VMEM((heads, 4, tokens, 3 * width), BF16),
        pltpu.VMEM((heads, strip, 3 * width), BF16),
        pltpu.VMEM((heads, strip, 3 * width), BF16),
    )


def fused(scale, lengths, activations, decay, out_grad, weight, shard_count, size):
    tokens, depth = activations.shape
    columns = out_grad.shape[1]
    heads = decay.shape[0]
    width = columns // heads
    half = heads // 2
    strip = size * depth // shard_count
    dma = pltpu.SemaphoreType.DMA
    away = pl.BlockSpec(memory_space=pltpu.HBM)
    return pl.pallas_call(
        functools.partial(fused_kernel, scale),
        in_specs=[pl.BlockSpec(memory_space=pltpu.SMEM)] + [away] * 4,
        out_specs=pl.BlockSpec(memory_space=pltpu.VMEM),
        out_shape=jax.ShapeDtypeStruct((3, strip, columns), F32),
        scratch_shapes=[
            pltpu.VMEM((size, tokens, depth), BF16),
            pltpu.VMEM((heads, tokens), F32),
            pltpu.VMEM((heads, tokens), F32),
            pltpu.VMEM((heads, tokens, width), F32),
            pltpu.VMEM((shard_count, heads, width), F32),
            pltpu.VMEM((heads, width), F32),
            pltpu.VMEM((3, tokens, columns), BF16),
            pltpu.VMEM((tokens, columns), BF16),
            pltpu.VMEM((3, tokens, columns), F32),
            pltpu.VMEM((2, 2, 4, tokens, strip), BF16),
            pltpu.VMEM((2, heads, width, width), F32),
            pltpu.VMEM((2, heads, width, width), BF16),
            pltpu.VMEM((2, heads, width, width), BF16),
            pltpu.VMEM((2, half, width, width), BF16),
            pltpu.VMEM((3, half, width, width), BF16),
            pltpu.VMEM((2, half, width, width), BF16),
            pltpu.VMEM((2, half, width, width), BF16),
            pltpu.VMEM((heads, width, width), BF16),
            pltpu.VMEM((heads, width, width), BF16),
            pltpu.VMEM((2, tokens, 3 * width), BF16),
            dma((3,)),
            dma((size,)),
            dma((2, size)),
            dma((size, PIECES)),
            dma,
            dma,
            dma,
            dma,
            dma,
            dma,
            dma,
            dma((2,)),
            dma((2,)),
            dma,
            dma((3, half // 2)),
            dma((2,)),
        ] + [dma, dma((heads,))] * 4 + [dma((2,)), dma, pltpu.SemaphoreType.REGULAR, pltpu.SemaphoreType.REGULAR],
        compiler_params=pltpu.CompilerParams(collective_id=1, has_side_effects=True, vmem_limit_bytes=GRANT << 20),
        name="fused",
    )(lengths, *(pltpu.with_memory_space_constraint(value, pltpu.HBM) for value in (activations, decay, out_grad, weight)))


FIRST = 1
GRANT = 46
UNROLL = 4


def pick(value, bit, mine, me):
    at = (me >> (bit + 1)) & 1
    return lax.dynamic_index_in_dim(value, at if mine else 1 - at, value.ndim - 3 - bit, keepdims=True)


def scatter_sum(lhs, rhs, bits, me, size):
    def times(block):
        flat = block.reshape((-1,) + block.shape[-2:])
        if flat.shape[0] == 1:
            result = contract(flat[0], rhs, ROWS)
        else:
            result = contract(flat, rhs, ((1,), (0,)))
        return result.reshape(block.shape[:-2] + (block.shape[-1], rhs.shape[1]))

    received = []
    keep = lhs
    for bit in bits:
        send = times(pick(keep, bit, False, me))
        for value in received:
            send = send + pick(value, bit, False, me).astype(F32)
        keep = pick(keep, bit, True, me)
        received = [pick(value, bit, True, me) for value in received]
        received.append(swap(send.astype(BF16), size, 2 << bit))
    total = times(keep)
    for value in received:
        total = total + value.astype(F32)
    return total.reshape(lhs.shape[-1], rhs.shape[1])


def is_square(shard_count, size):
    chips = shard_count // 2
    return chips == size and chips.bit_length() - 1 == 2


def shards(activations, qkv_weight, log_decay, lengths, out_grad):
    size = lax.axis_size("context")
    me = lax.axis_index("context")
    core = me & 1
    chip = me >> 1
    chips = size // 2
    tokens = activations.shape[0]
    heads = log_decay.shape[1]
    columns = out_grad.shape[1]
    width = columns // heads
    half = heads // 2
    scale = width ** -0.5

    if is_square(size, lax.axis_size("tensor")):
        return fused(
            scale, lengths, activations, log_decay.T, out_grad, qkv_weight.transpose(1, 0, 2), size, lax.axis_size("tensor")
        ).transpose(1, 0, 2)

    token_at = jnp.arange(tokens, dtype=jnp.int32)
    live = token_at < lengths[0]
    run_sum = jnp.cumsum(log_decay * live.astype(F32)[:, None], axis=0)
    run_wide = jnp.repeat(run_sum, width, axis=1)
    run_rows = run_sum.T
    own_total = run_sum[-1].astype(BF16).astype(F32)
    total_block = jnp.broadcast_to(jnp.pad(own_total, (0, 128 - heads))[None], (8, 128))
    live_column = live.astype(F32)[:, None]
    every, q, k, v, totals = project(
        activations, qkv_weight.transpose(1, 0, 2), live_column, total_block, size, lax.axis_size("tensor")
    )
    totals = totals[:, 0, :heads]

    rows = qkv_weight.shape[0] // size
    blocks = every.shape[2] // (2 * rows)
    low_rows, high_rows = [
        jnp.stack(
            [every[:, :, (2 * at + which) * rows : (2 * at + which + 1) * rows] for at in range(blocks)], axis=1
        ).reshape(chips, tokens, rows)
        for which in (0, 1)
    ]
    own_rows = jnp.where(core == 0, low_rows, high_rows)
    other_rows = swap(jnp.where(core == 0, high_rows, low_rows), size, 1)
    lhs = jnp.concatenate([own_rows, other_rows], axis=1)

    depth = chips.bit_length() - 1
    orders = (tuple(range(depth)), tuple(reversed(range(depth))))
    lhs = lhs.reshape((2,) * depth + lhs.shape[1:])
    lefts = []
    for order in orders:
        if not depth:
            lefts.append(lhs)
            continue
        moved = swap(pick(lhs, order[0], False, me), size, 2 << order[0])
        lefts.append(jnp.concatenate([pick(lhs, order[0], True, me), moved], axis=-2))

    head_spec = pl.BlockSpec((tokens, width), lambda h: (0, h))
    square_spec = pl.BlockSpec((1, width, width), lambda h: (h, 0, 0))
    wide = lambda kind: jax.ShapeDtypeStruct((tokens, columns), kind)
    squares = jax.ShapeDtypeStruct((heads, width, width), BF16)
    state, grad_state = pl.pallas_call(
        functools.partial(states_kernel, scale),
        grid=(heads,),
        in_specs=[head_spec] * 5,
        out_specs=[square_spec] * 2,
        out_shape=[squares] * 2,
        cost_estimate=pl.CostEstimate(flops=4 * tokens * columns * width, bytes_accessed=12 * tokens * columns, transcendentals=0),
        name="states",
    )(q, k, v, out_grad, run_wide)

    both = jnp.stack([state, grad_state])
    other = swap(both, size, 1)
    mine_half = lax.dynamic_slice_in_dim(both, core * half, half, 1).astype(F32)
    other_half = lax.dynamic_slice_in_dim(other, core * half, half, 1).astype(F32)
    pair_totals = lax.dynamic_slice_in_dim(totals, chip * 2, 2, 0)
    pair_half = lax.dynamic_slice_in_dim(pair_totals, core * half, half, 1)
    low, high = [jnp.where(core == which, mine_half, other_half) for which in (0, 1)]
    chip_state = (jnp.exp(pair_half[1])[:, None, None] * low[0] + high[0]).astype(BF16)
    chip_grad = (low[1] + jnp.exp(pair_half[0])[:, None, None] * high[1]).astype(BF16)

    arrivals = [
        swap(jnp.where((chip ^ step) > chip, chip_state, chip_grad), size, 2 * step) for step in range(1, chips)
    ]

    dq, dk, dv = pl.pallas_call(
        functools.partial(intra_kernel, scale),
        grid=(heads,),
        in_specs=[head_spec] * 5 + [pl.BlockSpec((heads, tokens), lambda h: (0, 0))],
        out_specs=[head_spec] * 3,
        out_shape=[wide(F32)] * 3,
        cost_estimate=pl.CostEstimate(
            flops=10 * tokens * tokens * columns, bytes_accessed=24 * tokens * columns, transcendentals=heads * tokens * tokens
        ),
        name="intra",
    )(q, k, v, out_grad, run_wide, run_rows)

    arrivals, dq, dk, dv = lax.optimization_barrier((arrivals, dq, dk, dv))
    upto = jnp.cumsum(totals, axis=0)
    totals_half = lax.dynamic_slice_in_dim(totals, core * half, half, 1)
    upto_half = lax.dynamic_slice_in_dim(upto, core * half, half, 1)
    chip_before = lax.dynamic_index_in_dim(upto_half - totals_half, chip * 2, 0, keepdims=False)
    chip_upto = lax.dynamic_index_in_dim(upto_half, chip * 2 + 1, 0, keepdims=False)
    incoming = jnp.zeros((half, width, width), F32)
    later = jnp.zeros((half, width, width), F32)
    for step in range(1, chips):
        peer = chip ^ step
        goes_up = peer > chip
        arrived = arrivals[step - 1].astype(F32)
        peer_upto = lax.dynamic_index_in_dim(upto_half, peer * 2 + 1, 0, keepdims=False)
        peer_before = lax.dynamic_index_in_dim(upto_half - totals_half, peer * 2, 0, keepdims=False)
        gap = jnp.where(goes_up, peer_before - chip_upto, chip_before - peer_upto)
        term = jnp.exp(gap)[:, None, None] * arrived
        incoming = incoming + jnp.where(goes_up, 0.0, term)
        later = later + jnp.where(goes_up, term, 0.0)
    from_chips = jnp.stack([incoming, later]).astype(BF16)
    other_chips = swap(from_chips, size, 1)
    is_low = core == 0
    from_chips = jnp.concatenate(
        [jnp.where(is_low, from_chips, other_chips), jnp.where(is_low, other_chips, from_chips)], axis=1
    ).astype(F32)
    incoming = jnp.where(
        is_low, from_chips[0], jnp.exp(pair_totals[0])[:, None, None] * from_chips[0] + other[0].astype(F32)
    ).astype(BF16)
    later = jnp.where(
        is_low, jnp.exp(pair_totals[1])[:, None, None] * from_chips[1] + other[1].astype(F32), from_chips[1]
    ).astype(BF16)

    grads = pl.pallas_call(
        functools.partial(inter_kernel, scale),
        grid=(heads,),
        in_specs=[pl.BlockSpec(memory_space=pltpu.SMEM)] + [head_spec] * 4 + [square_spec] * 2 + [head_spec] * 3,
        out_specs=[head_spec] * 3,
        out_shape=[wide(BF16)] * 3,
        cost_estimate=pl.CostEstimate(flops=6 * tokens * columns * width, bytes_accessed=28 * tokens * columns, transcendentals=0),
        name="inter",
    )(lengths, k, v, out_grad, run_wide, incoming, later, dq, dk, dv)

    results = []
    piece = columns // 2
    for part in grads:
        halves = [part[:, :piece], part[:, piece:]]
        if depth:
            moved = [swap(value, size, 2 << order[0]) for value, order in zip(halves, orders)]
            others = swap(jnp.concatenate(moved, axis=1), size, 1)
        partner = swap(part, size, 1)
        pieces = []
        for at, order in enumerate(orders):
            columns_at = slice(at * piece, (at + 1) * piece)
            rhs = [halves[at], partner[:, columns_at]]
            if depth:
                rhs += [moved[at], others[:, columns_at]]
            pieces.append(scatter_sum(lefts[at], jnp.concatenate(rhs, axis=0), order[1:], me, size))
        results.append(jnp.concatenate(pieces, axis=1))
    return jnp.stack(results, axis=1)


def solution(mesh):
    step = jax.shard_map(
        shards,
        mesh=mesh,
        in_specs=(
            P("context", "tensor"),
            P(None, None, "tensor"),
            P("context", "tensor"),
            P("context"),
            P("context", "tensor"),
        ),
        out_specs=P("context", None, "tensor"),
        check_vma=False,
    )
    if is_square(mesh.shape["context"], mesh.shape["tensor"]):
        return step
    return step
```

```python
import functools

import jax
import jax.numpy as jnp
from jax import lax
from jax.experimental import pallas as pl
from jax.experimental.pallas import tpu as pltpu
from jax.sharding import PartitionSpec as P


F32 = jnp.float32
BF16 = jnp.bfloat16


def contract(a, b, dims):
    return lax.dot_general(a, b, (dims, ((), ())), preferred_element_type=F32)


ROWS = ((0,), (0,))
LANES = ((1,), (1,))
PLAIN = ((1,), (0,))


def states_kernel(scale, q_ref, k_ref, v_ref, g_ref, c_ref, state_ref, grad_ref):
    c = c_ref[...]
    total = c[-1:, :]
    weighted_k = (k_ref[...].astype(F32) * jnp.exp(total - c)).astype(BF16)
    state_ref[0] = contract(weighted_k, v_ref[...], ROWS).astype(BF16)
    weighted_q = (q_ref[...].astype(F32) * (scale * jnp.exp(c))).astype(BF16)
    grad_ref[0] = contract(weighted_q, g_ref[...], ROWS).astype(BF16)


def intra_kernel(scale, q_ref, k_ref, v_ref, g_ref, c_ref, ct_ref, dq_ref, dk_ref, dv_ref):
    head = pl.program_id(0)
    q, k, v, g = q_ref[...], k_ref[...], v_ref[...], g_ref[...]
    tokens, width = q.shape
    column = jnp.concatenate([c_ref[...]] * (tokens // width), axis=1)
    gap = column - ct_ref[pl.ds(head, 1), :]
    row_at = lax.broadcasted_iota(jnp.int32, (tokens, tokens), 0)
    col_at = lax.broadcasted_iota(jnp.int32, (tokens, tokens), 1)
    decay = jnp.exp(jnp.where(row_at >= col_at, gap, -jnp.inf))
    prob = (contract(q, k, LANES) * scale * decay).astype(BF16)
    score = (contract(g, v, LANES) * decay).astype(BF16)
    dq_ref[...] = scale * contract(score, k, PLAIN)
    dk_ref[...] = scale * contract(score, q, ROWS)
    dv_ref[...] = contract(prob, g, ROWS)


def inter_kernel(scale, len_ref, k_ref, v_ref, g_ref, c_ref, in_ref, later_ref, dq_ref, dk_ref, dv_ref,
                 oq_ref, ok_ref, ov_ref):
    c = c_ref[...]
    live = lax.broadcasted_iota(jnp.int32, c.shape, 0) < len_ref[0]
    until = jnp.exp(c[-1:, :] - c)
    dq = dq_ref[...] + scale * jnp.exp(c) * contract(g_ref[...], in_ref[0], LANES)
    dk = dk_ref[...] + until * contract(v_ref[...], later_ref[0], LANES)
    dv = dv_ref[...] + until * contract(k_ref[...], later_ref[0], PLAIN)
    oq_ref[...] = jnp.where(live, dq, 0.0).astype(BF16)
    ok_ref[...] = jnp.where(live, dk, 0.0).astype(BF16)
    ov_ref[...] = jnp.where(live, dv, 0.0).astype(BF16)


def swap(value, size, distance):
    return lax.ppermute(value, "context", [(i, i ^ distance) for i in range(size)])


PIECES = 4
TILE = 512


def project_kernel(act_ref, live_ref, total_ref, weight_ref, every_ref, q_ref, k_ref, v_ref, totals_ref,
                   weights, sums, own_sem, weight_sem, send_sem, recv_sem, total_send, total_recv):
    size, me = lax.axis_size("tensor"), lax.axis_index("tensor")
    shard_count, shard = lax.axis_size("context"), lax.axis_index("context")
    depth = act_ref.shape[1]
    piece = act_ref.shape[0] // PIECES
    columns = q_ref.shape[1]
    tiles = columns // TILE

    def load(owner, part):
        rows = pl.ds(pl.multiple_of(owner * depth, depth), depth)
        return pltpu.make_async_copy(weight_ref.at[part, rows], weights.at[owner, part], weight_sem.at[owner, part])

    for at in range(size):
        owner = lax.rem(me + at, size)
        for part in range(3):
            load(owner, part).start()

    barrier = pltpu.get_barrier_semaphore()
    for target in (me - 1, me + 1):
        @pl.when((target >= 0) & (target < size))
        def _():
            pl.semaphore_signal(barrier, inc=1, device_id={"tensor": target}, device_id_type=pl.DeviceIdType.MESH)

    @pl.loop(1, shard_count)
    def _(step):
        peer = lax.rem(shard + step, shard_count)
        pl.semaphore_signal(barrier, inc=1, device_id={"context": peer}, device_id_type=pl.DeviceIdType.MESH)

    neighbours = jnp.where(me > 0, 1, 0) + jnp.where(me < size - 1, 1, 0)
    pl.semaphore_wait(barrier, neighbours + shard_count - 1)

    def rows_of(at):
        return pl.ds(pl.multiple_of(at * piece, piece), piece)

    def send(source, owner, at, side):
        return pltpu.make_async_remote_copy(
            src_ref=source,
            dst_ref=every_ref.at[owner, rows_of(at)],
            send_sem=send_sem.at[side, owner, at],
            recv_sem=recv_sem.at[owner, at],
            device_id={"tensor": me + 1 - 2 * side},
            device_id_type=pl.DeviceIdType.MESH,
        )

    def has_target(side):
        target = me + 1 - 2 * side
        return (target >= 0) & (target < size)

    def send_total(step):
        peer = lax.rem(shard + step, shard_count)
        return pltpu.make_async_remote_copy(
            src_ref=total_ref,
            dst_ref=totals_ref.at[shard],
            send_sem=total_send.at[peer],
            recv_sem=total_recv.at[shard],
            device_id={"context": peer},
            device_id_type=pl.DeviceIdType.MESH,
        )

    for at in range(PIECES):
        for side in range(2):
            @pl.when(has_target(side))
            def _():
                send(act_ref.at[rows_of(at)], me, at, side).start()

    @pl.loop(1, shard_count)
    def _(step):
        send_total(step).start()

    own = pltpu.make_async_copy(act_ref, every_ref.at[me], own_sem)
    own.start()
    totals_ref[shard] = total_ref[...]

    for part in range(3):
        load(me, part).wait()

    @pl.loop(0, 3 * tiles)
    def _(tile):
        part = tile // tiles
        cols = pl.ds(pl.multiple_of(lax.rem(tile, tiles) * TILE, TILE), TILE)
        sums[part, :, cols] = jnp.dot(act_ref[...], weights[me, part, :, cols], preferred_element_type=F32)

    own.wait()
    for distance in range(1, size):
        for side in range(2):
            owner = me + (2 * side - 1) * distance

            @pl.when((owner >= 0) & (owner < size))
            def _():
                for part in range(3):
                    load(owner, part).wait()

        @pl.loop(0, PIECES)
        def _(at):
            for side in range(2):
                owner = me + (2 * side - 1) * distance

                @pl.when((owner >= 0) & (owner < size))
                def _():
                    pltpu.make_async_copy(
                        every_ref.at[owner, rows_of(at)], every_ref.at[owner, rows_of(at)], recv_sem.at[owner, at]
                    ).wait()

                    @pl.when(has_target(side))
                    def _():
                        send(every_ref.at[owner, rows_of(at)], owner, at, side).start()

            @pl.loop(0, 2)
            def _(side):
                owner = me + (2 * side - 1) * distance

                @pl.when((owner >= 0) & (owner < size))
                def _():
                    @pl.loop(0, 3 * tiles)
                    def _(tile):
                        part = tile // tiles
                        cols = pl.ds(pl.multiple_of(lax.rem(tile, tiles) * TILE, TILE), TILE)
                        sums[part, rows_of(at), cols] += jnp.dot(
                            every_ref[owner, rows_of(at), :], weights[owner, part, :, cols], preferred_element_type=F32
                        )

    live = live_ref[...]
    for part, ref in enumerate((q_ref, k_ref, v_ref)):
        @pl.loop(0, tiles)
        def _(tile):
            cols = pl.ds(pl.multiple_of(tile * TILE, TILE), TILE)
            ref[:, cols] = (sums[part, :, cols] * live).astype(BF16)

    for side in range(2):
        @pl.when(has_target(side))
        def _():
            for distance in range(size):
                owner = me + (2 * side - 1) * distance

                @pl.when((owner >= 0) & (owner < size))
                def _():
                    for at in range(PIECES):
                        send(every_ref.at[owner, rows_of(at)], owner, at, side).wait_send()

    @pl.loop(1, shard_count)
    def _(step):
        peer = lax.rem(shard + step, shard_count)
        send_total(step).wait_send()
        pltpu.make_async_copy(total_ref, totals_ref.at[peer], total_recv.at[peer]).wait()


def project(activations, weight, live, total, shard_count, size):
    tokens, depth = activations.shape
    columns = weight.shape[2]
    vmem = pl.BlockSpec(memory_space=pltpu.VMEM)
    heads_out = [jax.ShapeDtypeStruct((tokens, columns), BF16)] * 3
    return pl.pallas_call(
        project_kernel,
        in_specs=[vmem] * 3 + [pl.BlockSpec(memory_space=pl.ANY)],
        out_specs=[vmem] * 5,
        out_shape=[jax.ShapeDtypeStruct((size, tokens, depth), BF16)]
        + heads_out
        + [jax.ShapeDtypeStruct((shard_count,) + total.shape, F32)],
        scratch_shapes=[
            pltpu.VMEM((size, 3, depth, columns), BF16),
            pltpu.VMEM((3, tokens, columns), F32),
            pltpu.SemaphoreType.DMA,
            pltpu.SemaphoreType.DMA((size, 3)),
            pltpu.SemaphoreType.DMA((2, size, PIECES)),
            pltpu.SemaphoreType.DMA((size, PIECES)),
            pltpu.SemaphoreType.DMA((shard_count,)),
            pltpu.SemaphoreType.DMA((shard_count,)),
        ],
        compiler_params=pltpu.CompilerParams(collective_id=0, has_side_effects=True, vmem_limit_bytes=48 << 20),
        name="project",
    )(activations, live, total, weight)


def flips(chip):
    bx, by = lax.rem(chip, 2), chip // 2
    return chip + 1 - 2 * bx, chip + 2 - 4 * by, 3 - chip


def fused_kernel(scale, len_ref, act_ref, decay_ref, grad_ref, weight_ref, out_ref,
                 every, decay, run, wide, totals, own_total, qkv, g_ref, sums, rows_ref, acc, own, pair, mixed, mixed_in,
                 prefix, prefix_in, incoming, later,
                 run_out, run_near, wide_near, qkv_near, grad_near, ends_near,
                 input_sem, weight_sem, send_sem, recv_sem, total_send, total_recv, local_sem, mate_send, mate_recv,
                 row_send, row_recv, own_send, own_recv, mixed_send, mixed_recv, prefix_sem, pair_send, pair_recv,
                 near_send, near_recv, relay_send, relay_recv, hop_send, hop_recv, pass_send, run_send, run_recv,
                 copy_send, copy_recv, plain_send, plain_recv, ends_send, ends_recv, ready):
    size, me = lax.axis_size("tensor"), lax.axis_index("tensor")
    shard_count, shard = lax.axis_size("context"), lax.axis_index("context")
    core, chip = lax.rem(shard, 2), shard // 2
    others = flips(chip)
    chip_x, chip_y, chip_far = others
    partner = chip * 2 + 1 - core
    is_low = core == 0
    tokens, depth = act_ref.shape
    columns = grad_ref.shape[1]
    heads = decay_ref.shape[0]
    width = columns // heads
    half = heads // 2
    piece = tokens // PIECES
    tiles = columns // TILE
    strip = rows_ref.shape[-1]
    block = tokens // 2
    last = jnp.maximum(me, size - 1 - me)
    is_end = (me == 0) | (me == size - 1)
    is_inner = (me == 1) | (me == size - 2)
    outward = jnp.where(me == 1, 0, size - 1)
    far_block = jnp.where(me < size // 2, size - 1, 0)

    def shared(order, side):
        return half // 2 + order + half * side

    def move(source, target, send_at, recv_at, peer):
        return pltpu.make_async_remote_copy(
            src_ref=source, dst_ref=target, send_sem=send_at, recv_sem=recv_at,
            device_id={"context": peer}, device_id_type=pl.DeviceIdType.MESH,
        )

    def whole(view, sem):
        return pltpu.make_async_copy(view, view, sem)

    def rows_of(at):
        return pl.ds(pl.multiple_of(at * piece, piece), piece)

    def cols_of(head):
        return pl.ds(pl.multiple_of(head * width, width), width)

    def strip_of(which):
        return pl.ds(pl.multiple_of(which * strip, strip), strip)

    def at_order(index):
        return lax.rem(core * half + index, heads)

    def send(source, owner, at, side):
        return pltpu.make_async_remote_copy(
            src_ref=source,
            dst_ref=every.at[owner, rows_of(at)],
            send_sem=send_sem.at[side, owner],
            recv_sem=recv_sem.at[owner, at],
            device_id={"tensor": me + 1 - 2 * side},
            device_id_type=pl.DeviceIdType.MESH,
        )

    def has_target(side):
        target = me + 1 - 2 * side
        return (target >= 0) & (target < size)

    def send_total(step):
        peer = lax.rem(shard + step, shard_count)
        return move(own_total, totals.at[shard], total_send, total_recv, peer)

    def keep(source, at, order, which):
        return pltpu.make_async_copy(
            source.at[rows_of(at), strip_of(core)], rows_ref.at[order, which, 0, rows_of(at)], local_sem
        )

    def mate(source, at, order, which):
        return move(
            source.at[rows_of(at), strip_of(1 - core)], rows_ref.at[order, which, 1, rows_of(at)],
            mate_send, mate_recv, partner,
        )

    def across(source, at, order, which, other):
        target = core + other - 2 * core * other
        return move(
            source.at[rows_of(at), strip_of(target)], rows_ref.at[order, which, 2 + other, rows_of(at)],
            row_send.at[order, which], row_recv.at[order, which], others[order] * 2 + target,
        )

    def deliver(source, owner, at):
        for order in range(2):
            near, far = others[order], others[1 - order]

            @pl.when(((owner == near) | (owner == chip_far)) & jnp.logical_not(is_end & (owner == far_block)))
            def _():
                which = jnp.where(owner == near, 0, 1)
                for other in range(2):
                    across(source, at, order, which, other).start()

            @pl.when((owner == chip) | (owner == far))
            def _():
                which = jnp.where(owner == chip, 0, 1)
                keep(source, at, order, which).start()
                mate(source, at, order, which).start()

    def rows_wait():
        for order in range(2):
            for which in range(2):
                whole(rows_ref.at[order, which, pl.ds(2, 2)], row_recv.at[order, which]).wait()

    def pass_rows():
        for order in range(2):
            @pl.when((far_block == chip) | (far_block == others[1 - order]))
            def _():
                which = jnp.where(far_block == chip, 0, 1)
                view = rows_ref.at[order, which, pl.ds(2, 2)]
                pltpu.make_async_remote_copy(
                    src_ref=view, dst_ref=view, send_sem=pass_send.at[order], recv_sem=row_recv.at[order, which],
                    device_id={"tensor": outward}, device_id_type=pl.DeviceIdType.MESH,
                ).start()

    def grad_share(order, side):
        return move(
            grad_ref.at[:, cols_of(shared(order, side))], grad_near.at[2 * order + side], copy_send, copy_recv,
            others[order] * 2 + core,
        )

    def run_share(order):
        return move(run_out, run_near.at[order], run_send, run_recv, others[order] * 2 + core)

    def qkv_share(order, side, at):
        return move(
            qkv.at[:, rows_of(at), cols_of(shared(order, side))], qkv_near.at[2 * order + side, :, rows_of(at)],
            plain_send, plain_recv, others[order] * 2 + core,
        )

    def ends_share(order, side):
        for kind, ref in enumerate((incoming, later)):
            move(
                ref.at[shared(order, side)], ends_near.at[kind, 2 * order + side], ends_send, ends_recv,
                others[order] * 2 + core,
            ).start()

    act_copy = pltpu.make_async_copy(act_ref, every.at[me], input_sem.at[0])
    decay_copy = pltpu.make_async_copy(decay_ref, decay, input_sem.at[1])
    grad_copy = pltpu.make_async_copy(grad_ref, g_ref, input_sem.at[2])

    barrier = pltpu.get_barrier_semaphore()
    for target in (me - 1, me + 1):
        @pl.when((target >= 0) & (target < size))
        def _():
            pl.semaphore_signal(barrier, inc=1, device_id={"tensor": target}, device_id_type=pl.DeviceIdType.MESH)

    @pl.loop(1, shard_count)
    def _(step):
        peer = lax.rem(shard + step, shard_count)
        pl.semaphore_signal(barrier, inc=1, device_id={"context": peer}, device_id_type=pl.DeviceIdType.MESH)

    act_copy.start()
    decay_copy.start()
    neighbours = jnp.where(me > 0, 1, 0) + jnp.where(me < size - 1, 1, 0)
    pl.semaphore_wait(barrier, neighbours + shard_count - 1)

    for at in range(PIECES):
        for side in range(2):
            @pl.when(has_target(side))
            def _():
                send(act_ref.at[rows_of(at)], me, at, side).start()

    @pl.loop(0, PIECES)
    def _(at):
        deliver(act_ref, me, at)

    @pl.when(is_end)
    def _():
        for order in range(2):
            for side in range(2):
                grad_share(order, side).start()

    def running_sums():
        token_at = lax.broadcasted_iota(jnp.int32, (heads, tokens), 1)
        masked = jnp.where(token_at < len_ref[0], decay[...], 0.0)
        row_at = lax.broadcasted_iota(jnp.int32, (tokens, tokens), 0)
        col_at = lax.broadcasted_iota(jnp.int32, (tokens, tokens), 1)
        upto = jnp.where(row_at <= col_at, 1.0, 0.0)
        c = lax.dot_general(
            masked, upto, (PLAIN, ((), ())), precision=lax.Precision.HIGHEST, preferred_element_type=F32
        )
        run[...] = c
        run_out[0:heads] = c
        run_out[heads : 2 * heads] = jnp.where(token_at < len_ref[0], 1.0, 0.0)
        total = c[:, tokens - 1 :].astype(BF16).astype(F32)
        own_total[...] = jnp.broadcast_to(total, own_total.shape)
        totals[shard] = jnp.broadcast_to(total, own_total.shape)
        column = jnp.concatenate([c, jnp.zeros((width - heads, tokens), F32)], axis=0).T
        for head in range(heads):
            wide[head] = jnp.broadcast_to(column[:, head : head + 1], (tokens, width))

    def half_move(index):
        side = index + core - 2 * index * core
        part = pl.ds((1 - side) * half, half)
        return move(own.at[:, part], pair.at[:, part], own_send.at[index], own_recv.at[index], partner)

    def states(at, first):
        @pl.loop(0, half, unroll=UNROLL)
        def _(index):
            head = first + index
            cols, rows = cols_of(head), rows_of(at)
            c = wide[head, rows, :]
            total = wide[head, tokens - 1 :, :]
            weighted_k = (qkv[1, rows, cols].astype(F32) * jnp.exp(total - c)).astype(BF16)
            acc[0, head] += contract(weighted_k, qkv[2, rows, cols], ROWS)
            weighted_q = (qkv[0, rows, cols].astype(F32) * (scale * jnp.exp(c))).astype(BF16)
            acc[1, head] += contract(weighted_q, g_ref[rows, cols], ROWS)

    def project_all(weights):
        def load(owner, part):
            rows = pl.ds(pl.multiple_of(owner * depth, depth), depth)
            return pltpu.make_async_copy(weight_ref.at[part, rows], weights.at[owner, part], weight_sem.at[owner])

        def loaded(owner):
            return pltpu.make_async_copy(weights.at[owner], weights.at[owner], weight_sem.at[owner])

        for at in range(size):
            owner = lax.rem(me + at, size)
            for part in range(3):
                load(owner, part).start()
        grad_copy.start()

        decay_copy.wait()
        running_sums()

        @pl.loop(1, shard_count)
        def _(step):
            send_total(step).start()

        @pl.when(is_end)
        def _():
            for order in range(2):
                run_share(order).start()

        acc[...] = jnp.zeros_like(acc)
        act_copy.wait()
        loaded(me).wait()

        def tile_at(tile):
            return tile // tiles, pl.ds(pl.multiple_of(lax.rem(tile, tiles) * TILE, TILE), TILE)

        @pl.loop(0, 3 * tiles)
        def _(tile):
            part, cols = tile_at(tile)
            sums[part, :, cols] = jnp.dot(every[me], weights[me, part, :, cols], preferred_element_type=F32)

        grad_copy.wait()

        for distance in range(1, size):
            for side in range(2):
                owner = me + (2 * side - 1) * distance

                @pl.when((owner >= 0) & (owner < size))
                def _():
                    loaded(owner).wait()

            @pl.loop(0, PIECES)
            def _(at):
                rows = rows_of(at)
                for side in range(2):
                    owner = me + (2 * side - 1) * distance

                    @pl.when((owner >= 0) & (owner < size))
                    def _():
                        pltpu.make_async_copy(
                            every.at[owner, rows], every.at[owner, rows], recv_sem.at[owner, at]
                        ).wait()

                        @pl.when(has_target(side))
                        def _():
                            send(every.at[owner, rows], owner, at, side).start()

                        deliver(every.at[owner], owner, at)

                @pl.loop(0, 2)
                def _(side):
                    owner = me + (2 * side - 1) * distance
                    valid = (owner >= 0) & (owner < size)

                    def product(part, cols):
                        return sums[part, rows, cols] + jnp.dot(
                            every[owner, rows, :], weights[owner, part, :, cols], preferred_element_type=F32
                        )

                    @pl.when(valid & (distance < last))
                    def _():
                        @pl.loop(0, 3 * tiles)
                        def _(tile):
                            part, cols = tile_at(tile)
                            sums[part, rows, cols] = product(part, cols)

                    if distance >= size // 2:
                        @pl.when(valid & (distance == last))
                        def _():
                            token_at = at * piece + lax.broadcasted_iota(jnp.int32, (piece, TILE), 0)
                            live = token_at < len_ref[0]

                            for index in range(2):
                                first = (1 - core if index == 0 else core) * half

                                @pl.loop(0, 3 * tiles // 2)
                                def _(tile):
                                    part, start = tile // (tiles // 2), lax.rem(tile, tiles // 2) * TILE
                                    cols = pl.ds(pl.multiple_of(first * width + start, width), TILE)
                                    qkv[part, rows, cols] = jnp.where(live, product(part, cols), 0.0).astype(BF16)

                                states(at, first)

                                @pl.when(is_end)
                                def _():
                                    for order in range(2):
                                        qkv_share(order, 1 - core if index == 0 else core, at).start()

                                @pl.when(at == PIECES - 1)
                                def _():
                                    own[:, pl.ds(first, half)] = acc[:, pl.ds(first, half)].astype(BF16)
                                    half_move(index).start()

    pl.run_scoped(project_all, pltpu.VMEM((size, 3, depth, columns), BF16))

    def half_wait(index):
        side = index + core - 2 * index * core
        part = pl.ds(side * half, half)
        pltpu.make_async_copy(pair.at[:, part], pair.at[:, part], own_recv.at[index]).wait()

    def mixed_move(step, part):
        kind = jnp.where(others[step] > chip, 0, 1)
        at = pl.ds(part * 2, 2)
        return move(
            mixed.at[kind, at], mixed_in.at[step, at], mixed_send, mixed_recv.at[step, part], others[step] * 2 + core
        )

    prefix_move = move(prefix, prefix_in, prefix_sem.at[0], prefix_sem.at[1], partner)

    def total_of(which, head):
        return totals[which, pl.ds(head, 1), :]

    def within(q, k, v, g, column_at, row_at_block):
        dq, dk, dv = [None] * 2, [None] * 2, [None] * 2

        def add(held, part, value):
            held[part] = value if held[part] is None else held[part] + value

        for t in range(2):
            column = jnp.concatenate([column_at(t)] * (block // width), axis=1)
            for s in range(t + 1):
                gap = column - row_at_block(s)
                if s == t:
                    row_at = lax.broadcasted_iota(jnp.int32, (block, block), 0)
                    col_at = lax.broadcasted_iota(jnp.int32, (block, block), 1)
                    gap = jnp.where(row_at >= col_at, gap, -jnp.inf)
                decayed = jnp.exp(gap)
                prob = (contract(q[t], k[s], LANES) * scale * decayed).astype(BF16)
                score = (contract(g[t], v[s], LANES) * decayed).astype(BF16)
                add(dq, t, contract(score, k[s], PLAIN))
                add(dk, s, contract(score, q[t], ROWS))
                add(dv, s, contract(prob, g[t], ROWS))
        return [scale * value for value in dq], [scale * value for value in dk], dv

    blocks = [slice(part * block, (part + 1) * block) for part in range(2)]

    def intra(first, stop):
        @pl.loop(first, stop)
        def _(index):
            head = at_order(index)
            cols = cols_of(head)
            q, k, v = [[qkv[part, rows, cols] for rows in blocks] for part in range(3)]
            g = [g_ref[rows, cols] for rows in blocks]
            results = within(
                q, k, v, g, lambda t: wide[head, blocks[t], :], lambda s: run[pl.ds(head, 1), blocks[s]]
            )
            for part, values in enumerate(results):
                for index, value in enumerate(values):
                    sums[part, blocks[index], cols] = value

    def recompute(relay_move, grads):
        whole(run_near, run_recv).wait()
        for order in range(2):
            column = jnp.concatenate([run_near[order], jnp.zeros((width - 2 * heads, tokens), F32)], axis=0).T
            for side in range(2):
                head = shared(order, side)
                wide_near[2 * order + side] = jnp.broadcast_to(column[:, head : head + 1], (tokens, width))
            wide_near[4 + order] = jnp.broadcast_to(column[:, heads : heads + 1], (tokens, width))
        whole(grad_near, copy_recv).wait()
        whole(qkv_near, plain_recv).wait()
        whole(ends_near, ends_recv).wait()

        @pl.loop(0, 4)
        def _(slot):
            order = slot // 2
            head = shared(order, lax.rem(slot, 2))
            q, k, v = [[qkv_near[slot, part, rows, :] for rows in blocks] for part in range(3)]
            g = [grad_near[slot, rows, :] for rows in blocks]
            dq, dk, dv = within(
                q, k, v, g, lambda t: wide_near[slot, blocks[t], :], lambda s: run_near[order, pl.ds(head, 1), blocks[s]]
            )
            entering, leaving = ends_near[0, slot], ends_near[1, slot]
            final = wide_near[slot, tokens - 1 :, :]
            for part, rows in enumerate(blocks):
                c = wide_near[slot, rows, :]
                live = wide_near[4 + order, rows, :] > 0.5
                until = jnp.exp(final - c)
                values = (
                    dq[part] + scale * jnp.exp(c) * contract(g[part], entering, LANES),
                    dk[part] + until * contract(v[part], leaving, LANES),
                    dv[part] + until * contract(k[part], leaving, PLAIN),
                )
                for at, value in enumerate(values):
                    grads[head, 2, rows, at * width : (at + 1) * width] = jnp.where(live, value, 0.0).astype(BF16)
            relay_move(head).start()

    def spread(ref, at, head):
        sum_in, sum_later = ref[0, at].astype(F32), ref[1, at].astype(F32)
        incoming[head] = jnp.where(
            is_low, sum_in, jnp.exp(total_of(chip * 2, head)) * sum_in + pair[0, head].astype(F32)
        ).astype(BF16)
        later[head] = jnp.where(
            is_low, jnp.exp(total_of(chip * 2 + 1, head)) * sum_later + pair[1, head].astype(F32), sum_later
        ).astype(BF16)

    def settle():
        for side in range(2):
            @pl.when(has_target(side))
            def _():
                for distance in range(size):
                    owner = me + (2 * side - 1) * distance

                    @pl.when((owner >= 0) & (owner < size))
                    def _():
                        whole(every.at[owner], send_sem.at[side, owner]).wait()

        whole(totals.at[pl.ds(0, shard_count - 1)], total_send).wait()
        whole(rows_ref.at[:, :, 1], mate_send).wait()
        for order in range(2):
            for which in range(2):
                block_at = chip_far if which else others[order]

                @pl.when(jnp.logical_not(is_end & (block_at == far_block)))
                def _():
                    whole(rows_ref.at[order, which, pl.ds(2, 2)], row_send.at[order, which]).wait()

            @pl.when(is_inner & ((far_block == chip) | (far_block == others[1 - order])))
            def _():
                whole(rows_ref.at[order, 0, pl.ds(2, 2)], pass_send.at[order]).wait()

        @pl.when(is_end)
        def _():
            whole(run_near, run_send).wait()
            whole(grad_near, copy_send).wait()
            whole(qkv_near, plain_send).wait()
            whole(ends_near, ends_send).wait()

        for index in range(2):
            half_move(index).wait_send()
        whole(mixed_in, mixed_send).wait()
        prefix_move.wait_send()

    def finish_all(grads, hop, hop_in):
        for target in (partner, chip_x * 2 + core, chip_y * 2 + core):
            pl.semaphore_signal(ready, inc=1, device_id={"context": target}, device_id_type=pl.DeviceIdType.MESH)

        whole(totals.at[pl.ds(0, shard_count - 1)], total_recv).wait()

        intra(0, FIRST)
        half_wait(0)

        for at in range(half):
            head = core * half + at
            mine, theirs = [[ref[kind, head].astype(F32) for kind in range(2)] for ref in (own, pair)]
            low, high = [
                [jnp.where(is_low == first, mine[kind], theirs[kind]) for kind in range(2)] for first in (True, False)
            ]
            mixed[0, at] = (jnp.exp(total_of(chip * 2 + 1, head)) * low[0] + high[0]).astype(BF16)
            mixed[1, at] = (low[1] + jnp.exp(total_of(chip * 2, head)) * high[1]).astype(BF16)

        for part in range(half // 2):
            for step in (2, 0, 1):
                mixed_move(step, part).start()

        def gather_states(part):
            for step in range(3):
                mixed_move(step, part).wait_recv()

            for at in range(2 * part, 2 * part + 2):
                head = core * half + at
                sum_in = jnp.zeros((width, width), F32)
                sum_later = jnp.zeros((width, width), F32)
                for step in range(3):
                    peer = others[step]
                    goes_up = peer > chip
                    first = jnp.where(goes_up, chip, peer) * 2 + 1
                    stop = jnp.where(goes_up, peer, chip) * 2
                    gap = jnp.zeros((1, width), F32)
                    for which in range(shard_count):
                        gap = gap + jnp.where((which > first) & (which < stop), total_of(which, head), 0.0)
                    term = jnp.exp(gap) * mixed_in[step, at].astype(F32)
                    sum_in = sum_in + jnp.where(goes_up, 0.0, term)
                    sum_later = sum_later + jnp.where(goes_up, term, 0.0)
                prefix[0, at] = sum_in.astype(BF16)
                prefix[1, at] = sum_later.astype(BF16)
                spread(prefix, at, head)

        def pair_move(head):
            return move(grads.at[head, 0], grads.at[head, 1], pair_send, pair_recv.at[head], partner)

        def near_move(head):
            near = chip_x + lax.rem(head, 2) * (chip_y - chip_x)
            return move(grads.at[head, 0], grads.at[head, 2], near_send, near_recv.at[head], near * 2 + core)

        def relay_move(head):
            return move(grads.at[head, 2], grads.at[head, 3], relay_send, relay_recv.at[head], partner)

        def hop_move(head):
            target = chip_y + lax.rem(head, 2) * (chip_x - chip_y)
            return move(hop.at[head], hop_in.at[head], hop_send, hop_recv.at[head], target * 2 + core)

        live = lax.broadcasted_iota(jnp.int32, (tokens, width), 0) < len_ref[0]

        def inter(first, stop):
            @pl.loop(first, stop)
            def _(index):
                head = at_order(index)
                cols = cols_of(head)
                c = wide[head]
                until = jnp.exp(wide[head, tokens - 1 :, :] - c)
                k, v, g = qkv[1, :, cols], qkv[2, :, cols], g_ref[:, cols]
                dq = sums[0, :, cols] + scale * jnp.exp(c) * contract(g, incoming[head], LANES)
                dk = sums[1, :, cols] + until * contract(v, later[head], LANES)
                dv = sums[2, :, cols] + until * contract(k, later[head], PLAIN)
                for part, value in enumerate((dq, dk, dv)):
                    grads[head, 0, :, part * width : (part + 1) * width] = jnp.where(live, value, 0.0).astype(BF16)

                @pl.when(jnp.logical_not(is_end & (lax.rem(index, half) >= half // 2)))
                def _():
                    near_move(head).start()

                pair_move(head).start()

        intra(FIRST, 3)
        half_wait(1)
        for part in range(half // 2):
            gather_states(part)
            if part == 0:
                pl.semaphore_wait(ready, 3)
            if part == half // 2 - 1:
                @pl.when(is_end)
                def _():
                    for order in range(2):
                        ends_share(order, core)

            inter(2 * part, 2 * part + 2)
            intra(2 * part + 3, 2 * part + 5)
            if part == 0:
                @pl.when(is_inner)
                def _():
                    rows_wait()
                    pass_rows()
        prefix_move.start()
        intra(half + 3, heads)
        prefix_move.wait_recv()
        for at in range(half):
            spread(prefix_in, at, (1 - core) * half + at)

        @pl.when(is_end)
        def _():
            for order in range(2):
                ends_share(order, 1 - core)

        inter(half, heads)

        @pl.when(is_end)
        def _():
            recompute(relay_move, grads)


        whole(rows_ref.at[:, :, 0], local_sem).wait()
        whole(rows_ref.at[:, :, 1], mate_recv).wait()

        @pl.when(is_end)
        def _():
            rows_wait()


        def product(head, which):
            lhs = rows_ref[lax.rem(head, 2), which].reshape(4 * tokens, strip)
            return contract(lhs, grads[head].reshape(4 * tokens, 3 * width), ROWS)

        def relay(index):
            head = at_order(index)
            near_move(head).wait_recv()
            relay_move(head).start()

        @pl.when(jnp.logical_not(is_end))
        def _():
            for index in range(half):
                relay(index)

        @pl.loop(0, half // 2)
        def _(turn):
            group = jnp.where(is_end, half // 2 - 1 - turn, turn)

            @pl.when(jnp.logical_not(is_end))
            def _():
                for index in range(2):
                    relay(half + 2 * turn + index)

            @pl.when(is_end & (turn > 0))
            def _():
                for index in (0, 1, half, half + 1):
                    relay(index)

            def head_at(index):
                return 2 * group + lax.rem(index, 2) + (index // 2) * half

            @pl.loop(0, 4)
            def _(index):
                head = head_at(index)
                pair_move(head).wait_recv()
                relay_move(head).wait_recv()
                hop[head] = product(head, 1).astype(BF16)
                hop_move(head).start()

            @pl.loop(0, 4)
            def _(index):
                head = head_at(index)
                value = product(head, 0)
                for part in range(3):
                    out_ref[part, :, cols_of(head)] = value[:, part * width : (part + 1) * width]

        settle()

        @pl.when(is_end)
        def _():
            whole(grads.at[pl.ds(0, half), 0], near_send).wait()

        @pl.when(jnp.logical_not(is_end))
        def _():
            whole(grads.at[:, 0], near_send).wait()

        whole(grads.at[:, 0], pair_send).wait()
        whole(grads.at[:, 0], relay_send).wait()

        @pl.loop(0, heads)
        def _(index):
            turn = index // 4
            group = jnp.where(is_end, half // 2 - 1 - turn, turn)
            head = 2 * group + lax.rem(index, 2) + (lax.rem(index, 4) // 2) * half
            hop_move(head).wait_recv()
            for part in range(3):
                out_ref[part, :, cols_of(head)] += hop_in[head, :, part * width : (part + 1) * width].astype(F32)

        whole(hop, hop_send).wait()

    pl.run_scoped(
        finish_all,
        pltpu.VMEM((heads, 4, tokens, 3 * width), BF16),
        pltpu.VMEM((heads, strip, 3 * width), BF16),
        pltpu.VMEM((heads, strip, 3 * width), BF16),
    )


def fused(scale, lengths, activations, decay, out_grad, weight, shard_count, size):
    tokens, depth = activations.shape
    columns = out_grad.shape[1]
    heads = decay.shape[0]
    width = columns // heads
    half = heads // 2
    strip = size * depth // shard_count
    dma = pltpu.SemaphoreType.DMA
    away = pl.BlockSpec(memory_space=pltpu.HBM)
    return pl.pallas_call(
        functools.partial(fused_kernel, scale),
        in_specs=[pl.BlockSpec(memory_space=pltpu.SMEM)] + [away] * 4,
        out_specs=pl.BlockSpec(memory_space=pltpu.VMEM),
        out_shape=jax.ShapeDtypeStruct((3, strip, columns), F32),
        scratch_shapes=[
            pltpu.VMEM((size, tokens, depth), BF16),
            pltpu.VMEM((heads, tokens), F32),
            pltpu.VMEM((heads, tokens), F32),
            pltpu.VMEM((heads, tokens, width), F32),
            pltpu.VMEM((shard_count, heads, width), F32),
            pltpu.VMEM((heads, width), F32),
            pltpu.VMEM((3, tokens, columns), BF16),
            pltpu.VMEM((tokens, columns), BF16),
            pltpu.VMEM((3, tokens, columns), F32),
            pltpu.VMEM((2, 2, 4, tokens, strip), BF16),
            pltpu.VMEM((2, heads, width, width), F32),
            pltpu.VMEM((2, heads, width, width), BF16),
            pltpu.VMEM((2, heads, width, width), BF16),
            pltpu.VMEM((2, half, width, width), BF16),
            pltpu.VMEM((3, half, width, width), BF16),
            pltpu.VMEM((2, half, width, width), BF16),
            pltpu.VMEM((2, half, width, width), BF16),
            pltpu.VMEM((heads, width, width), BF16),
            pltpu.VMEM((heads, width, width), BF16),
            pltpu.VMEM((2 * heads, tokens), F32),
            pltpu.VMEM((2, 2 * heads, tokens), F32),
            pltpu.VMEM((6, tokens, width), F32),
            pltpu.VMEM((4, 3, tokens, width), BF16),
            pltpu.VMEM((4, tokens, width), BF16),
            pltpu.VMEM((2, 4, width, width), BF16),
            dma((3,)),
            dma((size,)),
            dma((2, size)),
            dma((size, PIECES)),
            dma,
            dma,
            dma,
            dma,
            dma,
            dma((2, 2)),
            dma((2, 2)),
            dma((2,)),
            dma((2,)),
            dma,
            dma((3, half // 2)),
            dma((2,)),
        ] + [dma, dma((heads,))] * 4 + [dma((2,))] + [dma] * 8 + [pltpu.SemaphoreType.REGULAR],
        compiler_params=pltpu.CompilerParams(collective_id=1, has_side_effects=True, vmem_limit_bytes=GRANT << 20),
        name="fused",
    )(lengths, *(pltpu.with_memory_space_constraint(value, pltpu.HBM) for value in (activations, decay, out_grad, weight)))


FIRST = 1
GRANT = 48
UNROLL = 4


def pick(value, bit, mine, me):
    at = (me >> (bit + 1)) & 1
    return lax.dynamic_index_in_dim(value, at if mine else 1 - at, value.ndim - 3 - bit, keepdims=True)


def scatter_sum(lhs, rhs, bits, me, size):
    def times(block):
        flat = block.reshape((-1,) + block.shape[-2:])
        if flat.shape[0] == 1:
            result = contract(flat[0], rhs, ROWS)
        else:
            result = contract(flat, rhs, ((1,), (0,)))
        return result.reshape(block.shape[:-2] + (block.shape[-1], rhs.shape[1]))

    received = []
    keep = lhs
    for bit in bits:
        send = times(pick(keep, bit, False, me))
        for value in received:
            send = send + pick(value, bit, False, me).astype(F32)
        keep = pick(keep, bit, True, me)
        received = [pick(value, bit, True, me) for value in received]
        received.append(swap(send.astype(BF16), size, 2 << bit))
    total = times(keep)
    for value in received:
        total = total + value.astype(F32)
    return total.reshape(lhs.shape[-1], rhs.shape[1])


def is_square(shard_count, size):
    chips = shard_count // 2
    return chips == size and chips.bit_length() - 1 == 2


def shards(activations, qkv_weight, log_decay, lengths, out_grad):
    size = lax.axis_size("context")
    me = lax.axis_index("context")
    core = me & 1
    chip = me >> 1
    chips = size // 2
    tokens = activations.shape[0]
    heads = log_decay.shape[1]
    columns = out_grad.shape[1]
    width = columns // heads
    half = heads // 2
    scale = width ** -0.5

    if is_square(size, lax.axis_size("tensor")):
        return fused(
            scale, lengths, activations, log_decay.T, out_grad, qkv_weight.transpose(1, 0, 2), size, lax.axis_size("tensor")
        ).transpose(1, 0, 2)

    token_at = jnp.arange(tokens, dtype=jnp.int32)
    live = token_at < lengths[0]
    run_sum = jnp.cumsum(log_decay * live.astype(F32)[:, None], axis=0)
    run_wide = jnp.repeat(run_sum, width, axis=1)
    run_rows = run_sum.T
    own_total = run_sum[-1].astype(BF16).astype(F32)
    total_block = jnp.broadcast_to(jnp.pad(own_total, (0, 128 - heads))[None], (8, 128))
    live_column = live.astype(F32)[:, None]
    every, q, k, v, totals = project(
        activations, qkv_weight.transpose(1, 0, 2), live_column, total_block, size, lax.axis_size("tensor")
    )
    totals = totals[:, 0, :heads]

    rows = qkv_weight.shape[0] // size
    blocks = every.shape[2] // (2 * rows)
    low_rows, high_rows = [
        jnp.stack(
            [every[:, :, (2 * at + which) * rows : (2 * at + which + 1) * rows] for at in range(blocks)], axis=1
        ).reshape(chips, tokens, rows)
        for which in (0, 1)
    ]
    own_rows = jnp.where(core == 0, low_rows, high_rows)
    other_rows = swap(jnp.where(core == 0, high_rows, low_rows), size, 1)
    lhs = jnp.concatenate([own_rows, other_rows], axis=1)

    depth = chips.bit_length() - 1
    orders = (tuple(range(depth)), tuple(reversed(range(depth))))
    lhs = lhs.reshape((2,) * depth + lhs.shape[1:])
    lefts = []
    for order in orders:
        if not depth:
            lefts.append(lhs)
            continue
        moved = swap(pick(lhs, order[0], False, me), size, 2 << order[0])
        lefts.append(jnp.concatenate([pick(lhs, order[0], True, me), moved], axis=-2))

    head_spec = pl.BlockSpec((tokens, width), lambda h: (0, h))
    square_spec = pl.BlockSpec((1, width, width), lambda h: (h, 0, 0))
    wide = lambda kind: jax.ShapeDtypeStruct((tokens, columns), kind)
    squares = jax.ShapeDtypeStruct((heads, width, width), BF16)
    state, grad_state = pl.pallas_call(
        functools.partial(states_kernel, scale),
        grid=(heads,),
        in_specs=[head_spec] * 5,
        out_specs=[square_spec] * 2,
        out_shape=[squares] * 2,
        cost_estimate=pl.CostEstimate(flops=4 * tokens * columns * width, bytes_accessed=12 * tokens * columns, transcendentals=0),
        name="states",
    )(q, k, v, out_grad, run_wide)

    both = jnp.stack([state, grad_state])
    other = swap(both, size, 1)
    mine_half = lax.dynamic_slice_in_dim(both, core * half, half, 1).astype(F32)
    other_half = lax.dynamic_slice_in_dim(other, core * half, half, 1).astype(F32)
    pair_totals = lax.dynamic_slice_in_dim(totals, chip * 2, 2, 0)
    pair_half = lax.dynamic_slice_in_dim(pair_totals, core * half, half, 1)
    low, high = [jnp.where(core == which, mine_half, other_half) for which in (0, 1)]
    chip_state = (jnp.exp(pair_half[1])[:, None, None] * low[0] + high[0]).astype(BF16)
    chip_grad = (low[1] + jnp.exp(pair_half[0])[:, None, None] * high[1]).astype(BF16)

    arrivals = [
        swap(jnp.where((chip ^ step) > chip, chip_state, chip_grad), size, 2 * step) for step in range(1, chips)
    ]

    dq, dk, dv = pl.pallas_call(
        functools.partial(intra_kernel, scale),
        grid=(heads,),
        in_specs=[head_spec] * 5 + [pl.BlockSpec((heads, tokens), lambda h: (0, 0))],
        out_specs=[head_spec] * 3,
        out_shape=[wide(F32)] * 3,
        cost_estimate=pl.CostEstimate(
            flops=10 * tokens * tokens * columns, bytes_accessed=24 * tokens * columns, transcendentals=heads * tokens * tokens
        ),
        name="intra",
    )(q, k, v, out_grad, run_wide, run_rows)

    arrivals, dq, dk, dv = lax.optimization_barrier((arrivals, dq, dk, dv))
    upto = jnp.cumsum(totals, axis=0)
    totals_half = lax.dynamic_slice_in_dim(totals, core * half, half, 1)
    upto_half = lax.dynamic_slice_in_dim(upto, core * half, half, 1)
    chip_before = lax.dynamic_index_in_dim(upto_half - totals_half, chip * 2, 0, keepdims=False)
    chip_upto = lax.dynamic_index_in_dim(upto_half, chip * 2 + 1, 0, keepdims=False)
    incoming = jnp.zeros((half, width, width), F32)
    later = jnp.zeros((half, width, width), F32)
    for step in range(1, chips):
        peer = chip ^ step
        goes_up = peer > chip
        arrived = arrivals[step - 1].astype(F32)
        peer_upto = lax.dynamic_index_in_dim(upto_half, peer * 2 + 1, 0, keepdims=False)
        peer_before = lax.dynamic_index_in_dim(upto_half - totals_half, peer * 2, 0, keepdims=False)
        gap = jnp.where(goes_up, peer_before - chip_upto, chip_before - peer_upto)
        term = jnp.exp(gap)[:, None, None] * arrived
        incoming = incoming + jnp.where(goes_up, 0.0, term)
        later = later + jnp.where(goes_up, term, 0.0)
    from_chips = jnp.stack([incoming, later]).astype(BF16)
    other_chips = swap(from_chips, size, 1)
    is_low = core == 0
    from_chips = jnp.concatenate(
        [jnp.where(is_low, from_chips, other_chips), jnp.where(is_low, other_chips, from_chips)], axis=1
    ).astype(F32)
    incoming = jnp.where(
        is_low, from_chips[0], jnp.exp(pair_totals[0])[:, None, None] * from_chips[0] + other[0].astype(F32)
    ).astype(BF16)
    later = jnp.where(
        is_low, jnp.exp(pair_totals[1])[:, None, None] * from_chips[1] + other[1].astype(F32), from_chips[1]
    ).astype(BF16)

    grads = pl.pallas_call(
        functools.partial(inter_kernel, scale),
        grid=(heads,),
        in_specs=[pl.BlockSpec(memory_space=pltpu.SMEM)] + [head_spec] * 4 + [square_spec] * 2 + [head_spec] * 3,
        out_specs=[head_spec] * 3,
        out_shape=[wide(BF16)] * 3,
        cost_estimate=pl.CostEstimate(flops=6 * tokens * columns * width, bytes_accessed=28 * tokens * columns, transcendentals=0),
        name="inter",
    )(lengths, k, v, out_grad, run_wide, incoming, later, dq, dk, dv)

    results = []
    piece = columns // 2
    for part in grads:
        halves = [part[:, :piece], part[:, piece:]]
        if depth:
            moved = [swap(value, size, 2 << order[0]) for value, order in zip(halves, orders)]
            others = swap(jnp.concatenate(moved, axis=1), size, 1)
        partner = swap(part, size, 1)
        pieces = []
        for at, order in enumerate(orders):
            columns_at = slice(at * piece, (at + 1) * piece)
            rhs = [halves[at], partner[:, columns_at]]
            if depth:
                rhs += [moved[at], others[:, columns_at]]
            pieces.append(scatter_sum(lefts[at], jnp.concatenate(rhs, axis=0), order[1:], me, size))
        results.append(jnp.concatenate(pieces, axis=1))
    return jnp.stack(results, axis=1)


def solution(mesh):
    step = jax.shard_map(
        shards,
        mesh=mesh,
        in_specs=(
            P("context", "tensor"),
            P(None, None, "tensor"),
            P("context", "tensor"),
            P("context"),
            P("context", "tensor"),
        ),
        out_specs=P("context", None, "tensor"),
        check_vma=False,
    )
    if is_square(mesh.shape["context"], mesh.shape["tensor"]):
        return step
    return step
```

```python
import functools

import jax
import jax.numpy as jnp
from jax import lax
from jax.experimental import pallas as pl
from jax.experimental.pallas import tpu as pltpu
from jax.sharding import PartitionSpec as P


F32 = jnp.float32
BF16 = jnp.bfloat16


def contract(a, b, dims):
    return lax.dot_general(a, b, (dims, ((), ())), preferred_element_type=F32)


ROWS = ((0,), (0,))
LANES = ((1,), (1,))
PLAIN = ((1,), (0,))


def states_kernel(scale, q_ref, k_ref, v_ref, g_ref, c_ref, state_ref, grad_ref):
    c = c_ref[...]
    total = c[-1:, :]
    weighted_k = (k_ref[...].astype(F32) * jnp.exp(total - c)).astype(BF16)
    state_ref[0] = contract(weighted_k, v_ref[...], ROWS).astype(BF16)
    weighted_q = (q_ref[...].astype(F32) * (scale * jnp.exp(c))).astype(BF16)
    grad_ref[0] = contract(weighted_q, g_ref[...], ROWS).astype(BF16)


def intra_kernel(scale, q_ref, k_ref, v_ref, g_ref, c_ref, ct_ref, dq_ref, dk_ref, dv_ref):
    head = pl.program_id(0)
    q, k, v, g = q_ref[...], k_ref[...], v_ref[...], g_ref[...]
    tokens, width = q.shape
    column = jnp.concatenate([c_ref[...]] * (tokens // width), axis=1)
    gap = column - ct_ref[pl.ds(head, 1), :]
    row_at = lax.broadcasted_iota(jnp.int32, (tokens, tokens), 0)
    col_at = lax.broadcasted_iota(jnp.int32, (tokens, tokens), 1)
    decay = jnp.exp(jnp.where(row_at >= col_at, gap, -jnp.inf))
    prob = (contract(q, k, LANES) * scale * decay).astype(BF16)
    score = (contract(g, v, LANES) * decay).astype(BF16)
    dq_ref[...] = scale * contract(score, k, PLAIN)
    dk_ref[...] = scale * contract(score, q, ROWS)
    dv_ref[...] = contract(prob, g, ROWS)


def inter_kernel(scale, len_ref, k_ref, v_ref, g_ref, c_ref, in_ref, later_ref, dq_ref, dk_ref, dv_ref,
                 oq_ref, ok_ref, ov_ref):
    c = c_ref[...]
    live = lax.broadcasted_iota(jnp.int32, c.shape, 0) < len_ref[0]
    until = jnp.exp(c[-1:, :] - c)
    dq = dq_ref[...] + scale * jnp.exp(c) * contract(g_ref[...], in_ref[0], LANES)
    dk = dk_ref[...] + until * contract(v_ref[...], later_ref[0], LANES)
    dv = dv_ref[...] + until * contract(k_ref[...], later_ref[0], PLAIN)
    oq_ref[...] = jnp.where(live, dq, 0.0).astype(BF16)
    ok_ref[...] = jnp.where(live, dk, 0.0).astype(BF16)
    ov_ref[...] = jnp.where(live, dv, 0.0).astype(BF16)


def swap(value, size, distance):
    return lax.ppermute(value, "context", [(i, i ^ distance) for i in range(size)])


PIECES = 4
TILE = 512


def project_kernel(act_ref, live_ref, total_ref, weight_ref, every_ref, q_ref, k_ref, v_ref, totals_ref,
                   weights, sums, own_sem, weight_sem, send_sem, recv_sem, total_send, total_recv):
    size, me = lax.axis_size("tensor"), lax.axis_index("tensor")
    shard_count, shard = lax.axis_size("context"), lax.axis_index("context")
    depth = act_ref.shape[1]
    piece = act_ref.shape[0] // PIECES
    columns = q_ref.shape[1]
    tiles = columns // TILE

    def load(owner, part):
        rows = pl.ds(pl.multiple_of(owner * depth, depth), depth)
        return pltpu.make_async_copy(weight_ref.at[part, rows], weights.at[owner, part], weight_sem.at[owner, part])

    for at in range(size):
        owner = lax.rem(me + at, size)
        for part in range(3):
            load(owner, part).start()

    barrier = pltpu.get_barrier_semaphore()
    for target in (me - 1, me + 1):
        @pl.when((target >= 0) & (target < size))
        def _():
            pl.semaphore_signal(barrier, inc=1, device_id={"tensor": target}, device_id_type=pl.DeviceIdType.MESH)

    @pl.loop(1, shard_count)
    def _(step):
        peer = lax.rem(shard + step, shard_count)
        pl.semaphore_signal(barrier, inc=1, device_id={"context": peer}, device_id_type=pl.DeviceIdType.MESH)

    neighbours = jnp.where(me > 0, 1, 0) + jnp.where(me < size - 1, 1, 0)
    pl.semaphore_wait(barrier, neighbours + shard_count - 1)

    def rows_of(at):
        return pl.ds(pl.multiple_of(at * piece, piece), piece)

    def send(source, owner, at, side):
        return pltpu.make_async_remote_copy(
            src_ref=source,
            dst_ref=every_ref.at[owner, rows_of(at)],
            send_sem=send_sem.at[side, owner, at],
            recv_sem=recv_sem.at[owner, at],
            device_id={"tensor": me + 1 - 2 * side},
            device_id_type=pl.DeviceIdType.MESH,
        )

    def has_target(side):
        target = me + 1 - 2 * side
        return (target >= 0) & (target < size)

    def send_total(step):
        peer = lax.rem(shard + step, shard_count)
        return pltpu.make_async_remote_copy(
            src_ref=total_ref,
            dst_ref=totals_ref.at[shard],
            send_sem=total_send.at[peer],
            recv_sem=total_recv.at[shard],
            device_id={"context": peer},
            device_id_type=pl.DeviceIdType.MESH,
        )

    for at in range(PIECES):
        for side in range(2):
            @pl.when(has_target(side))
            def _():
                send(act_ref.at[rows_of(at)], me, at, side).start()

    @pl.loop(1, shard_count)
    def _(step):
        send_total(step).start()

    own = pltpu.make_async_copy(act_ref, every_ref.at[me], own_sem)
    own.start()
    totals_ref[shard] = total_ref[...]

    for part in range(3):
        load(me, part).wait()

    @pl.loop(0, 3 * tiles)
    def _(tile):
        part = tile // tiles
        cols = pl.ds(pl.multiple_of(lax.rem(tile, tiles) * TILE, TILE), TILE)
        sums[part, :, cols] = jnp.dot(act_ref[...], weights[me, part, :, cols], preferred_element_type=F32)

    own.wait()
    for distance in range(1, size):
        for side in range(2):
            owner = me + (2 * side - 1) * distance

            @pl.when((owner >= 0) & (owner < size))
            def _():
                for part in range(3):
                    load(owner, part).wait()

        @pl.loop(0, PIECES)
        def _(at):
            for side in range(2):
                owner = me + (2 * side - 1) * distance

                @pl.when((owner >= 0) & (owner < size))
                def _():
                    pltpu.make_async_copy(
                        every_ref.at[owner, rows_of(at)], every_ref.at[owner, rows_of(at)], recv_sem.at[owner, at]
                    ).wait()

                    @pl.when(has_target(side))
                    def _():
                        send(every_ref.at[owner, rows_of(at)], owner, at, side).start()

            @pl.loop(0, 2)
            def _(side):
                owner = me + (2 * side - 1) * distance

                @pl.when((owner >= 0) & (owner < size))
                def _():
                    @pl.loop(0, 3 * tiles)
                    def _(tile):
                        part = tile // tiles
                        cols = pl.ds(pl.multiple_of(lax.rem(tile, tiles) * TILE, TILE), TILE)
                        sums[part, rows_of(at), cols] += jnp.dot(
                            every_ref[owner, rows_of(at), :], weights[owner, part, :, cols], preferred_element_type=F32
                        )

    live = live_ref[...]
    for part, ref in enumerate((q_ref, k_ref, v_ref)):
        @pl.loop(0, tiles)
        def _(tile):
            cols = pl.ds(pl.multiple_of(tile * TILE, TILE), TILE)
            ref[:, cols] = (sums[part, :, cols] * live).astype(BF16)

    for side in range(2):
        @pl.when(has_target(side))
        def _():
            for distance in range(size):
                owner = me + (2 * side - 1) * distance

                @pl.when((owner >= 0) & (owner < size))
                def _():
                    for at in range(PIECES):
                        send(every_ref.at[owner, rows_of(at)], owner, at, side).wait_send()

    @pl.loop(1, shard_count)
    def _(step):
        peer = lax.rem(shard + step, shard_count)
        send_total(step).wait_send()
        pltpu.make_async_copy(total_ref, totals_ref.at[peer], total_recv.at[peer]).wait()


def project(activations, weight, live, total, shard_count, size):
    tokens, depth = activations.shape
    columns = weight.shape[2]
    vmem = pl.BlockSpec(memory_space=pltpu.VMEM)
    heads_out = [jax.ShapeDtypeStruct((tokens, columns), BF16)] * 3
    return pl.pallas_call(
        project_kernel,
        in_specs=[vmem] * 3 + [pl.BlockSpec(memory_space=pl.ANY)],
        out_specs=[vmem] * 5,
        out_shape=[jax.ShapeDtypeStruct((size, tokens, depth), BF16)]
        + heads_out
        + [jax.ShapeDtypeStruct((shard_count,) + total.shape, F32)],
        scratch_shapes=[
            pltpu.VMEM((size, 3, depth, columns), BF16),
            pltpu.VMEM((3, tokens, columns), F32),
            pltpu.SemaphoreType.DMA,
            pltpu.SemaphoreType.DMA((size, 3)),
            pltpu.SemaphoreType.DMA((2, size, PIECES)),
            pltpu.SemaphoreType.DMA((size, PIECES)),
            pltpu.SemaphoreType.DMA((shard_count,)),
            pltpu.SemaphoreType.DMA((shard_count,)),
        ],
        compiler_params=pltpu.CompilerParams(collective_id=0, has_side_effects=True, vmem_limit_bytes=48 << 20),
        name="project",
    )(activations, live, total, weight)


def flips(chip):
    bx, by = lax.rem(chip, 2), chip // 2
    return chip + 1 - 2 * bx, chip + 2 - 4 * by, 3 - chip


def fused_kernel(scale, len_ref, act_ref, decay_ref, grad_ref, weight_ref, out_ref,
                 every, decay, run, wide, totals, own_total, qkv, g_ref, sums, rows_ref, acc, own, pair, mixed, mixed_in,
                 prefix, prefix_in, incoming, later,
                 run_out, run_near, wide_near, qkv_near, grad_near, ends_near,
                 input_sem, weight_sem, send_sem, recv_sem, total_send, total_recv, local_sem, mate_send, mate_recv,
                 row_send, row_recv, own_send, own_recv, mixed_send, mixed_recv, prefix_send, prefix_recv, pair_send, pair_recv,
                 near_send, near_recv, relay_send, relay_recv, hop_send, hop_recv, pass_send, run_send, run_recv,
                 copy_send, copy_recv, plain_send, plain_recv, ends_send, ends_recv, ready):
    size, me = lax.axis_size("tensor"), lax.axis_index("tensor")
    shard_count, shard = lax.axis_size("context"), lax.axis_index("context")
    core, chip = lax.rem(shard, 2), shard // 2
    others = flips(chip)
    chip_x, chip_y, chip_far = others
    partner = chip * 2 + 1 - core
    is_low = core == 0
    tokens, depth = act_ref.shape
    columns = grad_ref.shape[1]
    heads = decay_ref.shape[0]
    width = columns // heads
    half = heads // 2
    piece = tokens // PIECES
    tiles = columns // TILE
    strip = rows_ref.shape[-1]
    block = tokens // 2
    last = jnp.maximum(me, size - 1 - me)
    is_end = (me == 0) | (me == size - 1)
    is_inner = (me == 1) | (me == size - 2)
    outward = jnp.where(me == 1, 0, size - 1)
    far_block = jnp.where(me < size // 2, size - 1, 0)

    def shared(order, side):
        return order + half * side

    def move(source, target, send_at, recv_at, peer):
        return pltpu.make_async_remote_copy(
            src_ref=source, dst_ref=target, send_sem=send_at, recv_sem=recv_at,
            device_id={"context": peer}, device_id_type=pl.DeviceIdType.MESH,
        )

    def whole(view, sem):
        return pltpu.make_async_copy(view, view, sem)

    def rows_of(at):
        return pl.ds(pl.multiple_of(at * piece, piece), piece)

    def cols_of(head):
        return pl.ds(pl.multiple_of(head * width, width), width)

    def strip_of(which):
        return pl.ds(pl.multiple_of(which * strip, strip), strip)

    def at_order(index):
        return lax.rem(core * half + index, heads)

    def send(source, owner, at, side):
        return pltpu.make_async_remote_copy(
            src_ref=source,
            dst_ref=every.at[owner, rows_of(at)],
            send_sem=send_sem.at[side, owner],
            recv_sem=recv_sem.at[owner, at],
            device_id={"tensor": me + 1 - 2 * side},
            device_id_type=pl.DeviceIdType.MESH,
        )

    def has_target(side):
        target = me + 1 - 2 * side
        return (target >= 0) & (target < size)

    def send_total(step):
        peer = lax.rem(shard + step, shard_count)
        return move(own_total, totals.at[shard], total_send, total_recv, peer)

    def keep(source, at, order, which):
        return pltpu.make_async_copy(
            source.at[rows_of(at), strip_of(core)], rows_ref.at[order, which, 0, rows_of(at)], local_sem
        )

    def mate(source, at, order, which):
        return move(
            source.at[rows_of(at), strip_of(1 - core)], rows_ref.at[order, which, 1, rows_of(at)],
            mate_send, mate_recv, partner,
        )

    def across(source, at, order, which, other):
        target = core + other - 2 * core * other
        return move(
            source.at[rows_of(at), strip_of(target)], rows_ref.at[order, which, 2 + other, rows_of(at)],
            row_send.at[order, which], row_recv.at[order, which], others[order] * 2 + target,
        )

    def deliver(source, owner, at):
        for order in range(2):
            near, far = others[order], others[1 - order]

            @pl.when(((owner == near) | (owner == chip_far)) & jnp.logical_not(is_end & (owner == far_block)))
            def _():
                which = jnp.where(owner == near, 0, 1)
                for other in range(2):
                    across(source, at, order, which, other).start()

            @pl.when((owner == chip) | (owner == far))
            def _():
                which = jnp.where(owner == chip, 0, 1)
                keep(source, at, order, which).start()
                mate(source, at, order, which).start()

    def rows_wait(which):
        for order in range(2):
            whole(rows_ref.at[order, which, pl.ds(2, 2)], row_recv.at[order, which]).wait()

    def pass_rows():
        for order in range(2):
            @pl.when((far_block == chip) | (far_block == others[1 - order]))
            def _():
                which = jnp.where(far_block == chip, 0, 1)
                view = rows_ref.at[order, which, pl.ds(2, 2)]
                pltpu.make_async_remote_copy(
                    src_ref=view, dst_ref=view, send_sem=pass_send.at[order], recv_sem=row_recv.at[order, which],
                    device_id={"tensor": outward}, device_id_type=pl.DeviceIdType.MESH,
                ).start()

    def grad_share(order, side):
        return move(
            grad_ref.at[:, cols_of(shared(order, side))], grad_near.at[2 * order + side], copy_send, copy_recv,
            others[order] * 2 + core,
        )

    def run_share(order):
        return move(run_out, run_near.at[order], run_send, run_recv, others[order] * 2 + core)

    def qkv_share(order, side, at):
        return move(
            qkv.at[:, rows_of(at), cols_of(shared(order, side))], qkv_near.at[2 * order + side, :, rows_of(at)],
            plain_send, plain_recv, others[order] * 2 + core,
        )

    def ends_share(order, side):
        for kind, ref in enumerate((incoming, later)):
            move(
                ref.at[shared(order, side)], ends_near.at[side, kind, order], ends_send, ends_recv.at[side],
                others[order] * 2 + core,
            ).start()

    act_copy = pltpu.make_async_copy(act_ref, every.at[me], input_sem.at[0])
    decay_copy = pltpu.make_async_copy(decay_ref, decay, input_sem.at[1])
    grad_copy = pltpu.make_async_copy(grad_ref, g_ref, input_sem.at[2])

    barrier = pltpu.get_barrier_semaphore()
    for target in (me - 1, me + 1):
        @pl.when((target >= 0) & (target < size))
        def _():
            pl.semaphore_signal(barrier, inc=1, device_id={"tensor": target}, device_id_type=pl.DeviceIdType.MESH)

    @pl.loop(1, shard_count)
    def _(step):
        peer = lax.rem(shard + step, shard_count)
        pl.semaphore_signal(barrier, inc=1, device_id={"context": peer}, device_id_type=pl.DeviceIdType.MESH)

    act_copy.start()
    decay_copy.start()
    neighbours = jnp.where(me > 0, 1, 0) + jnp.where(me < size - 1, 1, 0)
    pl.semaphore_wait(barrier, neighbours + shard_count - 1)

    for at in range(PIECES):
        for side in range(2):
            @pl.when(has_target(side))
            def _():
                send(act_ref.at[rows_of(at)], me, at, side).start()

    @pl.loop(0, PIECES)
    def _(at):
        deliver(act_ref, me, at)

    @pl.when(is_end)
    def _():
        for order in range(2):
            for side in range(2):
                grad_share(order, side).start()

    def running_sums():
        token_at = lax.broadcasted_iota(jnp.int32, (heads, tokens), 1)
        masked = jnp.where(token_at < len_ref[0], decay[...], 0.0)
        row_at = lax.broadcasted_iota(jnp.int32, (tokens, tokens), 0)
        col_at = lax.broadcasted_iota(jnp.int32, (tokens, tokens), 1)
        upto = jnp.where(row_at <= col_at, 1.0, 0.0)
        c = lax.dot_general(
            masked, upto, (PLAIN, ((), ())), precision=lax.Precision.HIGHEST, preferred_element_type=F32
        )
        run[...] = c
        run_out[0:heads] = c
        run_out[heads : 2 * heads] = jnp.where(token_at < len_ref[0], 1.0, 0.0)
        total = c[:, tokens - 1 :].astype(BF16).astype(F32)
        own_total[...] = jnp.broadcast_to(total, own_total.shape)
        totals[shard] = jnp.broadcast_to(total, own_total.shape)
        column = jnp.concatenate([c, jnp.zeros((width - heads, tokens), F32)], axis=0).T
        for head in range(heads):
            wide[head] = jnp.broadcast_to(column[:, head : head + 1], (tokens, width))

    def half_move(index):
        side = index + core - 2 * index * core
        part = pl.ds((1 - side) * half, half)
        return move(own.at[:, part], pair.at[:, part], own_send.at[index], own_recv.at[index], partner)

    def states(at, first):
        @pl.loop(0, half, unroll=UNROLL)
        def _(index):
            head = first + index
            cols, rows = cols_of(head), rows_of(at)
            c = wide[head, rows, :]
            total = wide[head, tokens - 1 :, :]
            weighted_k = (qkv[1, rows, cols].astype(F32) * jnp.exp(total - c)).astype(BF16)
            acc[0, head] += contract(weighted_k, qkv[2, rows, cols], ROWS)
            weighted_q = (qkv[0, rows, cols].astype(F32) * (scale * jnp.exp(c))).astype(BF16)
            acc[1, head] += contract(weighted_q, g_ref[rows, cols], ROWS)

    def project_all(weights):
        def load(owner, part):
            rows = pl.ds(pl.multiple_of(owner * depth, depth), depth)
            return pltpu.make_async_copy(weight_ref.at[part, rows], weights.at[owner, part], weight_sem.at[owner])

        def loaded(owner):
            return pltpu.make_async_copy(weights.at[owner], weights.at[owner], weight_sem.at[owner])

        for at in range(size):
            owner = lax.rem(me + at, size)
            for part in range(3):
                load(owner, part).start()
        grad_copy.start()

        decay_copy.wait()
        running_sums()

        @pl.loop(1, shard_count)
        def _(step):
            send_total(step).start()

        @pl.when(is_end)
        def _():
            for order in range(2):
                run_share(order).start()

        acc[...] = jnp.zeros_like(acc)
        act_copy.wait()
        loaded(me).wait()

        def tile_at(tile):
            return tile // tiles, pl.ds(pl.multiple_of(lax.rem(tile, tiles) * TILE, TILE), TILE)

        @pl.loop(0, 3 * tiles)
        def _(tile):
            part, cols = tile_at(tile)
            sums[part, :, cols] = jnp.dot(every[me], weights[me, part, :, cols], preferred_element_type=F32)

        grad_copy.wait()

        for distance in range(1, size):
            for side in range(2):
                owner = me + (2 * side - 1) * distance

                @pl.when((owner >= 0) & (owner < size))
                def _():
                    loaded(owner).wait()

            @pl.loop(0, PIECES)
            def _(at):
                rows = rows_of(at)
                for side in range(2):
                    owner = me + (2 * side - 1) * distance

                    @pl.when((owner >= 0) & (owner < size))
                    def _():
                        pltpu.make_async_copy(
                            every.at[owner, rows], every.at[owner, rows], recv_sem.at[owner, at]
                        ).wait()

                        @pl.when(has_target(side))
                        def _():
                            send(every.at[owner, rows], owner, at, side).start()

                        deliver(every.at[owner], owner, at)

                @pl.loop(0, 2)
                def _(side):
                    owner = me + (2 * side - 1) * distance
                    valid = (owner >= 0) & (owner < size)

                    def product(part, cols):
                        return sums[part, rows, cols] + jnp.dot(
                            every[owner, rows, :], weights[owner, part, :, cols], preferred_element_type=F32
                        )

                    @pl.when(valid & (distance < last))
                    def _():
                        @pl.loop(0, 3 * tiles)
                        def _(tile):
                            part, cols = tile_at(tile)
                            sums[part, rows, cols] = product(part, cols)

                    if distance >= size // 2:
                        @pl.when(valid & (distance == last))
                        def _():
                            token_at = at * piece + lax.broadcasted_iota(jnp.int32, (piece, TILE), 0)
                            live = token_at < len_ref[0]

                            for index in range(2):
                                first = (1 - core if index == 0 else core) * half

                                @pl.loop(0, 3 * tiles // 2)
                                def _(tile):
                                    part, start = tile // (tiles // 2), lax.rem(tile, tiles // 2) * TILE
                                    cols = pl.ds(pl.multiple_of(first * width + start, width), TILE)
                                    qkv[part, rows, cols] = jnp.where(live, product(part, cols), 0.0).astype(BF16)

                                states(at, first)

                                @pl.when(is_end & ((at < PIECES - 1) | (index == 0)))
                                def _():
                                    for order in range(2):
                                        qkv_share(order, 1 - core if index == 0 else core, at).start()

                                @pl.when(at == PIECES - 1)
                                def _():
                                    own[:, pl.ds(first, half)] = acc[:, pl.ds(first, half)].astype(BF16)
                                    half_move(index).start()

    pl.run_scoped(project_all, pltpu.VMEM((size, 3, depth, columns), BF16))

    def half_wait(index):
        side = index + core - 2 * index * core
        part = pl.ds(side * half, half)
        pltpu.make_async_copy(pair.at[:, part], pair.at[:, part], own_recv.at[index]).wait()

    def mixed_move(step, part):
        kind = jnp.where(others[step] > chip, 0, 1)
        at = pl.ds(part * 2, 2)
        return move(
            mixed.at[kind, at], mixed_in.at[step, at], mixed_send, mixed_recv.at[step, part], others[step] * 2 + core
        )

    def prefix_move(part):
        at = pl.ds(2 * part, 2)
        return move(prefix.at[:, at], prefix_in.at[:, at], prefix_send, prefix_recv.at[part], partner)

    def total_of(which, head):
        return totals[which, pl.ds(head, 1), :]

    def within(q, k, v, g, column_at, row_at_block):
        dq, dk, dv = [None] * 2, [None] * 2, [None] * 2

        def add(held, part, value):
            held[part] = value if held[part] is None else held[part] + value

        for t in range(2):
            column = jnp.concatenate([column_at(t)] * (block // width), axis=1)
            for s in range(t + 1):
                gap = column - row_at_block(s)
                if s == t:
                    row_at = lax.broadcasted_iota(jnp.int32, (block, block), 0)
                    col_at = lax.broadcasted_iota(jnp.int32, (block, block), 1)
                    gap = jnp.where(row_at >= col_at, gap, -jnp.inf)
                decayed = jnp.exp(gap)
                prob = (contract(q[t], k[s], LANES) * scale * decayed).astype(BF16)
                score = (contract(g[t], v[s], LANES) * decayed).astype(BF16)
                add(dq, t, contract(score, k[s], PLAIN))
                add(dk, s, contract(score, q[t], ROWS))
                add(dv, s, contract(prob, g[t], ROWS))
        return [scale * value for value in dq], [scale * value for value in dk], dv

    blocks = [slice(part * block, (part + 1) * block) for part in range(2)]

    def intra(first, stop):
        @pl.loop(first, stop)
        def _(index):
            head = at_order(index)
            cols = cols_of(head)
            q, k, v = [[qkv[part, rows, cols] for rows in blocks] for part in range(3)]
            g = [g_ref[rows, cols] for rows in blocks]
            results = within(
                q, k, v, g, lambda t: wide[head, blocks[t], :], lambda s: run[pl.ds(head, 1), blocks[s]]
            )
            for part, values in enumerate(results):
                for index, value in enumerate(values):
                    sums[part, blocks[index], cols] = value

    def recompute(relay_move, grads):
        whole(run_near, run_recv).wait()
        for order in range(2):
            column = jnp.concatenate([run_near[order], jnp.zeros((width - 2 * heads, tokens), F32)], axis=0).T
            for side in range(2):
                head = shared(order, side)
                wide_near[2 * order + side] = jnp.broadcast_to(column[:, head : head + 1], (tokens, width))
            wide_near[4 + order] = jnp.broadcast_to(column[:, heads : heads + 1], (tokens, width))
        whole(grad_near, copy_recv).wait()
        whole(qkv_near, plain_recv).wait()

        for index in range(2):
            side = core if index == 0 else 1 - core
            whole(ends_near.at[side], ends_recv.at[side]).wait()

            @pl.loop(0, 2)
            def _(order):
                slot = 2 * order + side
                head = shared(order, side)
                q, k, v = [[qkv_near[slot, part, rows, :] for rows in blocks] for part in range(3)]
                g = [grad_near[slot, rows, :] for rows in blocks]
                dq, dk, dv = within(
                    q, k, v, g, lambda t: wide_near[slot, blocks[t], :], lambda s: run_near[order, pl.ds(head, 1), blocks[s]]
                )
                entering, leaving = ends_near[side, 0, order], ends_near[side, 1, order]
                final = wide_near[slot, tokens - 1 :, :]
                for part, rows in enumerate(blocks):
                    c = wide_near[slot, rows, :]
                    live = wide_near[4 + order, rows, :] > 0.5
                    until = jnp.exp(final - c)
                    values = (
                        dq[part] + scale * jnp.exp(c) * contract(g[part], entering, LANES),
                        dk[part] + until * contract(v[part], leaving, LANES),
                        dv[part] + until * contract(k[part], leaving, PLAIN),
                    )
                    for at, value in enumerate(values):
                        grads[head, 2, rows, at * width : (at + 1) * width] = jnp.where(live, value, 0.0).astype(BF16)
                relay_move(head).start()

    def spread(ref, at, head):
        sum_in, sum_later = ref[0, at].astype(F32), ref[1, at].astype(F32)
        incoming[head] = jnp.where(
            is_low, sum_in, jnp.exp(total_of(chip * 2, head)) * sum_in + pair[0, head].astype(F32)
        ).astype(BF16)
        later[head] = jnp.where(
            is_low, jnp.exp(total_of(chip * 2 + 1, head)) * sum_later + pair[1, head].astype(F32), sum_later
        ).astype(BF16)

    def settle():
        for side in range(2):
            @pl.when(has_target(side))
            def _():
                for distance in range(size):
                    owner = me + (2 * side - 1) * distance

                    @pl.when((owner >= 0) & (owner < size))
                    def _():
                        whole(every.at[owner], send_sem.at[side, owner]).wait()

        whole(totals.at[pl.ds(0, shard_count - 1)], total_send).wait()
        whole(rows_ref.at[:, :, 1], mate_send).wait()
        for order in range(2):
            for which in range(2):
                block_at = chip_far if which else others[order]

                @pl.when(jnp.logical_not(is_end & (block_at == far_block)))
                def _():
                    whole(rows_ref.at[order, which, pl.ds(2, 2)], row_send.at[order, which]).wait()

            @pl.when(is_inner & ((far_block == chip) | (far_block == others[1 - order])))
            def _():
                whole(rows_ref.at[order, 0, pl.ds(2, 2)], pass_send.at[order]).wait()

        @pl.when(is_end)
        def _():
            whole(run_near, run_send).wait()
            whole(grad_near, copy_send).wait()
            whole(qkv_near, plain_send).wait()
            whole(ends_near, ends_send).wait()

        for index in range(2):
            half_move(index).wait_send()
        whole(mixed_in, mixed_send).wait()
        whole(prefix_in, prefix_send).wait()

    def finish_all(grads, hop, hop_in):
        for target in (partner, chip_x * 2 + core, chip_y * 2 + core):
            pl.semaphore_signal(ready, inc=1, device_id={"context": target}, device_id_type=pl.DeviceIdType.MESH)

        whole(totals.at[pl.ds(0, shard_count - 1)], total_recv).wait()

        intra(0, FIRST)
        half_wait(0)

        for at in range(half):
            head = core * half + at
            mine, theirs = [[ref[kind, head].astype(F32) for kind in range(2)] for ref in (own, pair)]
            low, high = [
                [jnp.where(is_low == first, mine[kind], theirs[kind]) for kind in range(2)] for first in (True, False)
            ]
            mixed[0, at] = (jnp.exp(total_of(chip * 2 + 1, head)) * low[0] + high[0]).astype(BF16)
            mixed[1, at] = (low[1] + jnp.exp(total_of(chip * 2, head)) * high[1]).astype(BF16)

        for part in range(half // 2):
            for step in (2, 0, 1):
                mixed_move(step, part).start()

        @pl.when(is_end)
        def _():
            for order in range(2):
                qkv_share(order, core, PIECES - 1).start()

        def gather_states(part):
            for step in range(3):
                mixed_move(step, part).wait_recv()

            for at in range(2 * part, 2 * part + 2):
                head = core * half + at
                sum_in = jnp.zeros((width, width), F32)
                sum_later = jnp.zeros((width, width), F32)
                for step in range(3):
                    peer = others[step]
                    goes_up = peer > chip
                    first = jnp.where(goes_up, chip, peer) * 2 + 1
                    stop = jnp.where(goes_up, peer, chip) * 2
                    gap = jnp.zeros((1, width), F32)
                    for which in range(shard_count):
                        gap = gap + jnp.where((which > first) & (which < stop), total_of(which, head), 0.0)
                    term = jnp.exp(gap) * mixed_in[step, at].astype(F32)
                    sum_in = sum_in + jnp.where(goes_up, 0.0, term)
                    sum_later = sum_later + jnp.where(goes_up, term, 0.0)
                prefix[0, at] = sum_in.astype(BF16)
                prefix[1, at] = sum_later.astype(BF16)
                spread(prefix, at, head)

        def pair_move(head):
            return move(grads.at[head, 0], grads.at[head, 1], pair_send, pair_recv.at[head], partner)

        def near_move(head):
            near = chip_x + lax.rem(head, 2) * (chip_y - chip_x)
            return move(grads.at[head, 0], grads.at[head, 2], near_send, near_recv.at[head], near * 2 + core)

        def relay_move(head):
            return move(grads.at[head, 2], grads.at[head, 3], relay_send, relay_recv.at[head], partner)

        def hop_move(head):
            target = chip_y + lax.rem(head, 2) * (chip_x - chip_y)
            return move(hop.at[head], hop_in.at[head], hop_send, hop_recv.at[head], target * 2 + core)

        live = lax.broadcasted_iota(jnp.int32, (tokens, width), 0) < len_ref[0]

        def inter(first, stop):
            @pl.loop(first, stop)
            def _(index):
                head = at_order(index)
                cols = cols_of(head)
                c = wide[head]
                until = jnp.exp(wide[head, tokens - 1 :, :] - c)
                k, v, g = qkv[1, :, cols], qkv[2, :, cols], g_ref[:, cols]
                dq = sums[0, :, cols] + scale * jnp.exp(c) * contract(g, incoming[head], LANES)
                dk = sums[1, :, cols] + until * contract(v, later[head], LANES)
                dv = sums[2, :, cols] + until * contract(k, later[head], PLAIN)
                for part, value in enumerate((dq, dk, dv)):
                    grads[head, 0, :, part * width : (part + 1) * width] = jnp.where(live, value, 0.0).astype(BF16)

                @pl.when(jnp.logical_not(is_end & (lax.rem(index, half) < half // 2)))
                def _():
                    near_move(head).start()

                pair_move(head).start()

        def gather_others(part):
            prefix_move(part).wait_recv()
            for at in range(2 * part, 2 * part + 2):
                spread(prefix_in, at, (1 - core) * half + at)

        intra(FIRST, 3)
        half_wait(1)
        for part in range(half // 2):
            gather_states(part)
            prefix_move(part).start()
            if part == 0:
                pl.semaphore_wait(ready, 3)

                @pl.when(is_end)
                def _():
                    for order in range(2):
                        ends_share(order, core)

            inter(2 * part, 2 * part + 2)
            if part == 0:
                gather_others(part)

                @pl.when(is_end)
                def _():
                    for order in range(2):
                        ends_share(order, 1 - core)

            intra(2 * part + 3, 2 * part + 5)
            if part == 0:
                @pl.when(is_inner)
                def _():
                    rows_wait(0)
                    rows_wait(1)
                    pass_rows()

        intra(half + 3, heads)
        for part in range(1, half // 2):
            gather_others(part)

        inter(half, heads)

        @pl.when(is_end)
        def _():
            recompute(relay_move, grads)


        whole(rows_ref.at[:, :, 0], local_sem).wait()
        whole(rows_ref.at[:, :, 1], mate_recv).wait()

        @pl.when(is_end)
        def _():
            rows_wait(1)


        def product(head, which):
            lhs = rows_ref[lax.rem(head, 2), which].reshape(4 * tokens, strip)
            return contract(lhs, grads[head].reshape(4 * tokens, 3 * width), ROWS)

        def relay(index):
            head = at_order(index)
            near_move(head).wait_recv()
            relay_move(head).start()

        @pl.when(jnp.logical_not(is_end))
        def _():
            for index in range(half):
                relay(index)

        @pl.loop(0, half // 2)
        def _(turn):
            group = turn

            @pl.when(jnp.logical_not(is_end))
            def _():
                for index in range(2):
                    relay(half + 2 * turn + index)

            @pl.when(is_end & (turn > 0))
            def _():
                for index in (2, 3, half + 2, half + 3):
                    relay(index)

            def head_at(index):
                return 2 * group + lax.rem(index, 2) + (index // 2) * half

            @pl.loop(0, 4)
            def _(index):
                head = head_at(index)
                pair_move(head).wait_recv()
                relay_move(head).wait_recv()
                hop[head] = product(head, 1).astype(BF16)
                hop_move(head).start()

        @pl.when(is_end)
        def _():
            rows_wait(0)

        @pl.loop(0, heads)
        def _(head):
            value = product(head, 0)
            for part in range(3):
                out_ref[part, :, cols_of(head)] = value[:, part * width : (part + 1) * width]

        settle()

        @pl.when(is_end)
        def _():
            whole(grads.at[pl.ds(0, half), 0], near_send).wait()

        @pl.when(jnp.logical_not(is_end))
        def _():
            whole(grads.at[:, 0], near_send).wait()

        whole(grads.at[:, 0], pair_send).wait()
        whole(grads.at[:, 0], relay_send).wait()

        @pl.loop(0, heads)
        def _(index):
            head = 2 * (index // 4) + lax.rem(index, 2) + (lax.rem(index, 4) // 2) * half
            hop_move(head).wait_recv()
            for part in range(3):
                out_ref[part, :, cols_of(head)] += hop_in[head, :, part * width : (part + 1) * width].astype(F32)

        whole(hop, hop_send).wait()

    pl.run_scoped(
        finish_all,
        pltpu.VMEM((heads, 4, tokens, 3 * width), BF16),
        pltpu.VMEM((heads, strip, 3 * width), BF16),
        pltpu.VMEM((heads, strip, 3 * width), BF16),
    )


def fused(scale, lengths, activations, decay, out_grad, weight, shard_count, size):
    tokens, depth = activations.shape
    columns = out_grad.shape[1]
    heads = decay.shape[0]
    width = columns // heads
    half = heads // 2
    strip = size * depth // shard_count
    dma = pltpu.SemaphoreType.DMA
    away = pl.BlockSpec(memory_space=pltpu.HBM)
    return pl.pallas_call(
        functools.partial(fused_kernel, scale),
        in_specs=[pl.BlockSpec(memory_space=pltpu.SMEM)] + [away] * 4,
        out_specs=pl.BlockSpec(memory_space=pltpu.VMEM),
        out_shape=jax.ShapeDtypeStruct((3, strip, columns), F32),
        scratch_shapes=[
            pltpu.VMEM((size, tokens, depth), BF16),
            pltpu.VMEM((heads, tokens), F32),
            pltpu.VMEM((heads, tokens), F32),
            pltpu.VMEM((heads, tokens, width), F32),
            pltpu.VMEM((shard_count, heads, width), F32),
            pltpu.VMEM((heads, width), F32),
            pltpu.VMEM((3, tokens, columns), BF16),
            pltpu.VMEM((tokens, columns), BF16),
            pltpu.VMEM((3, tokens, columns), F32),
            pltpu.VMEM((2, 2, 4, tokens, strip), BF16),
            pltpu.VMEM((2, heads, width, width), F32),
            pltpu.VMEM((2, heads, width, width), BF16),
            pltpu.VMEM((2, heads, width, width), BF16),
            pltpu.VMEM((2, half, width, width), BF16),
            pltpu.VMEM((3, half, width, width), BF16),
            pltpu.VMEM((2, half, width, width), BF16),
            pltpu.VMEM((2, half, width, width), BF16),
            pltpu.VMEM((heads, width, width), BF16),
            pltpu.VMEM((heads, width, width), BF16),
            pltpu.VMEM((2 * heads, tokens), F32),
            pltpu.VMEM((2, 2 * heads, tokens), F32),
            pltpu.VMEM((6, tokens, width), F32),
            pltpu.VMEM((4, 3, tokens, width), BF16),
            pltpu.VMEM((4, tokens, width), BF16),
            pltpu.VMEM((2, 2, 2, width, width), BF16),
            dma((3,)),
            dma((size,)),
            dma((2, size)),
            dma((size, PIECES)),
            dma,
            dma,
            dma,
            dma,
            dma,
            dma((2, 2)),
            dma((2, 2)),
            dma((2,)),
            dma((2,)),
            dma,
            dma((3, half // 2)),
            dma,
            dma((half // 2,)),
        ] + [dma, dma((heads,))] * 4 + [dma((2,))] + [dma] * 7 + [dma((2,))] + [pltpu.SemaphoreType.REGULAR],
        compiler_params=pltpu.CompilerParams(collective_id=1, has_side_effects=True, vmem_limit_bytes=GRANT << 20),
        name="fused",
    )(lengths, *(pltpu.with_memory_space_constraint(value, pltpu.HBM) for value in (activations, decay, out_grad, weight)))


FIRST = 1
GRANT = 48
UNROLL = 4


def pick(value, bit, mine, me):
    at = (me >> (bit + 1)) & 1
    return lax.dynamic_index_in_dim(value, at if mine else 1 - at, value.ndim - 3 - bit, keepdims=True)


def scatter_sum(lhs, rhs, bits, me, size):
    def times(block):
        flat = block.reshape((-1,) + block.shape[-2:])
        if flat.shape[0] == 1:
            result = contract(flat[0], rhs, ROWS)
        else:
            result = contract(flat, rhs, ((1,), (0,)))
        return result.reshape(block.shape[:-2] + (block.shape[-1], rhs.shape[1]))

    received = []
    keep = lhs
    for bit in bits:
        send = times(pick(keep, bit, False, me))
        for value in received:
            send = send + pick(value, bit, False, me).astype(F32)
        keep = pick(keep, bit, True, me)
        received = [pick(value, bit, True, me) for value in received]
        received.append(swap(send.astype(BF16), size, 2 << bit))
    total = times(keep)
    for value in received:
        total = total + value.astype(F32)
    return total.reshape(lhs.shape[-1], rhs.shape[1])


def is_square(shard_count, size):
    chips = shard_count // 2
    return chips == size and chips.bit_length() - 1 == 2


def shards(activations, qkv_weight, log_decay, lengths, out_grad):
    size = lax.axis_size("context")
    me = lax.axis_index("context")
    core = me & 1
    chip = me >> 1
    chips = size // 2
    tokens = activations.shape[0]
    heads = log_decay.shape[1]
    columns = out_grad.shape[1]
    width = columns // heads
    half = heads // 2
    scale = width ** -0.5

    if is_square(size, lax.axis_size("tensor")):
        return fused(
            scale, lengths, activations, log_decay.T, out_grad, qkv_weight.transpose(1, 0, 2), size, lax.axis_size("tensor")
        ).transpose(1, 0, 2)

    token_at = jnp.arange(tokens, dtype=jnp.int32)
    live = token_at < lengths[0]
    run_sum = jnp.cumsum(log_decay * live.astype(F32)[:, None], axis=0)
    run_wide = jnp.repeat(run_sum, width, axis=1)
    run_rows = run_sum.T
    own_total = run_sum[-1].astype(BF16).astype(F32)
    total_block = jnp.broadcast_to(jnp.pad(own_total, (0, 128 - heads))[None], (8, 128))
    live_column = live.astype(F32)[:, None]
    every, q, k, v, totals = project(
        activations, qkv_weight.transpose(1, 0, 2), live_column, total_block, size, lax.axis_size("tensor")
    )
    totals = totals[:, 0, :heads]

    rows = qkv_weight.shape[0] // size
    blocks = every.shape[2] // (2 * rows)
    low_rows, high_rows = [
        jnp.stack(
            [every[:, :, (2 * at + which) * rows : (2 * at + which + 1) * rows] for at in range(blocks)], axis=1
        ).reshape(chips, tokens, rows)
        for which in (0, 1)
    ]
    own_rows = jnp.where(core == 0, low_rows, high_rows)
    other_rows = swap(jnp.where(core == 0, high_rows, low_rows), size, 1)
    lhs = jnp.concatenate([own_rows, other_rows], axis=1)

    depth = chips.bit_length() - 1
    orders = (tuple(range(depth)), tuple(reversed(range(depth))))
    lhs = lhs.reshape((2,) * depth + lhs.shape[1:])
    lefts = []
    for order in orders:
        if not depth:
            lefts.append(lhs)
            continue
        moved = swap(pick(lhs, order[0], False, me), size, 2 << order[0])
        lefts.append(jnp.concatenate([pick(lhs, order[0], True, me), moved], axis=-2))

    head_spec = pl.BlockSpec((tokens, width), lambda h: (0, h))
    square_spec = pl.BlockSpec((1, width, width), lambda h: (h, 0, 0))
    wide = lambda kind: jax.ShapeDtypeStruct((tokens, columns), kind)
    squares = jax.ShapeDtypeStruct((heads, width, width), BF16)
    state, grad_state = pl.pallas_call(
        functools.partial(states_kernel, scale),
        grid=(heads,),
        in_specs=[head_spec] * 5,
        out_specs=[square_spec] * 2,
        out_shape=[squares] * 2,
        cost_estimate=pl.CostEstimate(flops=4 * tokens * columns * width, bytes_accessed=12 * tokens * columns, transcendentals=0),
        name="states",
    )(q, k, v, out_grad, run_wide)

    both = jnp.stack([state, grad_state])
    other = swap(both, size, 1)
    mine_half = lax.dynamic_slice_in_dim(both, core * half, half, 1).astype(F32)
    other_half = lax.dynamic_slice_in_dim(other, core * half, half, 1).astype(F32)
    pair_totals = lax.dynamic_slice_in_dim(totals, chip * 2, 2, 0)
    pair_half = lax.dynamic_slice_in_dim(pair_totals, core * half, half, 1)
    low, high = [jnp.where(core == which, mine_half, other_half) for which in (0, 1)]
    chip_state = (jnp.exp(pair_half[1])[:, None, None] * low[0] + high[0]).astype(BF16)
    chip_grad = (low[1] + jnp.exp(pair_half[0])[:, None, None] * high[1]).astype(BF16)

    arrivals = [
        swap(jnp.where((chip ^ step) > chip, chip_state, chip_grad), size, 2 * step) for step in range(1, chips)
    ]

    dq, dk, dv = pl.pallas_call(
        functools.partial(intra_kernel, scale),
        grid=(heads,),
        in_specs=[head_spec] * 5 + [pl.BlockSpec((heads, tokens), lambda h: (0, 0))],
        out_specs=[head_spec] * 3,
        out_shape=[wide(F32)] * 3,
        cost_estimate=pl.CostEstimate(
            flops=10 * tokens * tokens * columns, bytes_accessed=24 * tokens * columns, transcendentals=heads * tokens * tokens
        ),
        name="intra",
    )(q, k, v, out_grad, run_wide, run_rows)

    arrivals, dq, dk, dv = lax.optimization_barrier((arrivals, dq, dk, dv))
    upto = jnp.cumsum(totals, axis=0)
    totals_half = lax.dynamic_slice_in_dim(totals, core * half, half, 1)
    upto_half = lax.dynamic_slice_in_dim(upto, core * half, half, 1)
    chip_before = lax.dynamic_index_in_dim(upto_half - totals_half, chip * 2, 0, keepdims=False)
    chip_upto = lax.dynamic_index_in_dim(upto_half, chip * 2 + 1, 0, keepdims=False)
    incoming = jnp.zeros((half, width, width), F32)
    later = jnp.zeros((half, width, width), F32)
    for step in range(1, chips):
        peer = chip ^ step
        goes_up = peer > chip
        arrived = arrivals[step - 1].astype(F32)
        peer_upto = lax.dynamic_index_in_dim(upto_half, peer * 2 + 1, 0, keepdims=False)
        peer_before = lax.dynamic_index_in_dim(upto_half - totals_half, peer * 2, 0, keepdims=False)
        gap = jnp.where(goes_up, peer_before - chip_upto, chip_before - peer_upto)
        term = jnp.exp(gap)[:, None, None] * arrived
        incoming = incoming + jnp.where(goes_up, 0.0, term)
        later = later + jnp.where(goes_up, term, 0.0)
    from_chips = jnp.stack([incoming, later]).astype(BF16)
    other_chips = swap(from_chips, size, 1)
    is_low = core == 0
    from_chips = jnp.concatenate(
        [jnp.where(is_low, from_chips, other_chips), jnp.where(is_low, other_chips, from_chips)], axis=1
    ).astype(F32)
    incoming = jnp.where(
        is_low, from_chips[0], jnp.exp(pair_totals[0])[:, None, None] * from_chips[0] + other[0].astype(F32)
    ).astype(BF16)
    later = jnp.where(
        is_low, jnp.exp(pair_totals[1])[:, None, None] * from_chips[1] + other[1].astype(F32), from_chips[1]
    ).astype(BF16)

    grads = pl.pallas_call(
        functools.partial(inter_kernel, scale),
        grid=(heads,),
        in_specs=[pl.BlockSpec(memory_space=pltpu.SMEM)] + [head_spec] * 4 + [square_spec] * 2 + [head_spec] * 3,
        out_specs=[head_spec] * 3,
        out_shape=[wide(BF16)] * 3,
        cost_estimate=pl.CostEstimate(flops=6 * tokens * columns * width, bytes_accessed=28 * tokens * columns, transcendentals=0),
        name="inter",
    )(lengths, k, v, out_grad, run_wide, incoming, later, dq, dk, dv)

    results = []
    piece = columns // 2
    for part in grads:
        halves = [part[:, :piece], part[:, piece:]]
        if depth:
            moved = [swap(value, size, 2 << order[0]) for value, order in zip(halves, orders)]
            others = swap(jnp.concatenate(moved, axis=1), size, 1)
        partner = swap(part, size, 1)
        pieces = []
        for at, order in enumerate(orders):
            columns_at = slice(at * piece, (at + 1) * piece)
            rhs = [halves[at], partner[:, columns_at]]
            if depth:
                rhs += [moved[at], others[:, columns_at]]
            pieces.append(scatter_sum(lefts[at], jnp.concatenate(rhs, axis=0), order[1:], me, size))
        results.append(jnp.concatenate(pieces, axis=1))
    return jnp.stack(results, axis=1)


def solution(mesh):
    step = jax.shard_map(
        shards,
        mesh=mesh,
        in_specs=(
            P("context", "tensor"),
            P(None, None, "tensor"),
            P("context", "tensor"),
            P("context"),
            P("context", "tensor"),
        ),
        out_specs=P("context", None, "tensor"),
        check_vma=False,
    )
    if is_square(mesh.shape["context"], mesh.shape["tensor"]):
        return step
    return step
```

```python
import functools

import jax
import jax.numpy as jnp
from jax import lax
from jax.experimental import pallas as pl
from jax.experimental.pallas import tpu as pltpu
from jax.sharding import PartitionSpec as P


F32 = jnp.float32
BF16 = jnp.bfloat16


def contract(a, b, dims):
    return lax.dot_general(a, b, (dims, ((), ())), preferred_element_type=F32)


ROWS = ((0,), (0,))
LANES = ((1,), (1,))
PLAIN = ((1,), (0,))


def states_kernel(scale, q_ref, k_ref, v_ref, g_ref, c_ref, state_ref, grad_ref):
    c = c_ref[...]
    total = c[-1:, :]
    weighted_k = (k_ref[...].astype(F32) * jnp.exp(total - c)).astype(BF16)
    state_ref[0] = contract(weighted_k, v_ref[...], ROWS).astype(BF16)
    weighted_q = (q_ref[...].astype(F32) * (scale * jnp.exp(c))).astype(BF16)
    grad_ref[0] = contract(weighted_q, g_ref[...], ROWS).astype(BF16)


def intra_kernel(scale, q_ref, k_ref, v_ref, g_ref, c_ref, ct_ref, dq_ref, dk_ref, dv_ref):
    head = pl.program_id(0)
    q, k, v, g = q_ref[...], k_ref[...], v_ref[...], g_ref[...]
    tokens, width = q.shape
    column = jnp.concatenate([c_ref[...]] * (tokens // width), axis=1)
    gap = column - ct_ref[pl.ds(head, 1), :]
    row_at = lax.broadcasted_iota(jnp.int32, (tokens, tokens), 0)
    col_at = lax.broadcasted_iota(jnp.int32, (tokens, tokens), 1)
    decay = jnp.exp(jnp.where(row_at >= col_at, gap, -jnp.inf))
    prob = (contract(q, k, LANES) * scale * decay).astype(BF16)
    score = (contract(g, v, LANES) * decay).astype(BF16)
    dq_ref[...] = scale * contract(score, k, PLAIN)
    dk_ref[...] = scale * contract(score, q, ROWS)
    dv_ref[...] = contract(prob, g, ROWS)


def inter_kernel(scale, len_ref, k_ref, v_ref, g_ref, c_ref, in_ref, later_ref, dq_ref, dk_ref, dv_ref,
                 oq_ref, ok_ref, ov_ref):
    c = c_ref[...]
    live = lax.broadcasted_iota(jnp.int32, c.shape, 0) < len_ref[0]
    until = jnp.exp(c[-1:, :] - c)
    dq = dq_ref[...] + scale * jnp.exp(c) * contract(g_ref[...], in_ref[0], LANES)
    dk = dk_ref[...] + until * contract(v_ref[...], later_ref[0], LANES)
    dv = dv_ref[...] + until * contract(k_ref[...], later_ref[0], PLAIN)
    oq_ref[...] = jnp.where(live, dq, 0.0).astype(BF16)
    ok_ref[...] = jnp.where(live, dk, 0.0).astype(BF16)
    ov_ref[...] = jnp.where(live, dv, 0.0).astype(BF16)


def swap(value, size, distance):
    return lax.ppermute(value, "context", [(i, i ^ distance) for i in range(size)])


PIECES = 4
TILE = 512


def project_kernel(act_ref, live_ref, total_ref, weight_ref, every_ref, q_ref, k_ref, v_ref, totals_ref,
                   weights, sums, own_sem, weight_sem, send_sem, recv_sem, total_send, total_recv):
    size, me = lax.axis_size("tensor"), lax.axis_index("tensor")
    shard_count, shard = lax.axis_size("context"), lax.axis_index("context")
    depth = act_ref.shape[1]
    piece = act_ref.shape[0] // PIECES
    columns = q_ref.shape[1]
    tiles = columns // TILE

    def load(owner, part):
        rows = pl.ds(pl.multiple_of(owner * depth, depth), depth)
        return pltpu.make_async_copy(weight_ref.at[part, rows], weights.at[owner, part], weight_sem.at[owner, part])

    for at in range(size):
        owner = lax.rem(me + at, size)
        for part in range(3):
            load(owner, part).start()

    barrier = pltpu.get_barrier_semaphore()
    for target in (me - 1, me + 1):
        @pl.when((target >= 0) & (target < size))
        def _():
            pl.semaphore_signal(barrier, inc=1, device_id={"tensor": target}, device_id_type=pl.DeviceIdType.MESH)

    @pl.loop(1, shard_count)
    def _(step):
        peer = lax.rem(shard + step, shard_count)
        pl.semaphore_signal(barrier, inc=1, device_id={"context": peer}, device_id_type=pl.DeviceIdType.MESH)

    neighbours = jnp.where(me > 0, 1, 0) + jnp.where(me < size - 1, 1, 0)
    pl.semaphore_wait(barrier, neighbours + shard_count - 1)

    def rows_of(at):
        return pl.ds(pl.multiple_of(at * piece, piece), piece)

    def send(source, owner, at, side):
        return pltpu.make_async_remote_copy(
            src_ref=source,
            dst_ref=every_ref.at[owner, rows_of(at)],
            send_sem=send_sem.at[side, owner, at],
            recv_sem=recv_sem.at[owner, at],
            device_id={"tensor": me + 1 - 2 * side},
            device_id_type=pl.DeviceIdType.MESH,
        )

    def has_target(side):
        target = me + 1 - 2 * side
        return (target >= 0) & (target < size)

    def send_total(step):
        peer = lax.rem(shard + step, shard_count)
        return pltpu.make_async_remote_copy(
            src_ref=total_ref,
            dst_ref=totals_ref.at[shard],
            send_sem=total_send.at[peer],
            recv_sem=total_recv.at[shard],
            device_id={"context": peer},
            device_id_type=pl.DeviceIdType.MESH,
        )

    for at in range(PIECES):
        for side in range(2):
            @pl.when(has_target(side))
            def _():
                send(act_ref.at[rows_of(at)], me, at, side).start()

    @pl.loop(1, shard_count)
    def _(step):
        send_total(step).start()

    own = pltpu.make_async_copy(act_ref, every_ref.at[me], own_sem)
    own.start()
    totals_ref[shard] = total_ref[...]

    for part in range(3):
        load(me, part).wait()

    @pl.loop(0, 3 * tiles)
    def _(tile):
        part = tile // tiles
        cols = pl.ds(pl.multiple_of(lax.rem(tile, tiles) * TILE, TILE), TILE)
        sums[part, :, cols] = jnp.dot(act_ref[...], weights[me, part, :, cols], preferred_element_type=F32)

    own.wait()
    for distance in range(1, size):
        for side in range(2):
            owner = me + (2 * side - 1) * distance

            @pl.when((owner >= 0) & (owner < size))
            def _():
                for part in range(3):
                    load(owner, part).wait()

        @pl.loop(0, PIECES)
        def _(at):
            for side in range(2):
                owner = me + (2 * side - 1) * distance

                @pl.when((owner >= 0) & (owner < size))
                def _():
                    pltpu.make_async_copy(
                        every_ref.at[owner, rows_of(at)], every_ref.at[owner, rows_of(at)], recv_sem.at[owner, at]
                    ).wait()

                    @pl.when(has_target(side))
                    def _():
                        send(every_ref.at[owner, rows_of(at)], owner, at, side).start()

            @pl.loop(0, 2)
            def _(side):
                owner = me + (2 * side - 1) * distance

                @pl.when((owner >= 0) & (owner < size))
                def _():
                    @pl.loop(0, 3 * tiles)
                    def _(tile):
                        part = tile // tiles
                        cols = pl.ds(pl.multiple_of(lax.rem(tile, tiles) * TILE, TILE), TILE)
                        sums[part, rows_of(at), cols] += jnp.dot(
                            every_ref[owner, rows_of(at), :], weights[owner, part, :, cols], preferred_element_type=F32
                        )

    live = live_ref[...]
    for part, ref in enumerate((q_ref, k_ref, v_ref)):
        @pl.loop(0, tiles)
        def _(tile):
            cols = pl.ds(pl.multiple_of(tile * TILE, TILE), TILE)
            ref[:, cols] = (sums[part, :, cols] * live).astype(BF16)

    for side in range(2):
        @pl.when(has_target(side))
        def _():
            for distance in range(size):
                owner = me + (2 * side - 1) * distance

                @pl.when((owner >= 0) & (owner < size))
                def _():
                    for at in range(PIECES):
                        send(every_ref.at[owner, rows_of(at)], owner, at, side).wait_send()

    @pl.loop(1, shard_count)
    def _(step):
        peer = lax.rem(shard + step, shard_count)
        send_total(step).wait_send()
        pltpu.make_async_copy(total_ref, totals_ref.at[peer], total_recv.at[peer]).wait()


def project(activations, weight, live, total, shard_count, size):
    tokens, depth = activations.shape
    columns = weight.shape[2]
    vmem = pl.BlockSpec(memory_space=pltpu.VMEM)
    heads_out = [jax.ShapeDtypeStruct((tokens, columns), BF16)] * 3
    return pl.pallas_call(
        project_kernel,
        in_specs=[vmem] * 3 + [pl.BlockSpec(memory_space=pl.ANY)],
        out_specs=[vmem] * 5,
        out_shape=[jax.ShapeDtypeStruct((size, tokens, depth), BF16)]
        + heads_out
        + [jax.ShapeDtypeStruct((shard_count,) + total.shape, F32)],
        scratch_shapes=[
            pltpu.VMEM((size, 3, depth, columns), BF16),
            pltpu.VMEM((3, tokens, columns), F32),
            pltpu.SemaphoreType.DMA,
            pltpu.SemaphoreType.DMA((size, 3)),
            pltpu.SemaphoreType.DMA((2, size, PIECES)),
            pltpu.SemaphoreType.DMA((size, PIECES)),
            pltpu.SemaphoreType.DMA((shard_count,)),
            pltpu.SemaphoreType.DMA((shard_count,)),
        ],
        compiler_params=pltpu.CompilerParams(collective_id=0, has_side_effects=True, vmem_limit_bytes=48 << 20),
        name="project",
    )(activations, live, total, weight)


def flips(chip):
    bx, by = lax.rem(chip, 2), chip // 2
    return chip + 1 - 2 * bx, chip + 2 - 4 * by, 3 - chip


def fused_kernel(scale, len_ref, act_ref, decay_ref, grad_ref, weight_ref, out_ref,
                 every, decay, run, wide, totals, own_total, qkv, g_ref, sums, rows_ref, acc, own, pair, mixed, mixed_in,
                 prefix, prefix_in, incoming, later,
                 run_out, run_near, wide_near, qkv_near, grad_near, ends_near, detour,
                 input_sem, weight_sem, send_sem, recv_sem, total_send, total_recv, local_sem, mate_send, mate_recv,
                 row_send, row_recv, own_send, own_recv, mixed_send, mixed_recv, prefix_send, prefix_recv, pair_send, pair_recv,
                 near_send, near_recv, relay_send, relay_recv, hop_send, hop_recv, pass_send, run_send, run_recv,
                 copy_send, copy_recv, plain_send, plain_recv, ends_send, ends_recv,
                 detour_send, detour_recv, third_recv, ready, opened):
    size, me = lax.axis_size("tensor"), lax.axis_index("tensor")
    shard_count, shard = lax.axis_size("context"), lax.axis_index("context")
    core, chip = lax.rem(shard, 2), shard // 2
    others = flips(chip)
    chip_x, chip_y, chip_far = others
    partner = chip * 2 + 1 - core
    is_low = core == 0
    tokens, depth = act_ref.shape
    columns = grad_ref.shape[1]
    heads = decay_ref.shape[0]
    width = columns // heads
    half = heads // 2
    piece = tokens // PIECES
    tiles = columns // TILE
    strip = rows_ref.shape[-1]
    block = tokens // 2
    last = jnp.maximum(me, size - 1 - me)
    is_end = (me == 0) | (me == size - 1)
    is_inner = (me == 1) | (me == size - 2)
    outward = jnp.where(me == 1, 0, size - 1)
    inward = jnp.where(me == 0, 1, size - 2)
    far_block = jnp.where(me < size // 2, size - 1, 0)

    def shared(order, side):
        return order + half * side

    def move(source, target, send_at, recv_at, peer):
        return pltpu.make_async_remote_copy(
            src_ref=source, dst_ref=target, send_sem=send_at, recv_sem=recv_at,
            device_id={"context": peer}, device_id_type=pl.DeviceIdType.MESH,
        )

    def whole(view, sem):
        return pltpu.make_async_copy(view, view, sem)

    def rows_of(at):
        return pl.ds(pl.multiple_of(at * piece, piece), piece)

    def cols_of(head):
        return pl.ds(pl.multiple_of(head * width, width), width)

    def strip_of(which):
        return pl.ds(pl.multiple_of(which * strip, strip), strip)

    def at_order(index):
        return lax.rem(core * half + index, heads)

    def send(source, owner, at, side):
        return pltpu.make_async_remote_copy(
            src_ref=source,
            dst_ref=every.at[owner, rows_of(at)],
            send_sem=send_sem.at[side, owner],
            recv_sem=recv_sem.at[owner, at],
            device_id={"tensor": me + 1 - 2 * side},
            device_id_type=pl.DeviceIdType.MESH,
        )

    def has_target(side):
        target = me + 1 - 2 * side
        return (target >= 0) & (target < size)

    def send_total(step):
        peer = lax.rem(shard + step, shard_count)
        return move(own_total, totals.at[shard], total_send, total_recv, peer)

    def keep(source, at, order, which):
        return pltpu.make_async_copy(
            source.at[rows_of(at), strip_of(core)], rows_ref.at[order, which, 0, rows_of(at)], local_sem
        )

    def mate(source, at, order, which):
        return move(
            source.at[rows_of(at), strip_of(1 - core)], rows_ref.at[order, which, 1, rows_of(at)],
            mate_send, mate_recv, partner,
        )

    def across(source, at, order, which, other):
        target = core + other - 2 * core * other
        return move(
            source.at[rows_of(at), strip_of(target)], rows_ref.at[order, which, 2 + other, rows_of(at)],
            row_send.at[order, which], row_recv.at[order, which], others[order] * 2 + target,
        )

    def deliver(source, owner, at):
        for order in range(2):
            near, far = others[order], others[1 - order]

            @pl.when(((owner == near) | (owner == chip_far)) & jnp.logical_not(is_end & (owner == far_block)))
            def _():
                which = jnp.where(owner == near, 0, 1)
                for other in range(2):
                    across(source, at, order, which, other).start()

            @pl.when((owner == chip) | (owner == far))
            def _():
                which = jnp.where(owner == chip, 0, 1)
                keep(source, at, order, which).start()
                mate(source, at, order, which).start()

    def rows_wait(which):
        for order in range(2):
            whole(rows_ref.at[order, which, pl.ds(2, 2)], row_recv.at[order, which]).wait()

    def pass_rows():
        for order in range(2):
            @pl.when((far_block == chip) | (far_block == others[1 - order]))
            def _():
                which = jnp.where(far_block == chip, 0, 1)
                view = rows_ref.at[order, which, pl.ds(2, 2)]
                pltpu.make_async_remote_copy(
                    src_ref=view, dst_ref=view, send_sem=pass_send.at[order], recv_sem=row_recv.at[order, which],
                    device_id={"tensor": outward}, device_id_type=pl.DeviceIdType.MESH,
                ).start()

    def grad_share(order, side):
        return move(
            grad_ref.at[:, cols_of(shared(order, side))], grad_near.at[2 * order + side], copy_send, copy_recv,
            others[order] * 2 + core,
        )

    def run_share(order):
        return move(run_out, run_near.at[order], run_send, run_recv, others[order] * 2 + core)

    def qkv_share(order, side, at):
        return move(
            qkv.at[:, rows_of(at), cols_of(shared(order, side))], qkv_near.at[2 * order + side, :, rows_of(at)],
            plain_send, plain_recv, others[order] * 2 + core,
        )

    def ends_share(order, side):
        for kind, ref in enumerate((incoming, later)):
            move(
                ref.at[shared(order, side)], ends_near.at[side, kind, order], ends_send, ends_recv.at[side],
                others[order] * 2 + core,
            ).start()

    act_copy = pltpu.make_async_copy(act_ref, every.at[me], input_sem.at[0])
    decay_copy = pltpu.make_async_copy(decay_ref, decay, input_sem.at[1])
    grad_copy = pltpu.make_async_copy(grad_ref, g_ref, input_sem.at[2])

    barrier = pltpu.get_barrier_semaphore()
    for target in (me - 1, me + 1):
        @pl.when((target >= 0) & (target < size))
        def _():
            pl.semaphore_signal(barrier, inc=1, device_id={"tensor": target}, device_id_type=pl.DeviceIdType.MESH)

    @pl.loop(1, shard_count)
    def _(step):
        peer = lax.rem(shard + step, shard_count)
        pl.semaphore_signal(barrier, inc=1, device_id={"context": peer}, device_id_type=pl.DeviceIdType.MESH)

    @pl.when(is_inner)
    def _():
        for near in (chip_x, chip_y):
            pl.semaphore_signal(
                barrier, inc=1, device_id={"context": near * 2 + core, "tensor": outward}, device_id_type=pl.DeviceIdType.MESH
            )

    act_copy.start()
    decay_copy.start()
    neighbours = jnp.where(me > 0, 1, 0) + jnp.where(me < size - 1, 1, 0) + jnp.where(is_end, 2, 0)
    pl.semaphore_wait(barrier, neighbours + shard_count - 1)

    for at in range(PIECES):
        for side in range(2):
            @pl.when(has_target(side))
            def _():
                send(act_ref.at[rows_of(at)], me, at, side).start()

    @pl.loop(0, PIECES)
    def _(at):
        deliver(act_ref, me, at)

    @pl.when(is_end)
    def _():
        for order in range(2):
            for side in range(2):
                grad_share(order, side).start()

    def running_sums():
        token_at = lax.broadcasted_iota(jnp.int32, (heads, tokens), 1)
        masked = jnp.where(token_at < len_ref[0], decay[...], 0.0)
        row_at = lax.broadcasted_iota(jnp.int32, (tokens, tokens), 0)
        col_at = lax.broadcasted_iota(jnp.int32, (tokens, tokens), 1)
        upto = jnp.where(row_at <= col_at, 1.0, 0.0)
        c = lax.dot_general(
            masked, upto, (PLAIN, ((), ())), precision=lax.Precision.HIGHEST, preferred_element_type=F32
        )
        run[...] = c
        run_out[0:heads] = c
        run_out[heads : 2 * heads] = jnp.where(token_at < len_ref[0], 1.0, 0.0)
        total = c[:, tokens - 1 :].astype(BF16).astype(F32)
        own_total[...] = jnp.broadcast_to(total, own_total.shape)
        totals[shard] = jnp.broadcast_to(total, own_total.shape)
        column = jnp.concatenate([c, jnp.zeros((width - heads, tokens), F32)], axis=0).T
        for head in range(heads):
            wide[head] = jnp.broadcast_to(column[:, head : head + 1], (tokens, width))

    def half_move(index):
        side = index + core - 2 * index * core
        part = pl.ds((1 - side) * half, half)
        return move(own.at[:, part], pair.at[:, part], own_send.at[index], own_recv.at[index], partner)

    def states(at, first):
        @pl.loop(0, half, unroll=UNROLL)
        def _(index):
            head = first + index
            cols, rows = cols_of(head), rows_of(at)
            c = wide[head, rows, :]
            total = wide[head, tokens - 1 :, :]
            weighted_k = (qkv[1, rows, cols].astype(F32) * jnp.exp(total - c)).astype(BF16)
            acc[0, head] += contract(weighted_k, qkv[2, rows, cols], ROWS)
            weighted_q = (qkv[0, rows, cols].astype(F32) * (scale * jnp.exp(c))).astype(BF16)
            acc[1, head] += contract(weighted_q, g_ref[rows, cols], ROWS)

    def project_all(weights):
        def load(owner, part):
            rows = pl.ds(pl.multiple_of(owner * depth, depth), depth)
            return pltpu.make_async_copy(weight_ref.at[part, rows], weights.at[owner, part], weight_sem.at[owner])

        def loaded(owner):
            return pltpu.make_async_copy(weights.at[owner], weights.at[owner], weight_sem.at[owner])

        for at in range(size):
            owner = lax.rem(me + at, size)
            for part in range(3):
                load(owner, part).start()
        grad_copy.start()

        decay_copy.wait()
        running_sums()

        @pl.loop(1, shard_count)
        def _(step):
            send_total(step).start()

        @pl.when(is_end)
        def _():
            for order in range(2):
                run_share(order).start()

        acc[...] = jnp.zeros_like(acc)
        act_copy.wait()
        loaded(me).wait()

        def tile_at(tile):
            return tile // tiles, pl.ds(pl.multiple_of(lax.rem(tile, tiles) * TILE, TILE), TILE)

        @pl.loop(0, 3 * tiles)
        def _(tile):
            part, cols = tile_at(tile)
            sums[part, :, cols] = jnp.dot(every[me], weights[me, part, :, cols], preferred_element_type=F32)

        grad_copy.wait()

        for distance in range(1, size):
            for side in range(2):
                owner = me + (2 * side - 1) * distance

                @pl.when((owner >= 0) & (owner < size))
                def _():
                    loaded(owner).wait()

            @pl.loop(0, PIECES)
            def _(at):
                rows = rows_of(at)
                for side in range(2):
                    owner = me + (2 * side - 1) * distance

                    @pl.when((owner >= 0) & (owner < size))
                    def _():
                        pltpu.make_async_copy(
                            every.at[owner, rows], every.at[owner, rows], recv_sem.at[owner, at]
                        ).wait()

                        @pl.when(has_target(side))
                        def _():
                            send(every.at[owner, rows], owner, at, side).start()

                        deliver(every.at[owner], owner, at)

                @pl.loop(0, 2)
                def _(side):
                    owner = me + (2 * side - 1) * distance
                    valid = (owner >= 0) & (owner < size)

                    def product(part, cols):
                        return sums[part, rows, cols] + jnp.dot(
                            every[owner, rows, :], weights[owner, part, :, cols], preferred_element_type=F32
                        )

                    @pl.when(valid & (distance < last))
                    def _():
                        @pl.loop(0, 3 * tiles)
                        def _(tile):
                            part, cols = tile_at(tile)
                            sums[part, rows, cols] = product(part, cols)

                    if distance >= size // 2:
                        @pl.when(valid & (distance == last))
                        def _():
                            token_at = at * piece + lax.broadcasted_iota(jnp.int32, (piece, TILE), 0)
                            live = token_at < len_ref[0]

                            for index in range(2):
                                first = (1 - core if index == 0 else core) * half

                                @pl.loop(0, 3 * tiles // 2)
                                def _(tile):
                                    part, start = tile // (tiles // 2), lax.rem(tile, tiles // 2) * TILE
                                    cols = pl.ds(pl.multiple_of(first * width + start, width), TILE)
                                    qkv[part, rows, cols] = jnp.where(live, product(part, cols), 0.0).astype(BF16)

                                states(at, first)

                                @pl.when(is_end & ((at < PIECES - 1) | (index == 0)))
                                def _():
                                    for order in range(2):
                                        qkv_share(order, 1 - core if index == 0 else core, at).start()

                                @pl.when(at == PIECES - 1)
                                def _():
                                    own[:, pl.ds(first, half)] = acc[:, pl.ds(first, half)].astype(BF16)
                                    half_move(index).start()

    pl.run_scoped(project_all, pltpu.VMEM((size, 3, depth, columns), BF16))

    def half_wait(index):
        side = index + core - 2 * index * core
        part = pl.ds(side * half, half)
        pltpu.make_async_copy(pair.at[:, part], pair.at[:, part], own_recv.at[index]).wait()

    def mixed_move(step, part):
        kind = jnp.where(others[step] > chip, 0, 1)
        at = pl.ds(part * 2, 2)
        return move(
            mixed.at[kind, at], mixed_in.at[step, at], mixed_send, mixed_recv.at[step, part], others[step] * 2 + core
        )

    def prefix_move(part):
        at = pl.ds(2 * part, 2)
        return move(prefix.at[:, at], prefix_in.at[:, at], prefix_send, prefix_recv.at[part], partner)

    def total_of(which, head):
        return totals[which, pl.ds(head, 1), :]

    def within(q, k, v, g, column_at, row_at_block):
        dq, dk, dv = [None] * 2, [None] * 2, [None] * 2

        def add(held, part, value):
            held[part] = value if held[part] is None else held[part] + value

        for t in range(2):
            column = jnp.concatenate([column_at(t)] * (block // width), axis=1)
            for s in range(t + 1):
                gap = column - row_at_block(s)
                if s == t:
                    row_at = lax.broadcasted_iota(jnp.int32, (block, block), 0)
                    col_at = lax.broadcasted_iota(jnp.int32, (block, block), 1)
                    gap = jnp.where(row_at >= col_at, gap, -jnp.inf)
                decayed = jnp.exp(gap)
                prob = (contract(q[t], k[s], LANES) * scale * decayed).astype(BF16)
                score = (contract(g[t], v[s], LANES) * decayed).astype(BF16)
                add(dq, t, contract(score, k[s], PLAIN))
                add(dk, s, contract(score, q[t], ROWS))
                add(dv, s, contract(prob, g[t], ROWS))
        return [scale * value for value in dq], [scale * value for value in dk], dv

    blocks = [slice(part * block, (part + 1) * block) for part in range(2)]

    def intra(first, stop):
        @pl.loop(first, stop)
        def _(index):
            head = at_order(index)
            cols = cols_of(head)
            q, k, v = [[qkv[part, rows, cols] for rows in blocks] for part in range(3)]
            g = [g_ref[rows, cols] for rows in blocks]
            results = within(
                q, k, v, g, lambda t: wide[head, blocks[t], :], lambda s: run[pl.ds(head, 1), blocks[s]]
            )
            for part, values in enumerate(results):
                for index, value in enumerate(values):
                    sums[part, blocks[index], cols] = value

    def recompute(relay_move, grads):
        whole(run_near, run_recv).wait()
        for order in range(2):
            column = jnp.concatenate([run_near[order], jnp.zeros((width - 2 * heads, tokens), F32)], axis=0).T
            for side in range(2):
                head = shared(order, side)
                wide_near[2 * order + side] = jnp.broadcast_to(column[:, head : head + 1], (tokens, width))
            wide_near[4 + order] = jnp.broadcast_to(column[:, heads : heads + 1], (tokens, width))
        whole(grad_near, copy_recv).wait()
        whole(qkv_near, plain_recv).wait()

        for index in range(2):
            side = core if index == 0 else 1 - core
            whole(ends_near.at[side], ends_recv.at[side]).wait()

            @pl.loop(0, 2)
            def _(order):
                slot = 2 * order + side
                head = shared(order, side)
                q, k, v = [[qkv_near[slot, part, rows, :] for rows in blocks] for part in range(3)]
                g = [grad_near[slot, rows, :] for rows in blocks]
                dq, dk, dv = within(
                    q, k, v, g, lambda t: wide_near[slot, blocks[t], :], lambda s: run_near[order, pl.ds(head, 1), blocks[s]]
                )
                entering, leaving = ends_near[side, 0, order], ends_near[side, 1, order]
                final = wide_near[slot, tokens - 1 :, :]
                for part, rows in enumerate(blocks):
                    c = wide_near[slot, rows, :]
                    live = wide_near[4 + order, rows, :] > 0.5
                    until = jnp.exp(final - c)
                    values = (
                        dq[part] + scale * jnp.exp(c) * contract(g[part], entering, LANES),
                        dk[part] + until * contract(v[part], leaving, LANES),
                        dv[part] + until * contract(k[part], leaving, PLAIN),
                    )
                    for at, value in enumerate(values):
                        grads[head, 2, rows, at * width : (at + 1) * width] = jnp.where(live, value, 0.0).astype(BF16)
                relay_move(head).start()

    def spread(ref, at, head):
        sum_in, sum_later = ref[0, at].astype(F32), ref[1, at].astype(F32)
        incoming[head] = jnp.where(
            is_low, sum_in, jnp.exp(total_of(chip * 2, head)) * sum_in + pair[0, head].astype(F32)
        ).astype(BF16)
        later[head] = jnp.where(
            is_low, jnp.exp(total_of(chip * 2 + 1, head)) * sum_later + pair[1, head].astype(F32), sum_later
        ).astype(BF16)

    def settle():
        for side in range(2):
            @pl.when(has_target(side))
            def _():
                for distance in range(size):
                    owner = me + (2 * side - 1) * distance

                    @pl.when((owner >= 0) & (owner < size))
                    def _():
                        whole(every.at[owner], send_sem.at[side, owner]).wait()

        whole(totals.at[pl.ds(0, shard_count - 1)], total_send).wait()
        whole(rows_ref.at[:, :, 1], mate_send).wait()
        for order in range(2):
            for which in range(2):
                block_at = chip_far if which else others[order]

                @pl.when(jnp.logical_not(is_end & (block_at == far_block)))
                def _():
                    whole(rows_ref.at[order, which, pl.ds(2, 2)], row_send.at[order, which]).wait()

            @pl.when(is_inner & ((far_block == chip) | (far_block == others[1 - order])))
            def _():
                whole(rows_ref.at[order, 0, pl.ds(2, 2)], pass_send.at[order]).wait()

        @pl.when(is_end)
        def _():
            whole(run_near, run_send).wait()
            whole(grad_near, copy_send).wait()
            whole(qkv_near, plain_send).wait()
            whole(ends_near, ends_send).wait()

        for index in range(2):
            half_move(index).wait_send()
        whole(mixed_in, mixed_send).wait()
        whole(prefix_in, prefix_send).wait()

    def finish_all(grads, hop, hop_in):
        for target in (partner, chip_x * 2 + core, chip_y * 2 + core):
            pl.semaphore_signal(ready, inc=1, device_id={"context": target}, device_id_type=pl.DeviceIdType.MESH)

        @pl.when(is_end)
        def _():
            pl.semaphore_signal(opened, inc=1, device_id={"tensor": inward}, device_id_type=pl.DeviceIdType.MESH)

        whole(totals.at[pl.ds(0, shard_count - 1)], total_recv).wait()

        intra(0, FIRST)
        half_wait(0)

        for at in range(half):
            head = core * half + at
            mine, theirs = [[ref[kind, head].astype(F32) for kind in range(2)] for ref in (own, pair)]
            low, high = [
                [jnp.where(is_low == first, mine[kind], theirs[kind]) for kind in range(2)] for first in (True, False)
            ]
            mixed[0, at] = (jnp.exp(total_of(chip * 2 + 1, head)) * low[0] + high[0]).astype(BF16)
            mixed[1, at] = (low[1] + jnp.exp(total_of(chip * 2, head)) * high[1]).astype(BF16)

        for part in range(half // 2):
            for step in (2, 0, 1):
                mixed_move(step, part).start()
            if part == 0:
                @pl.when(is_end)
                def _():
                    for order in range(2):
                        qkv_share(order, core, PIECES - 1).start()


        def gather_states(part):
            for step in range(3):
                mixed_move(step, part).wait_recv()

            for at in range(2 * part, 2 * part + 2):
                head = core * half + at
                sum_in = jnp.zeros((width, width), F32)
                sum_later = jnp.zeros((width, width), F32)
                for step in range(3):
                    peer = others[step]
                    goes_up = peer > chip
                    first = jnp.where(goes_up, chip, peer) * 2 + 1
                    stop = jnp.where(goes_up, peer, chip) * 2
                    gap = jnp.zeros((1, width), F32)
                    for which in range(shard_count):
                        gap = gap + jnp.where((which > first) & (which < stop), total_of(which, head), 0.0)
                    term = jnp.exp(gap) * mixed_in[step, at].astype(F32)
                    sum_in = sum_in + jnp.where(goes_up, 0.0, term)
                    sum_later = sum_later + jnp.where(goes_up, term, 0.0)
                prefix[0, at] = sum_in.astype(BF16)
                prefix[1, at] = sum_later.astype(BF16)
                spread(prefix, at, head)

        def pair_move(head):
            return move(grads.at[head, 0], grads.at[head, 1], pair_send, pair_recv.at[head], partner)

        def near_move(head):
            near = chip_x + lax.rem(head, 2) * (chip_y - chip_x)
            return move(grads.at[head, 0], grads.at[head, 2], near_send, near_recv.at[head], near * 2 + core)

        def two_thirds(head, slot):
            return grads.at[head, slot, :, pl.ds(0, 2 * width)]

        def third(head, slot):
            return grads.at[head, slot, :, pl.ds(2 * width, width)]

        def short_move(head):
            near = chip_x + lax.rem(head, 2) * (chip_y - chip_x)
            return move(two_thirds(head, 0), two_thirds(head, 2), near_send, near_recv.at[head], near * 2 + core)

        def out_move(slot):
            head = at_order(heads - 2 + slot)
            near = chip_x + lax.rem(head, 2) * (chip_y - chip_x)
            return pltpu.make_async_remote_copy(
                src_ref=third(head, 0), dst_ref=detour.at[slot], send_sem=near_send, recv_sem=detour_recv.at[slot],
                device_id={"context": near * 2 + core, "tensor": inward}, device_id_type=pl.DeviceIdType.MESH,
            )

        def hand_back(slot):
            whole(detour.at[slot], detour_recv.at[slot]).wait()
            pltpu.make_async_remote_copy(
                src_ref=detour.at[slot], dst_ref=third(at_order(heads - 2 + slot), 2), send_sem=detour_send,
                recv_sem=third_recv.at[slot], device_id={"tensor": outward}, device_id_type=pl.DeviceIdType.MESH,
            ).start()

        def relay_move(head):
            return move(grads.at[head, 2], grads.at[head, 3], relay_send, relay_recv.at[head], partner)

        def hop_move(head):
            target = chip_y + lax.rem(head, 2) * (chip_x - chip_y)
            return move(hop.at[head], hop_in.at[head], hop_send, hop_recv.at[head], target * 2 + core)

        live = lax.broadcasted_iota(jnp.int32, (tokens, width), 0) < len_ref[0]

        def inter(first, stop):
            @pl.loop(first, stop)
            def _(index):
                head = at_order(index)
                cols = cols_of(head)
                c = wide[head]
                until = jnp.exp(wide[head, tokens - 1 :, :] - c)
                k, v, g = qkv[1, :, cols], qkv[2, :, cols], g_ref[:, cols]
                dq = sums[0, :, cols] + scale * jnp.exp(c) * contract(g, incoming[head], LANES)
                dk = sums[1, :, cols] + until * contract(v, later[head], LANES)
                dv = sums[2, :, cols] + until * contract(k, later[head], PLAIN)
                for part, value in enumerate((dq, dk, dv)):
                    grads[head, 0, :, part * width : (part + 1) * width] = jnp.where(live, value, 0.0).astype(BF16)
                around = is_end & (index >= heads - 2)

                @pl.when(jnp.logical_not(around | (is_end & (lax.rem(index, half) < half // 2))))
                def _():
                    near_move(head).start()

                @pl.when(around)
                def _():
                    out_move(index - (heads - 2)).start()
                    short_move(head).start()

                pair_move(head).start()

        def gather_others(part):
            prefix_move(part).wait_recv()
            for at in range(2 * part, 2 * part + 2):
                spread(prefix_in, at, (1 - core) * half + at)

        intra(FIRST, 3)
        half_wait(1)
        for part in range(half // 2):
            gather_states(part)
            prefix_move(part).start()
            if part == 0:
                pl.semaphore_wait(ready, 3)

                @pl.when(is_end)
                def _():
                    for order in range(2):
                        ends_share(order, core)

            inter(2 * part, 2 * part + 2)
            if part == 0:
                gather_others(part)

                @pl.when(is_end)
                def _():
                    for order in range(2):
                        ends_share(order, 1 - core)

            intra(2 * part + 3, 2 * part + 5)
            if part == 0:
                @pl.when(is_inner)
                def _():
                    rows_wait(0)
                    rows_wait(1)
                    pass_rows()

        intra(half + 3, heads)
        for part in range(1, half // 2):
            gather_others(part)

        inter(half, heads)

        @pl.when(is_end)
        def _():
            recompute(relay_move, grads)


        whole(rows_ref.at[:, :, 0], local_sem).wait()
        whole(rows_ref.at[:, :, 1], mate_recv).wait()

        @pl.when(is_end)
        def _():
            rows_wait(1)


        def product(head, which):
            lhs = rows_ref[lax.rem(head, 2), which].reshape(4 * tokens, strip)
            return contract(lhs, grads[head].reshape(4 * tokens, 3 * width), ROWS)

        def relay(index):
            head = at_order(index)
            near_move(head).wait_recv()
            relay_move(head).start()

        @pl.when(jnp.logical_not(is_end))
        def _():
            for index in range(half):
                relay(index)

        @pl.loop(0, half // 2)
        def _(turn):
            group = turn

            @pl.when(is_inner & (turn == half // 2 - 1))
            def _():
                pl.semaphore_wait(opened, 1)
                for slot in range(2):
                    hand_back(slot)

            @pl.when(jnp.logical_not(is_end))
            def _():
                for index in range(2):
                    relay(half + 2 * turn + index)

            @pl.when(is_end & (turn > 0))
            def _():
                for index in (2, 3):
                    relay(index)
                for slot in range(2):
                    head = at_order(heads - 2 + slot)
                    whole(two_thirds(head, 2), near_recv.at[head]).wait()
                    whole(third(head, 2), third_recv.at[slot]).wait()
                    relay_move(head).start()

            def head_at(index):
                return 2 * group + lax.rem(index, 2) + (index // 2) * half

            @pl.loop(0, 4)
            def _(index):
                head = head_at(index)
                pair_move(head).wait_recv()
                relay_move(head).wait_recv()
                hop[head] = product(head, 1).astype(BF16)
                hop_move(head).start()

        @pl.when(is_end)
        def _():
            rows_wait(0)

        @pl.loop(0, heads)
        def _(head):
            value = product(head, 0)
            for part in range(3):
                out_ref[part, :, cols_of(head)] = value[:, part * width : (part + 1) * width]

        settle()

        @pl.when(is_inner)
        def _():
            whole(detour, detour_send).wait()

        @pl.when(is_end)
        def _():
            whole(grads.at[pl.ds(0, half), 0], near_send).wait()

        @pl.when(jnp.logical_not(is_end))
        def _():
            whole(grads.at[:, 0], near_send).wait()

        whole(grads.at[:, 0], pair_send).wait()
        whole(grads.at[:, 0], relay_send).wait()

        @pl.loop(0, heads)
        def _(index):
            head = 2 * (index // 4) + lax.rem(index, 2) + (lax.rem(index, 4) // 2) * half
            hop_move(head).wait_recv()
            for part in range(3):
                out_ref[part, :, cols_of(head)] += hop_in[head, :, part * width : (part + 1) * width].astype(F32)

        whole(hop, hop_send).wait()

    pl.run_scoped(
        finish_all,
        pltpu.VMEM((heads, 4, tokens, 3 * width), BF16),
        pltpu.VMEM((heads, strip, 3 * width), BF16),
        pltpu.VMEM((heads, strip, 3 * width), BF16),
    )


def fused(scale, lengths, activations, decay, out_grad, weight, shard_count, size):
    tokens, depth = activations.shape
    columns = out_grad.shape[1]
    heads = decay.shape[0]
    width = columns // heads
    half = heads // 2
    strip = size * depth // shard_count
    dma = pltpu.SemaphoreType.DMA
    away = pl.BlockSpec(memory_space=pltpu.HBM)
    return pl.pallas_call(
        functools.partial(fused_kernel, scale),
        in_specs=[pl.BlockSpec(memory_space=pltpu.SMEM)] + [away] * 4,
        out_specs=pl.BlockSpec(memory_space=pltpu.VMEM),
        out_shape=jax.ShapeDtypeStruct((3, strip, columns), F32),
        scratch_shapes=[
            pltpu.VMEM((size, tokens, depth), BF16),
            pltpu.VMEM((heads, tokens), F32),
            pltpu.VMEM((heads, tokens), F32),
            pltpu.VMEM((heads, tokens, width), F32),
            pltpu.VMEM((shard_count, heads, width), F32),
            pltpu.VMEM((heads, width), F32),
            pltpu.VMEM((3, tokens, columns), BF16),
            pltpu.VMEM((tokens, columns), BF16),
            pltpu.VMEM((3, tokens, columns), F32),
            pltpu.VMEM((2, 2, 4, tokens, strip), BF16),
            pltpu.VMEM((2, heads, width, width), F32),
            pltpu.VMEM((2, heads, width, width), BF16),
            pltpu.VMEM((2, heads, width, width), BF16),
            pltpu.VMEM((2, half, width, width), BF16),
            pltpu.VMEM((3, half, width, width), BF16),
            pltpu.VMEM((2, half, width, width), BF16),
            pltpu.VMEM((2, half, width, width), BF16),
            pltpu.VMEM((heads, width, width), BF16),
            pltpu.VMEM((heads, width, width), BF16),
            pltpu.VMEM((2 * heads, tokens), F32),
            pltpu.VMEM((2, 2 * heads, tokens), F32),
            pltpu.VMEM((6, tokens, width), F32),
            pltpu.VMEM((4, 3, tokens, width), BF16),
            pltpu.VMEM((4, tokens, width), BF16),
            pltpu.VMEM((2, 2, 2, width, width), BF16),
            pltpu.VMEM((2, tokens, width), BF16),
            dma((3,)),
            dma((size,)),
            dma((2, size)),
            dma((size, PIECES)),
            dma,
            dma,
            dma,
            dma,
            dma,
            dma((2, 2)),
            dma((2, 2)),
            dma((2,)),
            dma((2,)),
            dma,
            dma((3, half // 2)),
            dma,
            dma((half // 2,)),
        ] + [dma, dma((heads,))] * 4 + [dma((2,))] + [dma] * 7 + [dma((2,)), dma, dma((2,)), dma((2,))] + [pltpu.SemaphoreType.REGULAR] * 2,
        compiler_params=pltpu.CompilerParams(collective_id=1, has_side_effects=True, vmem_limit_bytes=GRANT << 20),
        name="fused",
    )(lengths, *(pltpu.with_memory_space_constraint(value, pltpu.HBM) for value in (activations, decay, out_grad, weight)))


FIRST = 1
GRANT = 49
UNROLL = 2


def pick(value, bit, mine, me):
    at = (me >> (bit + 1)) & 1
    return lax.dynamic_index_in_dim(value, at if mine else 1 - at, value.ndim - 3 - bit, keepdims=True)


def scatter_sum(lhs, rhs, bits, me, size):
    def times(block):
        flat = block.reshape((-1,) + block.shape[-2:])
        if flat.shape[0] == 1:
            result = contract(flat[0], rhs, ROWS)
        else:
            result = contract(flat, rhs, ((1,), (0,)))
        return result.reshape(block.shape[:-2] + (block.shape[-1], rhs.shape[1]))

    received = []
    keep = lhs
    for bit in bits:
        send = times(pick(keep, bit, False, me))
        for value in received:
            send = send + pick(value, bit, False, me).astype(F32)
        keep = pick(keep, bit, True, me)
        received = [pick(value, bit, True, me) for value in received]
        received.append(swap(send.astype(BF16), size, 2 << bit))
    total = times(keep)
    for value in received:
        total = total + value.astype(F32)
    return total.reshape(lhs.shape[-1], rhs.shape[1])


def is_square(shard_count, size):
    chips = shard_count // 2
    return chips == size and chips.bit_length() - 1 == 2


def shards(activations, qkv_weight, log_decay, lengths, out_grad):
    size = lax.axis_size("context")
    me = lax.axis_index("context")
    core = me & 1
    chip = me >> 1
    chips = size // 2
    tokens = activations.shape[0]
    heads = log_decay.shape[1]
    columns = out_grad.shape[1]
    width = columns // heads
    half = heads // 2
    scale = width ** -0.5

    if is_square(size, lax.axis_size("tensor")):
        return fused(
            scale, lengths, activations, log_decay.T, out_grad, qkv_weight.transpose(1, 0, 2), size, lax.axis_size("tensor")
        ).transpose(1, 0, 2)

    token_at = jnp.arange(tokens, dtype=jnp.int32)
    live = token_at < lengths[0]
    run_sum = jnp.cumsum(log_decay * live.astype(F32)[:, None], axis=0)
    run_wide = jnp.repeat(run_sum, width, axis=1)
    run_rows = run_sum.T
    own_total = run_sum[-1].astype(BF16).astype(F32)
    total_block = jnp.broadcast_to(jnp.pad(own_total, (0, 128 - heads))[None], (8, 128))
    live_column = live.astype(F32)[:, None]
    every, q, k, v, totals = project(
        activations, qkv_weight.transpose(1, 0, 2), live_column, total_block, size, lax.axis_size("tensor")
    )
    totals = totals[:, 0, :heads]

    rows = qkv_weight.shape[0] // size
    blocks = every.shape[2] // (2 * rows)
    low_rows, high_rows = [
        jnp.stack(
            [every[:, :, (2 * at + which) * rows : (2 * at + which + 1) * rows] for at in range(blocks)], axis=1
        ).reshape(chips, tokens, rows)
        for which in (0, 1)
    ]
    own_rows = jnp.where(core == 0, low_rows, high_rows)
    other_rows = swap(jnp.where(core == 0, high_rows, low_rows), size, 1)
    lhs = jnp.concatenate([own_rows, other_rows], axis=1)

    depth = chips.bit_length() - 1
    orders = (tuple(range(depth)), tuple(reversed(range(depth))))
    lhs = lhs.reshape((2,) * depth + lhs.shape[1:])
    lefts = []
    for order in orders:
        if not depth:
            lefts.append(lhs)
            continue
        moved = swap(pick(lhs, order[0], False, me), size, 2 << order[0])
        lefts.append(jnp.concatenate([pick(lhs, order[0], True, me), moved], axis=-2))

    head_spec = pl.BlockSpec((tokens, width), lambda h: (0, h))
    square_spec = pl.BlockSpec((1, width, width), lambda h: (h, 0, 0))
    wide = lambda kind: jax.ShapeDtypeStruct((tokens, columns), kind)
    squares = jax.ShapeDtypeStruct((heads, width, width), BF16)
    state, grad_state = pl.pallas_call(
        functools.partial(states_kernel, scale),
        grid=(heads,),
        in_specs=[head_spec] * 5,
        out_specs=[square_spec] * 2,
        out_shape=[squares] * 2,
        cost_estimate=pl.CostEstimate(flops=4 * tokens * columns * width, bytes_accessed=12 * tokens * columns, transcendentals=0),
        name="states",
    )(q, k, v, out_grad, run_wide)

    both = jnp.stack([state, grad_state])
    other = swap(both, size, 1)
    mine_half = lax.dynamic_slice_in_dim(both, core * half, half, 1).astype(F32)
    other_half = lax.dynamic_slice_in_dim(other, core * half, half, 1).astype(F32)
    pair_totals = lax.dynamic_slice_in_dim(totals, chip * 2, 2, 0)
    pair_half = lax.dynamic_slice_in_dim(pair_totals, core * half, half, 1)
    low, high = [jnp.where(core == which, mine_half, other_half) for which in (0, 1)]
    chip_state = (jnp.exp(pair_half[1])[:, None, None] * low[0] + high[0]).astype(BF16)
    chip_grad = (low[1] + jnp.exp(pair_half[0])[:, None, None] * high[1]).astype(BF16)

    arrivals = [
        swap(jnp.where((chip ^ step) > chip, chip_state, chip_grad), size, 2 * step) for step in range(1, chips)
    ]

    dq, dk, dv = pl.pallas_call(
        functools.partial(intra_kernel, scale),
        grid=(heads,),
        in_specs=[head_spec] * 5 + [pl.BlockSpec((heads, tokens), lambda h: (0, 0))],
        out_specs=[head_spec] * 3,
        out_shape=[wide(F32)] * 3,
        cost_estimate=pl.CostEstimate(
            flops=10 * tokens * tokens * columns, bytes_accessed=24 * tokens * columns, transcendentals=heads * tokens * tokens
        ),
        name="intra",
    )(q, k, v, out_grad, run_wide, run_rows)

    arrivals, dq, dk, dv = lax.optimization_barrier((arrivals, dq, dk, dv))
    upto = jnp.cumsum(totals, axis=0)
    totals_half = lax.dynamic_slice_in_dim(totals, core * half, half, 1)
    upto_half = lax.dynamic_slice_in_dim(upto, core * half, half, 1)
    chip_before = lax.dynamic_index_in_dim(upto_half - totals_half, chip * 2, 0, keepdims=False)
    chip_upto = lax.dynamic_index_in_dim(upto_half, chip * 2 + 1, 0, keepdims=False)
    incoming = jnp.zeros((half, width, width), F32)
    later = jnp.zeros((half, width, width), F32)
    for step in range(1, chips):
        peer = chip ^ step
        goes_up = peer > chip
        arrived = arrivals[step - 1].astype(F32)
        peer_upto = lax.dynamic_index_in_dim(upto_half, peer * 2 + 1, 0, keepdims=False)
        peer_before = lax.dynamic_index_in_dim(upto_half - totals_half, peer * 2, 0, keepdims=False)
        gap = jnp.where(goes_up, peer_before - chip_upto, chip_before - peer_upto)
        term = jnp.exp(gap)[:, None, None] * arrived
        incoming = incoming + jnp.where(goes_up, 0.0, term)
        later = later + jnp.where(goes_up, term, 0.0)
    from_chips = jnp.stack([incoming, later]).astype(BF16)
    other_chips = swap(from_chips, size, 1)
    is_low = core == 0
    from_chips = jnp.concatenate(
        [jnp.where(is_low, from_chips, other_chips), jnp.where(is_low, other_chips, from_chips)], axis=1
    ).astype(F32)
    incoming = jnp.where(
        is_low, from_chips[0], jnp.exp(pair_totals[0])[:, None, None] * from_chips[0] + other[0].astype(F32)
    ).astype(BF16)
    later = jnp.where(
        is_low, jnp.exp(pair_totals[1])[:, None, None] * from_chips[1] + other[1].astype(F32), from_chips[1]
    ).astype(BF16)

    grads = pl.pallas_call(
        functools.partial(inter_kernel, scale),
        grid=(heads,),
        in_specs=[pl.BlockSpec(memory_space=pltpu.SMEM)] + [head_spec] * 4 + [square_spec] * 2 + [head_spec] * 3,
        out_specs=[head_spec] * 3,
        out_shape=[wide(BF16)] * 3,
        cost_estimate=pl.CostEstimate(flops=6 * tokens * columns * width, bytes_accessed=28 * tokens * columns, transcendentals=0),
        name="inter",
    )(lengths, k, v, out_grad, run_wide, incoming, later, dq, dk, dv)

    results = []
    piece = columns // 2
    for part in grads:
        halves = [part[:, :piece], part[:, piece:]]
        if depth:
            moved = [swap(value, size, 2 << order[0]) for value, order in zip(halves, orders)]
            others = swap(jnp.concatenate(moved, axis=1), size, 1)
        partner = swap(part, size, 1)
        pieces = []
        for at, order in enumerate(orders):
            columns_at = slice(at * piece, (at + 1) * piece)
            rhs = [halves[at], partner[:, columns_at]]
            if depth:
                rhs += [moved[at], others[:, columns_at]]
            pieces.append(scatter_sum(lefts[at], jnp.concatenate(rhs, axis=0), order[1:], me, size))
        results.append(jnp.concatenate(pieces, axis=1))
    return jnp.stack(results, axis=1)


def solution(mesh):
    step = jax.shard_map(
        shards,
        mesh=mesh,
        in_specs=(
            P("context", "tensor"),
            P(None, None, "tensor"),
            P("context", "tensor"),
            P("context"),
            P("context", "tensor"),
        ),
        out_specs=P("context", None, "tensor"),
        check_vma=False,
    )
    if is_square(mesh.shape["context"], mesh.shape["tensor"]):
        return step
    return step
```
